128 devices in a mesh: row: 2 (over y_lo), col: 16 (over x, y_hi, core), mode: 4 (over z).
Axes of the slice: x: 4, y: 4 (y_hi: 2, y_lo: 2; y = y_hi * 2 + y_lo), z: 4, core: 2. Of those that a mesh axis runs over, the one named last changes fastest.
Arguments:
- object_slab: float32 [2, 4096, 4096], P(None, 'row', 'col'), may hold values from -4.2 to 4.2
- probe_modes: float32 [2, 4, 256, 256], P(None, 'mode'), may hold values from -4.2 to 4.2
- amplitudes: float32 [512, 256, 256], P(('row', 'col')), may hold values from 0.5 to 3.5
- scan_counts: int32 [32], replicated, may hold values from 1 to 16, as said below
- scan_positions: int32 [2, 512], P(None, ('row', 'col')), may hold values from 0 to 3840, as said below
Outputs:
- object_grad: float32 [2, 4096, 4096], P(None, 'row', 'col')
- probe_grad: float32 [2, 4, 256, 256], P(None, 'mode')
- position_grad: float32 [2, 512], P(None, ('row', 'col'))
The draws below stay inside these ranges and needn't reach their ends.
Inputs may be any that keep to these rules, and one draw needn't show every extreme that they name: `scan_counts`: each tile holds between 1 and 16 patterns, and some tile holds exactly 16; a tile's active slots are its first ones. `scan_positions`: every slot's window starts inside the tile that owns the slot (slot p is owned by tile p // 16, tiles numbered row index * 16 + column index) and lies wholly inside the object; inactive slots also carry such positions.
All inputs are finite; a program needn't handle non-finite values.
Results may differ from the reference program's by a relative error of at most 0.0003.
Values sent between devices are 32-bit elements; how exact they have to be, the bound alone decides.
A program may use at most 128 MiB of HBM per device.

```python
import jax
import jax.numpy as jnp
from jax import lax

W = 256
MODES = 4
TH = 2048
TW = 256
CAP = 16
H = 4096
WT = 4096
TILES = 32
PATTERNS = 512


def draw_scan_counts(key, part):
    first_key, second_key = jax.random.split(jax.random.fold_in(key, 11))
    base = jax.random.randint(first_key, (TILES,), 1, CAP + 1)
    fullest = jax.random.randint(second_key, (), 0, TILES)
    return jnp.where(jnp.arange(TILES) == fullest, CAP, base).astype(jnp.int32)


def draw_scan_positions(key, part):
    first_key, second_key = jax.random.split(jax.random.fold_in(key, 23))
    tile_cols = WT // TW
    tile_rows = H // TH
    pattern = jnp.arange(PATTERNS)
    owner = pattern // CAP
    owner_row = owner // tile_cols
    owner_col = owner % tile_cols
    high_rows = jnp.where(owner_row == tile_rows - 1, TH - W + 1, TH)
    high_cols = jnp.where(owner_col == tile_cols - 1, TW - W + 1, TW)
    offset_rows = jax.random.randint(first_key, (PATTERNS,), 0, high_rows)
    offset_cols = jax.random.randint(second_key, (PATTERNS,), 0, high_cols)
    offset_rows = jnp.where(pattern == 0, 0, offset_rows)
    offset_cols = jnp.where(pattern == 0, 0, offset_cols)
    offset_rows = jnp.where(pattern == PATTERNS - 1, TH - W, offset_rows)
    offset_cols = jnp.where(pattern == PATTERNS - 1, TW - W, offset_cols)
    return jnp.stack([owner_row * TH + offset_rows, owner_col * TW + offset_cols]).astype(jnp.int32)


def block_levels(stream_key, dims, cuts, least, high):
    loudness, own = 1.0, jax.random.fold_in(stream_key, 6)
    for position, blocks in cuts:
        heights = jnp.exp(jax.random.uniform(jax.random.fold_in(own, position), (blocks,), jnp.float32, least / len(cuts), high / len(cuts)))
        loudness = loudness * jnp.repeat(heights, dims[position] // blocks).reshape([-1 if axis == position else 1 for axis in range(len(dims))])
    return loudness


def scatter_about(own_key, dims, scale, limit, pieces=(), kind=jnp.bfloat16):
    drawn = jax.random.normal(own_key, dims, jnp.float32) * scale
    if len(pieces) > 0:
        drawn = block_levels(own_key, dims, pieces, -0.22, 0.18) * drawn
    return jnp.clip(drawn, min=-limit, max=limit).astype(kind)


def setup_inputs(seed: int = 0) -> dict:
    streams_of = jax.random.split(jax.random.key(seed), 6)
    object_slab = scatter_about(streams_of[0], (2, H, WT), 0.7, 4.2, ((1, 2), (2, 16)), jnp.float32)
    probe_modes = scatter_about(streams_of[1], (2, MODES, W, W), 0.7, 4.2, ((1, 4),), jnp.float32)
    amplitudes = jnp.clip(0.5 + 3.0 * jax.random.uniform(streams_of[2], (PATTERNS, W, W), jnp.float32) ** block_levels(streams_of[2], (PATTERNS, W, W), ((0, 32),), -0.2, 0.2), 0.5, 3.5)
    scan_counts = draw_scan_counts(jax.random.fold_in(streams_of[5], 71), 0)
    scan_positions = draw_scan_positions(jax.random.fold_in(streams_of[5], 71), 0)
    return {"object_slab": object_slab, "probe_modes": probe_modes, "amplitudes": amplitudes, "scan_counts": scan_counts, "scan_positions": scan_positions}


def reference(object_slab, probe_modes, amplitudes, scan_counts, scan_positions):
    probe_cx = lax.complex(probe_modes[0], probe_modes[1])

    def advance(totals, pattern):
        grad_slab, grad_probe = totals
        row_at = scan_positions[0, pattern]
        col_at = scan_positions[1, pattern]
        zero_index = jnp.int32(0)
        active = (pattern % CAP < scan_counts[pattern // CAP]).astype(object_slab.dtype)
        window_obj = lax.dynamic_slice(object_slab, (zero_index, row_at, col_at), (2, W, W))
        object_win = lax.complex(window_obj[0], window_obj[1])
        far_field = jnp.fft.fft2(probe_cx * object_win[None], norm='ortho')
        intensity = lax.optimization_barrier(jnp.sum(far_field.real * far_field.real + far_field.imag * far_field.imag, axis=0))
        factor = 0.25 * (1.0 - amplitudes[pattern] / jnp.sqrt(intensity + 0.5)) * active
        near_field = jnp.fft.ifft2(factor[None] * far_field, norm='ortho')
        grad_win = lax.optimization_barrier(jnp.sum(jnp.conj(probe_cx) * near_field, axis=0))
        grad_modes = jnp.conj(object_win)[None] * near_field
        diff_rows = (object_win[2:, :] - object_win[:-2, :]) * 0.5
        diff_cols = (object_win[:, 2:] - object_win[:, :-2]) * 0.5
        inner_rows = grad_win[1:-1, :]
        inner_cols = grad_win[:, 1:-1]
        along_rows = jnp.sum(inner_rows.real * diff_rows.real + inner_rows.imag * diff_rows.imag) / W
        along_cols = jnp.sum(inner_cols.real * diff_cols.real + inner_cols.imag * diff_cols.imag) / W
        region = lax.dynamic_slice(grad_slab, (zero_index, row_at, col_at), (2, W, W))
        region = region + jnp.stack([grad_win.real, grad_win.imag])
        grad_slab = lax.dynamic_update_slice(grad_slab, region, (zero_index, row_at, col_at))
        grad_probe = grad_probe + jnp.stack([grad_modes.real, grad_modes.imag])
        return ((grad_slab, grad_probe), jnp.stack([along_rows, along_cols]))
    start = (jnp.zeros_like(object_slab), jnp.zeros_like(probe_modes))
    (grad_slab, grad_probe), shift_grads = lax.scan(advance, start, jnp.arange(PATTERNS, dtype=jnp.int32))
    return (grad_slab, grad_probe / 16.0, shift_grads.T)
```

```python
import math
import functools
import numpy as np
import jax
import jax.numpy as jnp
from jax import lax
from jax.experimental import pallas as pl
from jax.experimental.pallas import tpu as pltpu
from jax.sharding import PartitionSpec as P

BF = jnp.bfloat16
F32 = jnp.float32


def hi_lo(x):
    hi = x.astype(BF)
    lo = (x - hi.astype(F32)).astype(BF)
    return hi, lo


def tables(window):
    half = window // 2
    n = np.arange(half)[:, None]
    j = np.arange(half)[None, :]
    scale = 1.0 / math.sqrt(window)
    forward, inverse = [], []
    for parity in range(2):
        angle = 2.0 * math.pi * ((n * (2 * j + parity)) % window) / window
        c, s = np.cos(angle) * scale, np.sin(angle) * scale
        forward.append(np.block([[c, -s], [s, c]]))
        inverse.append(np.block([[c.T, s.T], [-s.T, c.T]]))
    sides = []
    for axis in (1, 2):
        for table in (np.stack(forward), np.stack(inverse)):
            table = table.astype(np.float32)
            if axis == 2:
                table = np.swapaxes(table, 1, 2)
            hi = table.astype(BF)
            lo = (table - hi.astype(np.float32)).astype(BF)
            sides.append(np.concatenate([hi, lo, hi], axis=axis))
    order = np.concatenate([np.arange(0, window, 2), np.arange(1, window, 2)])
    shuffle = np.zeros((window, window), np.float32)
    shuffle[order, np.arange(window)] = 1.0
    return sides[0], sides[1], sides[2], sides[3], shuffle.astype(BF)


def cat(parts, axis):
    return jnp.concatenate(parts, axis=axis)


def mm(a, b):
    return jnp.dot(a, b, preferred_element_type=F32)


def make_compute(window, modes, slots, tile_rows, tile_cols):
    w, half = window, window // 2
    ch = 32
    ext_rows, ext_cols = tile_rows + w, tile_cols + w

    def kernel(meta, own, right, low, diag, probe, amps, rf, ri, lf, li, shuffle,
               g_own, g_right, g_low, g_diag, pg, along,
               ext, grad, amp_buf, win, fac, lhs, rhs, mid, far, near, amp_sem, sem):
        count = meta[2 * slots]
        mine = meta[2 * slots + 1]
        def quarters(whole, parts):
            pairs = []
            for k in range(4):
                for t in range(2):
                    down = slice(tile_rows, ext_rows) if k >= 2 else slice(0, tile_rows)
                    pairs.append((whole.at[2 * (k % 2) + t, :, down, :], parts[k].at[:, :, 128 * t:128 * t + 128]))
            return pairs

        loads = [
            pltpu.make_async_copy(part, inside, sem.at[k])
            for k, (inside, part) in enumerate(quarters(ext, (own, right, low, diag)))
        ]
        for copy in loads:
            copy.start()

        def amp_copies(slot, place):
            return [
                pltpu.make_async_copy(
                    amps.at[slot, :, 128 * t:128 * t + 128], amp_buf.at[place, t], amp_sem.at[place, t]
                )
                for t in range(2)
            ]

        for copy in amp_copies(0, 0):
            copy.start()

        def clear(i, carry):
            at = pl.multiple_of(i * ch, ch)
            for c in range(2):
                for t in range(4):
                    grad[t, c, pl.ds(at, ch), :] = jnp.zeros((ch, 128), F32)
            return carry

        lax.fori_loop(0, ext_rows // ch, clear, 0)
        pg[...] = jnp.zeros(pg.shape, F32)

        def no_shift(i, carry):
            along[0, i] = 0.0
            along[1, i] = 0.0
            return carry

        lax.fori_loop(0, slots, no_shift, 0)
        for copy in loads:
            copy.wait()

        def do_slot(slot, carry):
            row = meta[slot]
            col = meta[slots + slot]
            tile_at = col // 128
            off = lax.rem(col, 128)
            back = lax.rem(w + 128 - off, w + 128)
            place = lax.rem(slot, 2)
            for copy in amp_copies(slot, place):
                copy.wait()

            @pl.when(slot + 1 < count)
            def _():
                for copy in amp_copies(slot + 1, 1 - place):
                    copy.start()

            for c in range(2):
                for r in range(0, w, ch):
                    wide = cat([ext[tile_at + t, c, pl.ds(row + r, ch), :] for t in range(3)], 1)
                    win[c, r:r + ch, :] = pltpu.roll(wide, back, 1)[:, :w]

            for parity in range(2):
                a = cat([amp_buf[place, t, pl.ds(parity, half, stride=2), :] for t in range(2)], 1)
                a0, rest = a.astype(BF), None
                r1 = a - a0.astype(F32)
                a1 = r1.astype(BF)
                a2 = (r1 - a1.astype(F32)).astype(BF)
                fac[parity] = mm(a0, shuffle[...]) + mm(a1, shuffle[...]) + mm(a2, shuffle[...])

            for m in range(modes):
                for r in range(0, w, ch):
                    vre, vim = win[0, r:r + ch, :], win[1, r:r + ch, :]
                    pre, pim = probe[0, m, r:r + ch, :], probe[1, m, r:r + ch, :]
                    are = pre * vre - pim * vim
                    aim = pre * vim + pim * vre
                    for parity in range(2):
                        if parity == 0:
                            x = cat([are[:, :half] + are[:, half:], aim[:, :half] + aim[:, half:]], 1)
                        else:
                            x = cat([are[:, :half] - are[:, half:], aim[:, :half] - aim[:, half:]], 1)
                        hi, lo = hi_lo(x)
                        lhs[m, parity, r:r + ch, :w] = hi
                        lhs[m, parity, r:r + ch, w:] = lo
                for parity in range(2):
                    hi, lo = lhs[m, parity, :, :w], lhs[m, parity, :, w:]
                    mid[m, parity] = mm(cat([hi, hi, lo], 1), rf[parity])
                for r in range(0, half, ch):
                    e_top, e_bot = mid[m, 0, r:r + ch, :], mid[m, 0, half + r:half + r + ch, :]
                    o_top, o_bot = mid[m, 1, r:r + ch, :], mid[m, 1, half + r:half + r + ch, :]
                    for parity in range(2):
                        if parity == 0:
                            e, o = e_top + e_bot, o_top + o_bot
                        else:
                            e, o = e_top - e_bot, o_top - o_bot
                        hi, lo = hi_lo(cat([e[:, :half], o[:, :half]], 1))
                        rhs[m, parity, 0, r:r + ch, :] = hi
                        rhs[m, parity, 1, r:r + ch, :] = lo
                        hi, lo = hi_lo(cat([e[:, half:], o[:, half:]], 1))
                        rhs[m, parity, 0, half + r:half + r + ch, :] = hi
                        rhs[m, parity, 1, half + r:half + r + ch, :] = lo
                for parity in range(2):
                    hi, lo = rhs[m, parity, 0], rhs[m, parity, 1]
                    far[m, parity] = mm(lf[parity], cat([hi, hi, lo], 0))

            for parity in range(2):
                for r in range(0, half, ch):
                    total = None
                    for m in range(modes):
                        re = far[m, parity, r:r + ch, :]
                        im = far[m, parity, half + r:half + r + ch, :]
                        term = re * re + im * im
                        total = term if total is None else total + term
                    f = 0.25 * (1.0 - fac[parity, r:r + ch, :] * lax.rsqrt(total + 0.5))
                    fac[parity, r:r + ch, :] = f

            for m in range(modes):
                for parity in range(2):
                    for r in range(0, half, ch):
                        f = fac[parity, r:r + ch, :]
                        for part in range(2):
                            at = part * half + r
                            hi, lo = hi_lo(f * far[m, parity, at:at + ch, :])
                            rhs[m, parity, 0, at:at + ch, :] = hi
                            rhs[m, parity, 1, at:at + ch, :] = lo
                for parity in range(2):
                    hi, lo = rhs[m, parity, 0], rhs[m, parity, 1]
                    mid[m, parity] = mm(li[parity], cat([hi, hi, lo], 0))
                for r in range(0, half, ch):
                    e_re, e_im = mid[m, 0, r:r + ch, :], mid[m, 0, half + r:half + r + ch, :]
                    o_re, o_im = mid[m, 1, r:r + ch, :], mid[m, 1, half + r:half + r + ch, :]
                    for top in range(2):
                        if top == 0:
                            re, im = e_re + o_re, e_im + o_im
                        else:
                            re, im = e_re - o_re, e_im - o_im
                        at = top * half + r
                        for parity in range(2):
                            cols = slice(parity * half, parity * half + half)
                            hi, lo = hi_lo(cat([re[:, cols], im[:, cols]], 1))
                            lhs[m, parity, at:at + ch, :w] = hi
                            lhs[m, parity, at:at + ch, w:] = lo
                for parity in range(2):
                    hi, lo = lhs[m, parity, :, :w], lhs[m, parity, :, w:]
                    near[m, parity] = mm(cat([hi, hi, lo], 1), ri[parity])

            rows_sum = jnp.zeros((8, w), F32)
            cols_sum = jnp.zeros((8, w), F32)
            lanes = lax.broadcasted_iota(jnp.int32, (ch, w), 1)
            inner = (lanes >= 1) & (lanes <= w - 2)

            def near_of(m, r):
                e, o = near[m, 0, pl.ds(r, ch), :], near[m, 1, pl.ds(r, ch), :]
                s, d = e + o, e - o
                return cat([s[:, :half], d[:, :half]], 1), cat([s[:, half:], d[:, half:]], 1)

            for r in range(0, w, ch):
                gre = gim = None
                for m in range(modes):
                    nre, nim = near_of(m, r)
                    pre, pim = probe[0, m, r:r + ch, :], probe[1, m, r:r + ch, :]
                    tre = pre * nre + pim * nim
                    tim = pre * nim - pim * nre
                    gre = tre if gre is None else gre + tre
                    gim = tim if gim is None else gim + tim
                for c, g in ((0, gre), (1, gim)):
                    spread = pltpu.roll(cat([g, jnp.zeros((ch, 128), F32)], 1), off, 1)
                    for t in range(3):
                        grad[tile_at + t, c, pl.ds(row + r, ch), :] += spread[:, 128 * t:128 * t + 128]
                vre, vim = win[0, r:r + ch, :], win[1, r:r + ch, :]
                nre, nim = near_of(mine, r)
                pg[0, r:r + ch, :] += vre * nre + vim * nim
                pg[1, r:r + ch, :] += vre * nim - vim * nre
                dre = pltpu.roll(vre, w - 1, 1) - pltpu.roll(vre, 1, 1)
                dim = pltpu.roll(vim, w - 1, 1) - pltpu.roll(vim, 1, 1)
                t = jnp.where(inner, gre * dre + gim * dim, 0.0)
                cols_sum = cols_sum + jnp.sum(t.reshape(ch // 8, 8, w), axis=0)
                lo_r, hi_r = max(r, 1), min(r + ch, w - 1)
                up = [ext_rows_slice(win, c, r + 1, ch, w) for c in range(2)]
                dn = [ext_rows_slice(win, c, r - 1, ch, w) for c in range(2)]
                t = gre * (up[0] - dn[0]) + gim * (up[1] - dn[1])
                if lo_r != r or hi_r != r + ch:
                    idx = lax.broadcasted_iota(jnp.int32, (ch, w), 0) + r
                    t = jnp.where((idx >= lo_r) & (idx < hi_r), t, 0.0)
                rows_sum = rows_sum + jnp.sum(t.reshape(ch // 8, 8, w), axis=0)
            along[0, slot] = jnp.sum(rows_sum) * (0.5 / w)
            along[1, slot] = jnp.sum(cols_sum) * (0.5 / w)
            return carry

        def ext_rows_slice(ref, c, start, size, width):
            if start < 0:
                return cat([ref[c, 0:1, :], ref[c, 0:size - 1, :]], 0)
            if start + size > w:
                return cat([ref[c, start:w, :], ref[c, w - 1:w, :]], 0)
            return ref[c, start:start + size, :]

        lax.fori_loop(0, count, do_slot, 0)
        stores = [
            pltpu.make_async_copy(inside, part, sem.at[k])
            for k, (inside, part) in enumerate(quarters(grad, (g_own, g_right, g_low, g_diag)))
        ]
        for copy in stores:
            copy.start()
        for copy in stores:
            copy.wait()

    hbm = pl.BlockSpec(memory_space=pl.ANY)
    vmem = pl.BlockSpec(memory_space=pltpu.VMEM)
    smem = pl.BlockSpec(memory_space=pltpu.SMEM)
    shape = jax.ShapeDtypeStruct
    return pl.pallas_call(
        kernel,
        name="slots",
        in_specs=[smem, hbm, hbm, hbm, hbm, vmem, hbm, vmem, vmem, vmem, vmem, vmem],
        out_specs=[hbm, hbm, hbm, hbm, vmem, smem],
        out_shape=[
            shape((2, tile_rows, tile_cols), F32),
            shape((2, tile_rows, w), F32),
            shape((2, w, tile_cols), F32),
            shape((2, w, w), F32),
            shape((2, w, w), F32),
            shape((2, slots), F32),
        ],
        scratch_shapes=[
            pltpu.VMEM((ext_cols // 128, 2, ext_rows, 128), F32),
            pltpu.VMEM((ext_cols // 128, 2, ext_rows, 128), F32),
            pltpu.VMEM((2, 2, w, 128), F32),
            pltpu.VMEM((2, w, w), F32),
            pltpu.VMEM((2, half, w), F32),
            pltpu.VMEM((modes, 2, w, 2 * w), BF),
            pltpu.VMEM((modes, 2, 2, w, w), BF),
            pltpu.VMEM((modes, 2, w, w), F32),
            pltpu.VMEM((modes, 2, w, w), F32),
            pltpu.VMEM((modes, 2, w, w), F32),
            pltpu.SemaphoreType.DMA((2, 2)),
            pltpu.SemaphoreType.DMA((8,)),
        ],
        compiler_params=pltpu.CompilerParams(vmem_limit_bytes=60 << 20),
        cost_estimate=pl.CostEstimate(flops=10**11, bytes_accessed=10**7, transcendentals=0),
    )


def per_device(object_slab, probe_modes, amplitudes, scan_counts, scan_positions):
    window = probe_modes.shape[-1]
    tile_rows, tile_cols = object_slab.shape[1:]
    slots = amplitudes.shape[0]
    modes = lax.axis_size("mode")
    cols_n = lax.axis_size("col")
    rows_n = lax.axis_size("row")
    row_id, col_id, mode_id = lax.axis_index("row"), lax.axis_index("col"), lax.axis_index("mode")

    def diagonal(by):
        pairs = []
        for r in range(rows_n):
            for c in range(cols_n):
                if 0 <= r + by < rows_n and 0 <= c + by < cols_n:
                    pairs.append((r * cols_n + c, (r + by) * cols_n + c + by))
        return pairs

    def along(axis, by):
        n = lax.axis_size(axis)
        return [(i, i + by) for i in range(n) if 0 <= i + by < n]

    right = lax.ppermute(object_slab, "col", along("col", -1))
    top = object_slab[:, :window, :]
    low = lax.ppermute(top, "row", along("row", -1))
    diag = lax.ppermute(top, ("row", "col"), diagonal(-1))
    probe = lax.all_gather(probe_modes, "mode", axis=1, tiled=True)
    meta = jnp.concatenate([
        scan_positions[0] - row_id * tile_rows,
        scan_positions[1] - col_id * tile_cols,
        lax.dynamic_slice(scan_counts, (row_id * cols_n + col_id,), (1,)),
        mode_id[None].astype(jnp.int32),
    ])
    consts = [jnp.asarray(t) for t in tables(window)]
    compute = make_compute(window, modes, slots, tile_rows, tile_cols)
    g_own, g_right, g_low, g_diag, pg, shift = compute(
        meta, object_slab, right, low, diag, probe, amplitudes, *consts
    )
    from_left = lax.ppermute(g_right, "col", along("col", 1))
    from_up = lax.ppermute(g_low, "row", along("row", 1))
    from_diag = lax.ppermute(g_diag, ("row", "col"), diagonal(1))
    grad = g_own + from_left
    grad = grad.at[:, :window, :].add(from_up + from_diag)
    probe_total = lax.psum(pg, ("row", "col"))[:, None] / 16.0
    return (grad, probe_total, shift)


def solution(mesh):
    in_specs = (
        P(None, "row", "col"),
        P(None, "mode", None, None),
        P(("row", "col"), None, None),
        P(),
        P(None, ("row", "col")),
    )
    out_specs = (P(None, "row", "col"), P(None, "mode", None, None), P(None, ("row", "col")))
    return jax.shard_map(
        per_device, mesh=mesh, in_specs=in_specs, out_specs=out_specs, check_vma=False
    )
```

```python
import math
import functools
import numpy as np
import jax
import jax.numpy as jnp
from jax import lax
from jax.experimental import pallas as pl
from jax.experimental.pallas import tpu as pltpu
from jax.sharding import PartitionSpec as P

BF = jnp.bfloat16
F32 = jnp.float32


def hi_lo(x):
    hi = x.astype(BF)
    lo = (x - hi.astype(F32)).astype(BF)
    return hi, lo


def tables(window):
    half = window // 2
    n = np.arange(half)[:, None]
    j = np.arange(half)[None, :]
    scale = 1.0 / math.sqrt(window)
    forward, inverse = [], []
    for parity in range(2):
        angle = 2.0 * math.pi * ((n * (2 * j + parity)) % window) / window
        c, s = np.cos(angle) * scale, np.sin(angle) * scale
        forward.append(np.block([[c, -s], [s, c]]))
        inverse.append(np.block([[c.T, s.T], [-s.T, c.T]]))
    sides = []
    for axis in (1, 2):
        for table in (np.stack(forward), np.stack(inverse)):
            table = table.astype(np.float32)
            if axis == 2:
                table = np.swapaxes(table, 1, 2)
            hi = table.astype(BF)
            lo = (table - hi.astype(np.float32)).astype(BF)
            sides.append(np.concatenate([hi, lo, hi], axis=axis))
    order = np.concatenate([np.arange(0, window, 2), np.arange(1, window, 2)])
    shuffle = np.zeros((window, window), np.float32)
    shuffle[order, np.arange(window)] = 1.0
    return sides[0], sides[1], sides[2], sides[3], shuffle.astype(BF)


def cat(parts, axis):
    return jnp.concatenate(parts, axis=axis)


def mm(a, b):
    return jnp.dot(a, b, preferred_element_type=F32)


def make_compute(window, modes, slots, tile_rows, tile_cols):
    w, half = window, window // 2
    ch = 32
    ext_rows, ext_cols = tile_rows + w, tile_cols + w

    def kernel(meta, own, right, low, diag, probe, amps, rf, ri, lf, li, shuffle,
               g_own, g_right, g_low, g_diag, pg, along,
               ext, grad, amp_buf, win, fac, lhs, rhs, mid, far, near, amp_sem, sem):
        count = meta[2 * slots]
        mine = meta[2 * slots + 1]
        def quarters(whole, parts):
            pairs = []
            for k in range(4):
                for t in range(2):
                    down = slice(tile_rows, ext_rows) if k >= 2 else slice(0, tile_rows)
                    pairs.append((whole.at[2 * (k % 2) + t, :, down, :], parts[k].at[:, :, 128 * t:128 * t + 128]))
            return pairs

        loads = [
            pltpu.make_async_copy(part, inside, sem.at[k])
            for k, (inside, part) in enumerate(quarters(ext, (own, right, low, diag)))
        ]
        for copy in loads:
            copy.start()

        def amp_copies(slot, place):
            return [
                pltpu.make_async_copy(
                    amps.at[slot, :, 128 * t:128 * t + 128], amp_buf.at[place, t], amp_sem.at[place, t]
                )
                for t in range(2)
            ]

        for copy in amp_copies(0, 0):
            copy.start()

        def clear(i, carry):
            at = pl.multiple_of(i * ch, ch)
            for c in range(2):
                for t in range(4):
                    grad[t, c, pl.ds(at, ch), :] = jnp.zeros((ch, 128), F32)
            return carry

        lax.fori_loop(0, ext_rows // ch, clear, 0)
        pg[...] = jnp.zeros(pg.shape, F32)

        def no_shift(i, carry):
            along[0, i] = 0.0
            along[1, i] = 0.0
            return carry

        lax.fori_loop(0, slots, no_shift, 0)
        for copy in loads:
            copy.wait()

        def do_slot(slot, carry):
            row = meta[slot]
            col = meta[slots + slot]
            tile_at = col // 128
            off = lax.rem(col, 128)
            back = lax.rem(w + 128 - off, w + 128)
            place = lax.rem(slot, 2)
            for copy in amp_copies(slot, place):
                copy.wait()

            @pl.when(slot + 1 < count)
            def _():
                for copy in amp_copies(slot + 1, 1 - place):
                    copy.start()

            for c in range(2):
                for r in range(0, w, ch):
                    wide = cat([ext[tile_at + t, c, pl.ds(row + r, ch), :] for t in range(3)], 1)
                    win[c, r:r + ch, :] = pltpu.roll(wide, back, 1)[:, :w]

            for parity in range(2):
                a = cat([amp_buf[place, t, pl.ds(parity, half, stride=2), :] for t in range(2)], 1)
                a0, rest = a.astype(BF), None
                r1 = a - a0.astype(F32)
                a1 = r1.astype(BF)
                a2 = (r1 - a1.astype(F32)).astype(BF)
                fac[parity] = mm(a0, shuffle[...]) + mm(a1, shuffle[...]) + mm(a2, shuffle[...])

            for m in range(modes):
                for r in range(0, w, ch):
                    vre, vim = win[0, r:r + ch, :], win[1, r:r + ch, :]
                    pre, pim = probe[0, m, r:r + ch, :], probe[1, m, r:r + ch, :]
                    are = pre * vre - pim * vim
                    aim = pre * vim + pim * vre
                    for parity in range(2):
                        if parity == 0:
                            x = cat([are[:, :half] + are[:, half:], aim[:, :half] + aim[:, half:]], 1)
                        else:
                            x = cat([are[:, :half] - are[:, half:], aim[:, :half] - aim[:, half:]], 1)
                        hi, lo = hi_lo(x)
                        lhs[m, parity, r:r + ch, :w] = hi
                        lhs[m, parity, r:r + ch, w:] = lo
                for parity in range(2):
                    hi, lo = lhs[m, parity, :, :w], lhs[m, parity, :, w:]
                    mid[m, parity] = mm(cat([hi, hi, lo], 1), rf[parity])
                for r in range(0, half, ch):
                    e_top, e_bot = mid[m, 0, r:r + ch, :], mid[m, 0, half + r:half + r + ch, :]
                    o_top, o_bot = mid[m, 1, r:r + ch, :], mid[m, 1, half + r:half + r + ch, :]
                    for parity in range(2):
                        if parity == 0:
                            e, o = e_top + e_bot, o_top + o_bot
                        else:
                            e, o = e_top - e_bot, o_top - o_bot
                        hi, lo = hi_lo(cat([e[:, :half], o[:, :half]], 1))
                        rhs[m, parity, 0, r:r + ch, :] = hi
                        rhs[m, parity, 1, r:r + ch, :] = lo
                        hi, lo = hi_lo(cat([e[:, half:], o[:, half:]], 1))
                        rhs[m, parity, 0, half + r:half + r + ch, :] = hi
                        rhs[m, parity, 1, half + r:half + r + ch, :] = lo
                for parity in range(2):
                    hi, lo = rhs[m, parity, 0], rhs[m, parity, 1]
                    far[m, parity] = mm(lf[parity], cat([hi, hi, lo], 0))

            for parity in range(2):
                for r in range(0, half, ch):
                    total = None
                    for m in range(modes):
                        re = far[m, parity, r:r + ch, :]
                        im = far[m, parity, half + r:half + r + ch, :]
                        term = re * re + im * im
                        total = term if total is None else total + term
                    f = 0.25 * (1.0 - fac[parity, r:r + ch, :] * lax.rsqrt(total + 0.5))
                    fac[parity, r:r + ch, :] = f

            for m in range(modes):
                for parity in range(2):
                    for r in range(0, half, ch):
                        f = fac[parity, r:r + ch, :]
                        for part in range(2):
                            at = part * half + r
                            hi, lo = hi_lo(f * far[m, parity, at:at + ch, :])
                            rhs[m, parity, 0, at:at + ch, :] = hi
                            rhs[m, parity, 1, at:at + ch, :] = lo
                for parity in range(2):
                    hi, lo = rhs[m, parity, 0], rhs[m, parity, 1]
                    mid[m, parity] = mm(li[parity], cat([hi, hi, lo], 0))
                for r in range(0, half, ch):
                    e_re, e_im = mid[m, 0, r:r + ch, :], mid[m, 0, half + r:half + r + ch, :]
                    o_re, o_im = mid[m, 1, r:r + ch, :], mid[m, 1, half + r:half + r + ch, :]
                    for top in range(2):
                        if top == 0:
                            re, im = e_re + o_re, e_im + o_im
                        else:
                            re, im = e_re - o_re, e_im - o_im
                        at = top * half + r
                        for parity in range(2):
                            cols = slice(parity * half, parity * half + half)
                            hi, lo = hi_lo(cat([re[:, cols], im[:, cols]], 1))
                            lhs[m, parity, at:at + ch, :w] = hi
                            lhs[m, parity, at:at + ch, w:] = lo
                for parity in range(2):
                    hi, lo = lhs[m, parity, :, :w], lhs[m, parity, :, w:]
                    near[m, parity] = mm(cat([hi, hi, lo], 1), ri[parity])

            rows_sum = jnp.zeros((8, w), F32)
            cols_sum = jnp.zeros((8, w), F32)
            lanes = lax.broadcasted_iota(jnp.int32, (ch, w), 1)
            inner = (lanes >= 1) & (lanes <= w - 2)

            def near_of(m, r):
                e, o = near[m, 0, pl.ds(r, ch), :], near[m, 1, pl.ds(r, ch), :]
                s, d = e + o, e - o
                return cat([s[:, :half], d[:, :half]], 1), cat([s[:, half:], d[:, half:]], 1)

            for r in range(0, w, ch):
                gre = gim = None
                for m in range(modes):
                    nre, nim = near_of(m, r)
                    pre, pim = probe[0, m, r:r + ch, :], probe[1, m, r:r + ch, :]
                    tre = pre * nre + pim * nim
                    tim = pre * nim - pim * nre
                    gre = tre if gre is None else gre + tre
                    gim = tim if gim is None else gim + tim
                for c, g in ((0, gre), (1, gim)):
                    spread = pltpu.roll(cat([g, jnp.zeros((ch, 128), F32)], 1), off, 1)
                    for t in range(3):
                        grad[tile_at + t, c, pl.ds(row + r, ch), :] += spread[:, 128 * t:128 * t + 128]
                vre, vim = win[0, r:r + ch, :], win[1, r:r + ch, :]
                nre, nim = near_of(mine, r)
                pg[0, r:r + ch, :] += vre * nre + vim * nim
                pg[1, r:r + ch, :] += vre * nim - vim * nre
                dre = pltpu.roll(vre, w - 1, 1) - pltpu.roll(vre, 1, 1)
                dim = pltpu.roll(vim, w - 1, 1) - pltpu.roll(vim, 1, 1)
                t = jnp.where(inner, gre * dre + gim * dim, 0.0)
                cols_sum = cols_sum + jnp.sum(t.reshape(ch // 8, 8, w), axis=0)
                lo_r, hi_r = max(r, 1), min(r + ch, w - 1)
                up = [ext_rows_slice(win, c, r + 1, ch, w) for c in range(2)]
                dn = [ext_rows_slice(win, c, r - 1, ch, w) for c in range(2)]
                t = gre * (up[0] - dn[0]) + gim * (up[1] - dn[1])
                if lo_r != r or hi_r != r + ch:
                    idx = lax.broadcasted_iota(jnp.int32, (ch, w), 0) + r
                    t = jnp.where((idx >= lo_r) & (idx < hi_r), t, 0.0)
                rows_sum = rows_sum + jnp.sum(t.reshape(ch // 8, 8, w), axis=0)
            along[0, slot] = jnp.sum(rows_sum) * (0.5 / w)
            along[1, slot] = jnp.sum(cols_sum) * (0.5 / w)
            return carry

        def ext_rows_slice(ref, c, start, size, width):
            if start < 0:
                return cat([ref[c, 0:1, :], ref[c, 0:size - 1, :]], 0)
            if start + size > w:
                return cat([ref[c, start:w, :], ref[c, w - 1:w, :]], 0)
            return ref[c, start:start + size, :]

        lax.fori_loop(0, count, do_slot, 0)
        stores = [
            pltpu.make_async_copy(inside, part, sem.at[k])
            for k, (inside, part) in enumerate(quarters(grad, (g_own, g_right, g_low, g_diag)))
        ]
        for copy in stores:
            copy.start()
        for copy in stores:
            copy.wait()

    hbm = pl.BlockSpec(memory_space=pl.ANY)
    vmem = pl.BlockSpec(memory_space=pltpu.VMEM)
    smem = pl.BlockSpec(memory_space=pltpu.SMEM)
    shape = jax.ShapeDtypeStruct
    return pl.pallas_call(
        kernel,
        name="slots",
        in_specs=[smem, hbm, hbm, hbm, hbm, vmem, hbm, vmem, vmem, vmem, vmem, vmem],
        out_specs=[hbm, hbm, hbm, hbm, vmem, smem],
        out_shape=[
            shape((2, tile_rows, tile_cols), F32),
            shape((2, tile_rows, w), F32),
            shape((2, w, tile_cols), F32),
            shape((2, w, w), F32),
            shape((2, w, w), F32),
            shape((2, slots), F32),
        ],
        scratch_shapes=[
            pltpu.VMEM((ext_cols // 128, 2, ext_rows, 128), F32),
            pltpu.VMEM((ext_cols // 128, 2, ext_rows, 128), F32),
            pltpu.VMEM((2, 2, w, 128), F32),
            pltpu.VMEM((2, w, w), F32),
            pltpu.VMEM((2, half, w), F32),
            pltpu.VMEM((modes, 2, w, 2 * w), BF),
            pltpu.VMEM((modes, 2, 2, w, w), BF),
            pltpu.VMEM((modes, 2, w, w), F32),
            pltpu.VMEM((modes, 2, w, w), F32),
            pltpu.VMEM((modes, 2, w, w), F32),
            pltpu.SemaphoreType.DMA((2, 2)),
            pltpu.SemaphoreType.DMA((8,)),
        ],
        compiler_params=pltpu.CompilerParams(vmem_limit_bytes=60 << 20),
        cost_estimate=pl.CostEstimate(flops=10**11, bytes_accessed=10**7, transcendentals=0),
    )


MESH = pl.DeviceIdType.MESH


def place():
    return lax.axis_index("row"), lax.axis_index("col"), lax.axis_index("mode")


def device(r, c, m):
    return {"row": r, "col": c, "mode": m}


def remote(src, dst, send, recv, to):
    return pltpu.make_async_remote_copy(
        src_ref=src, dst_ref=dst, send_sem=send, recv_sem=recv, device_id=to, device_id_type=MESH
    )


def greet(to):
    pl.semaphore_signal(pltpu.get_barrier_semaphore(), inc=1, device_id=to, device_id_type=MESH)


class Quarters:
    def __init__(self, src, dst, modes, rows, to_col, sems):
        r, c, m = place()
        self.m, self.modes = m, modes
        self.rows = rows // modes // CHUNKS
        self.src, self.dst = src, dst
        self.ys, self.yr, self.zs, self.zr, self.ts, self.tr = sems
        self.peer = device(r, to_col, m)
        self.next = device(r, c, lax.rem(m + 1, modes))
        self.prev = device(r, c, lax.rem(m + modes - 1, modes))

    def part(self, ref, owner, i):
        at = pl.multiple_of((owner * CHUNKS + i) * self.rows, self.rows)
        return ref.at[:, pl.ds(at, self.rows), :]

    def first(self, i):
        mine = self.part(self.src, self.m, i)
        return remote(mine, self.part(self.dst, self.m, i), self.ys.at[i], self.yr.at[i], self.peer)

    def ring(self, i, way):
        mine = self.part(self.dst, self.m, i)
        return remote(mine, mine, self.zs.at[way, i], self.zr.at[way, i], self.next if way == 0 else self.prev)

    def relay(self, i):
        back = self.modes - 1 if i < CHUNKS // 2 else 1
        block = self.part(self.dst, lax.rem(self.m + back, self.modes), i)
        return remote(block, block, self.ts.at[i], self.tr.at[i], self.next if i < CHUNKS // 2 else self.prev)

    def start(self):
        for i in range(CHUNKS):
            self.first(i).start()

    def sent(self):
        for i in range(CHUNKS):
            self.first(i).wait_send()

    def take(self):
        for i in range(CHUNKS):
            self.first(i).wait_recv()
            self.ring(i, 0).start()
            self.ring(i, 1).start()

    def finish(self):
        for i in range(CHUNKS):
            way = 0 if i < CHUNKS // 2 else 1
            self.ring(i, way).wait_recv()
            self.relay(i).start()
        for i in range(CHUNKS):
            way = 1 if i < CHUNKS // 2 else 0
            self.ring(i, way).wait_recv()
        for i in range(CHUNKS):
            self.relay(i).wait_recv()
        for i in range(CHUNKS):
            self.ring(i, 0).wait_send()
            self.ring(i, 1).wait_send()
            self.relay(i).wait_send()


CHUNKS = 4


def quarter_sems():
    one = pltpu.SemaphoreType.DMA((CHUNKS,))
    two = pltpu.SemaphoreType.DMA((2, CHUNKS))
    return [one, one, two, two, one, one]


def make_spread(window, modes, tile_rows, tile_cols, rows_n, cols_n):
    w = window

    def kernel(tile, probe, right, low, diag, gathered, *sems):
        quarter, (one_s, one_r, p_s, p_r, x_s, x_r, own_sem) = sems[:6], sems[6:]
        r, c, m = place()
        core = lax.rem(c, 2)
        other = c + 1 - 2 * core
        odd, even = core == 1, core == 0
        has_left, has_right = c > 0, c < cols_n - 1
        top = tile.at[:, pl.ds(0, w), :]

        for k in range(1, modes):
            greet(device(r, c, lax.rem(m + k, modes)))
        greet(device(r, other, m))
        greet(device(rows_n - 1 - r, c, m))
        count = modes + 1
        away = jnp.where(odd, jnp.minimum(c + 1, cols_n - 1), jnp.maximum(c - 1, 0))
        has_away = jnp.where(odd, has_right, has_left)

        @pl.when(has_away)
        def _():
            greet(device(r, away, m))

        has_diag = has_away & jnp.where(odd, r == 0, r == 1)

        @pl.when(has_diag)
        def _():
            greet(device(rows_n - 1 - r, away, m))

        pl.semaphore_wait(
            pltpu.get_barrier_semaphore(),
            count + has_away.astype(jnp.int32) + has_diag.astype(jnp.int32),
        )

        strip = Quarters(tile, right, modes, tile_rows, away, quarter)
        whole = remote(tile, right, one_s.at[0], one_r.at[0], device(r, other, m))
        down = remote(top, low, one_s.at[1], one_r.at[1], device(rows_n - 1 - r, c, m))
        corner = remote(top, diag, one_s.at[2], one_r.at[2], device(rows_n - 1 - r, away, m))
        corner_on = remote(low, diag, one_s.at[2], one_r.at[2], device(r, other, m))

        def probe_copy(k):
            half = gathered.at[pl.ds(core, 1), pl.ds(m, 1)]
            return remote(
                probe.at[pl.ds(core, 1)], half, p_s.at[k], p_r.at[k], device(r, c, lax.rem(m + k, modes))
            )

        def probe_pass(k):
            half = gathered.at[pl.ds(core, 1), pl.ds(lax.rem(m + modes - k, modes), 1)]
            return remote(half, half, x_s.at[k], x_r.at[k], device(r, other, m))

        @pl.when(even & has_left)
        def _():
            strip.start()

        @pl.when(r == 1)
        def _():
            down.start()

        @pl.when(even & has_diag)
        def _():
            corner.start()

        for k in (1, 3, 2):
            probe_copy(k).start()

        @pl.when(odd)
        def _():
            whole.start()

        keep = pltpu.make_async_copy(probe, gathered.at[:, pl.ds(m, 1)], own_sem)
        keep.start()

        @pl.when(odd & has_right)
        def _():
            strip.take()

        @pl.when(r == 0)
        def _():
            down.wait_recv()

        @pl.when(odd & (r == 0))
        def _():
            corner_on.start()

        for k in (1, 3, 2):
            probe_copy(k).wait_recv()
            probe_pass(k).start()

        @pl.when(odd & has_right)
        def _():
            strip.finish()

        @pl.when(odd & has_diag)
        def _():
            corner.wait_recv()

        @pl.when(even)
        def _():
            whole.wait_recv()

        @pl.when(even & (r == 0))
        def _():
            corner_on.wait_recv()

        for k in (1, 3, 2):
            probe_pass(k).wait_recv()
            probe_pass(k).wait_send()
            probe_copy(k).wait_send()
        keep.wait()

        @pl.when(odd)
        def _():
            whole.wait_send()

        @pl.when(odd & (r == 0))
        def _():
            corner_on.wait_send()

        @pl.when(even & has_left)
        def _():
            strip.sent()

        @pl.when(r == 1)
        def _():
            down.wait_send()

        @pl.when(even & has_diag)
        def _():
            corner.wait_send()

    hbm = pl.BlockSpec(memory_space=pl.ANY)
    shape = jax.ShapeDtypeStruct
    return pl.pallas_call(
        kernel,
        name="spread",
        in_specs=[hbm, hbm],
        out_specs=[hbm] * 4,
        out_shape=[
            shape((2, tile_rows, tile_cols), F32),
            shape((2, w, tile_cols), F32),
            shape((2, w, tile_cols), F32),
            shape((2, modes, w, w), F32),
        ],
        scratch_shapes=quarter_sems() + [pltpu.SemaphoreType.DMA((3,))] * 2
        + [pltpu.SemaphoreType.DMA((modes,))] * 4 + [pltpu.SemaphoreType.DMA],
        compiler_params=pltpu.CompilerParams(collective_id=0, has_side_effects=True),
    )


def make_collect(window, modes, tile_rows, tile_cols, rows_n, cols_n):
    w = window
    group = rows_n * cols_n
    piece = 2 * w // group

    def kernel(g_right, g_low, g_diag, pg, right, low, diag, total, *sems):
        quarter, (one_s, one_r, a_s, a_r, b_s, b_r, in_sem, got, mine) = sems[:6], sems[6:]
        r, c, m = place()
        me = r * cols_n + c
        core = lax.rem(c, 2)
        other = c + 1 - 2 * core
        odd, even = core == 1, core == 0
        away = jnp.where(odd, jnp.minimum(c + 1, cols_n - 1), jnp.maximum(c - 1, 0))
        has_away = jnp.where(odd, c < cols_n - 1, c > 0)

        def partner(k):
            p = lax.rem(me + k, group)
            return device(p // cols_n, lax.rem(p, cols_n), m)

        def hello(k, carry):
            greet(partner(k))
            return carry

        lax.fori_loop(1, group, hello, 0)
        for k in (1, modes - 1):
            greet(device(r, c, lax.rem(m + k, modes)))
        pl.semaphore_wait(pltpu.get_barrier_semaphore(), group + 1)

        strip = Quarters(g_right, right, modes, tile_rows, away, quarter)
        whole = remote(g_right, right, one_s.at[0], one_r.at[0], device(r, other, m))
        down = remote(g_low, low, one_s.at[1], one_r.at[1], device(rows_n - 1 - r, c, m))
        to_c = jnp.minimum(c + 1, cols_n - 1)
        corner = remote(g_diag, diag, one_s.at[2], one_r.at[2], device(rows_n - 1 - r, to_c, m))
        send_diag = (r == 0) & (c < cols_n - 1)
        take_diag = (r == 1) & (c > 0)

        def scatter(k):
            p = lax.rem(me + k, group)
            rows = pl.ds(pl.multiple_of(p * piece, piece), piece)
            return remote(pg.at[rows, :], got.at[k], a_s, a_r, partner(k))

        def scatter_go(k, carry):
            scatter(k).start()
            return carry

        lax.fori_loop(1, group, scatter_go, 0)
        at_me = pl.ds(pl.multiple_of(me * piece, piece), piece)
        own = pltpu.make_async_copy(pg.at[at_me, :], got.at[0], in_sem)
        own.start()

        @pl.when(odd & has_away)
        def _():
            strip.start()

        @pl.when(r == 0)
        def _():
            down.start()

        @pl.when(send_diag)
        def _():
            corner.start()

        @pl.when(even)
        def _():
            whole.start()

        own.wait()
        rest = got.at[pl.ds(1, group - 1)]
        pltpu.make_async_copy(rest, rest, a_r).wait()

        def add(k, acc):
            return acc + got[k]

        mine[...] = lax.fori_loop(1, group, add, got[0]) * (1.0 / 16.0)

        def share(k):
            return remote(mine, total.at[at_me, :], b_s, b_r, partner(k))

        def share_go(k, carry):
            share(k).start()
            return carry

        keep = pltpu.make_async_copy(mine, total.at[at_me, :], in_sem)
        keep.start()
        lax.fori_loop(1, group, share_go, 0)

        @pl.when(even & has_away)
        def _():
            strip.take()
            strip.finish()

        @pl.when(r == 1)
        def _():
            down.wait_recv()

        @pl.when(take_diag)
        def _():
            corner.wait_recv()

        @pl.when(odd)
        def _():
            whole.wait_recv()

        keep.wait()
        many = total.at[pl.ds(0, (group - 1) * piece), :]
        pltpu.make_async_copy(many, many, b_r).wait()
        pltpu.make_async_copy(rest, rest, a_s).wait()
        pltpu.make_async_copy(many, many, b_s).wait()

        @pl.when(odd & has_away)
        def _():
            strip.sent()

        @pl.when(r == 0)
        def _():
            down.wait_send()

        @pl.when(send_diag)
        def _():
            corner.wait_send()

        @pl.when(even)
        def _():
            whole.wait_send()

    hbm = pl.BlockSpec(memory_space=pl.ANY)
    shape = jax.ShapeDtypeStruct
    dma = pltpu.SemaphoreType.DMA
    return pl.pallas_call(
        kernel,
        name="collect",
        in_specs=[hbm] * 4,
        out_specs=[hbm] * 4,
        out_shape=[
            shape((2, tile_rows, tile_cols), F32),
            shape((2, w, tile_cols), F32),
            shape((2, w, tile_cols), F32),
            shape((2 * w, w), F32),
        ],
        scratch_shapes=quarter_sems() + [dma((3,))] * 2 + [dma] * 5
        + [pltpu.VMEM((group, piece, w), F32), pltpu.VMEM((piece, w), F32)],
        compiler_params=pltpu.CompilerParams(collective_id=1, has_side_effects=True),
    )


def per_device(object_slab, probe_modes, amplitudes, scan_counts, scan_positions):
    window = probe_modes.shape[-1]
    tile_rows, tile_cols = object_slab.shape[1:]
    slots = amplitudes.shape[0]
    modes, cols_n, rows_n = (lax.axis_size(a) for a in ("mode", "col", "row"))
    row_id, col_id, mode_id = place()
    sizes = (window, modes, tile_rows, tile_cols, rows_n, cols_n)
    right, low, diag, probe = make_spread(*sizes)(object_slab, probe_modes)
    meta = jnp.concatenate([
        scan_positions[0] - row_id * tile_rows,
        scan_positions[1] - col_id * tile_cols,
        lax.dynamic_slice(scan_counts, (row_id * cols_n + col_id,), (1,)),
        mode_id[None].astype(jnp.int32),
    ])
    consts = [jnp.asarray(t) for t in tables(window)]
    compute = make_compute(window, modes, slots, tile_rows, tile_cols)
    g_own, g_right, g_low, g_diag, pg, shift = compute(
        meta, object_slab, right, low, diag, probe, amplitudes, *consts
    )
    from_left, from_up, from_diag, total = make_collect(*sizes)(
        g_right, g_low, g_diag, pg.reshape(2 * window, window)
    )
    below, inner = row_id > 0, col_id > 0
    strip = jnp.where(inner, from_left, 0.0)
    top = jnp.where(below, from_up, 0.0) + jnp.where(below & inner, from_diag, 0.0)
    top = jnp.pad(top, ((0, 0), (0, tile_rows - window), (0, 0)))
    grad = g_own + strip + top
    return (grad, total.reshape(2, 1, window, window), shift)


def solution(mesh):
    in_specs = (
        P(None, "row", "col"),
        P(None, "mode", None, None),
        P(("row", "col"), None, None),
        P(),
        P(None, ("row", "col")),
    )
    out_specs = (P(None, "row", "col"), P(None, "mode", None, None), P(None, ("row", "col")))
    return jax.shard_map(
        per_device, mesh=mesh, in_specs=in_specs, out_specs=out_specs, check_vma=False
    )
```

```python
import math
import functools
import numpy as np
import jax
import jax.numpy as jnp
from jax import lax
from jax.experimental import pallas as pl
from jax.experimental.pallas import tpu as pltpu
from jax.sharding import PartitionSpec as P

BF = jnp.bfloat16
F32 = jnp.float32


def hi_lo(x):
    hi = x.astype(BF)
    lo = (x - hi.astype(F32)).astype(BF)
    return hi, lo


def tables(window):
    half = window // 2
    n = np.arange(half)[:, None]
    j = np.arange(half)[None, :]
    scale = 1.0 / math.sqrt(window)
    forward, inverse = [], []
    for parity in range(2):
        angle = 2.0 * math.pi * ((n * (2 * j + parity)) % window) / window
        c, s = np.cos(angle) * scale, np.sin(angle) * scale
        forward.append(np.block([[c, -s], [s, c]]))
        inverse.append(np.block([[c.T, s.T], [-s.T, c.T]]))
    sides = []
    for axis in (1, 2):
        for table in (np.stack(forward), np.stack(inverse)):
            table = table.astype(np.float32)
            if axis == 2:
                table = np.swapaxes(table, 1, 2)
            hi = table.astype(BF)
            lo = (table - hi.astype(np.float32)).astype(BF)
            sides.append(np.concatenate([hi, lo, hi], axis=axis))
    order = np.concatenate([np.arange(0, window, 2), np.arange(1, window, 2)])
    shuffle = np.zeros((window, window), np.float32)
    shuffle[order, np.arange(window)] = 1.0
    return sides[0], sides[1], sides[2], sides[3], shuffle.astype(BF)


def cat(parts, axis):
    return jnp.concatenate(parts, axis=axis)


def mm(a, b):
    return jnp.dot(a, b, preferred_element_type=F32)


def make_compute(window, modes, slots, tile_rows, tile_cols, cols_n):
    w, half = window, window // 2
    ch = 32
    ext_rows, ext_cols = tile_rows + w, tile_cols + w

    def kernel(positions, counts, own, right, low, diag, probe, amps, rf, ri, lf, li, shuffle,
               g_own, g_right, g_low, g_diag, pg, along,
               ext, grad, amp_buf, win, fac, lhs, rhs, mid, far, near, amp_sem, sem):
        row_id, col_id, mine = place()
        count = counts[row_id * cols_n + col_id]
        def quarters(whole, parts):
            pairs = []
            for k in range(4):
                for t in range(2):
                    down = slice(tile_rows, ext_rows) if k >= 2 else slice(0, tile_rows)
                    pairs.append((whole.at[2 * (k % 2) + t, :, down, :], parts[k].at[:, :, 128 * t:128 * t + 128]))
            return pairs

        loads = [
            pltpu.make_async_copy(part, inside, sem.at[k])
            for k, (inside, part) in enumerate(quarters(ext, (own, right, low, diag)))
        ]
        for copy in loads:
            copy.start()

        def amp_copies(slot, place):
            return [
                pltpu.make_async_copy(
                    amps.at[slot, :, 128 * t:128 * t + 128], amp_buf.at[place, t], amp_sem.at[place, t]
                )
                for t in range(2)
            ]

        for copy in amp_copies(0, 0):
            copy.start()

        def clear(i, carry):
            at = pl.multiple_of(i * ch, ch)
            for c in range(2):
                for t in range(4):
                    grad[t, c, pl.ds(at, ch), :] = jnp.zeros((ch, 128), F32)
            return carry

        lax.fori_loop(0, ext_rows // ch, clear, 0)
        pg[...] = jnp.zeros(pg.shape, F32)

        def no_shift(i, carry):
            along[0, i] = 0.0
            along[1, i] = 0.0
            return carry

        lax.fori_loop(0, slots, no_shift, 0)
        for copy in loads:
            copy.wait()

        def do_slot(slot, carry):
            row = positions[0, slot] - row_id * tile_rows
            col = positions[1, slot] - col_id * tile_cols
            tile_at = col // 128
            off = lax.rem(col, 128)
            back = lax.rem(w + 128 - off, w + 128)
            place = lax.rem(slot, 2)
            for copy in amp_copies(slot, place):
                copy.wait()

            @pl.when(slot + 1 < count)
            def _():
                for copy in amp_copies(slot + 1, 1 - place):
                    copy.start()

            for c in range(2):
                for r in range(0, w, ch):
                    wide = cat([ext[tile_at + t, c, pl.ds(row + r, ch), :] for t in range(3)], 1)
                    win[c, r:r + ch, :] = pltpu.roll(wide, back, 1)[:, :w]

            for parity in range(2):
                a = cat([amp_buf[place, t, pl.ds(parity, half, stride=2), :] for t in range(2)], 1)
                a0, rest = a.astype(BF), None
                r1 = a - a0.astype(F32)
                a1 = r1.astype(BF)
                a2 = (r1 - a1.astype(F32)).astype(BF)
                fac[parity] = mm(a0, shuffle[...]) + mm(a1, shuffle[...]) + mm(a2, shuffle[...])

            for m in range(modes):
                for r in range(0, w, ch):
                    vre, vim = win[0, r:r + ch, :], win[1, r:r + ch, :]
                    pre, pim = probe[0, m, r:r + ch, :], probe[1, m, r:r + ch, :]
                    are = pre * vre - pim * vim
                    aim = pre * vim + pim * vre
                    for parity in range(2):
                        if parity == 0:
                            x = cat([are[:, :half] + are[:, half:], aim[:, :half] + aim[:, half:]], 1)
                        else:
                            x = cat([are[:, :half] - are[:, half:], aim[:, :half] - aim[:, half:]], 1)
                        hi, lo = hi_lo(x)
                        lhs[m, parity, r:r + ch, :w] = hi
                        lhs[m, parity, r:r + ch, w:] = lo
                for parity in range(2):
                    hi, lo = lhs[m, parity, :, :w], lhs[m, parity, :, w:]
                    mid[m, parity] = mm(cat([hi, hi, lo], 1), rf[parity])
                for r in range(0, half, ch):
                    e_top, e_bot = mid[m, 0, r:r + ch, :], mid[m, 0, half + r:half + r + ch, :]
                    o_top, o_bot = mid[m, 1, r:r + ch, :], mid[m, 1, half + r:half + r + ch, :]
                    for parity in range(2):
                        if parity == 0:
                            e, o = e_top + e_bot, o_top + o_bot
                        else:
                            e, o = e_top - e_bot, o_top - o_bot
                        hi, lo = hi_lo(cat([e[:, :half], o[:, :half]], 1))
                        rhs[m, parity, 0, r:r + ch, :] = hi
                        rhs[m, parity, 1, r:r + ch, :] = lo
                        hi, lo = hi_lo(cat([e[:, half:], o[:, half:]], 1))
                        rhs[m, parity, 0, half + r:half + r + ch, :] = hi
                        rhs[m, parity, 1, half + r:half + r + ch, :] = lo
                for parity in range(2):
                    hi, lo = rhs[m, parity, 0], rhs[m, parity, 1]
                    far[m, parity] = mm(lf[parity], cat([hi, hi, lo], 0))

            for parity in range(2):
                for r in range(0, half, ch):
                    total = None
                    for m in range(modes):
                        re = far[m, parity, r:r + ch, :]
                        im = far[m, parity, half + r:half + r + ch, :]
                        term = re * re + im * im
                        total = term if total is None else total + term
                    f = 0.25 * (1.0 - fac[parity, r:r + ch, :] * lax.rsqrt(total + 0.5))
                    fac[parity, r:r + ch, :] = f

            for m in range(modes):
                for parity in range(2):
                    for r in range(0, half, ch):
                        f = fac[parity, r:r + ch, :]
                        for part in range(2):
                            at = part * half + r
                            hi, lo = hi_lo(f * far[m, parity, at:at + ch, :])
                            rhs[m, parity, 0, at:at + ch, :] = hi
                            rhs[m, parity, 1, at:at + ch, :] = lo
                for parity in range(2):
                    hi, lo = rhs[m, parity, 0], rhs[m, parity, 1]
                    mid[m, parity] = mm(li[parity], cat([hi, hi, lo], 0))
                for r in range(0, half, ch):
                    e_re, e_im = mid[m, 0, r:r + ch, :], mid[m, 0, half + r:half + r + ch, :]
                    o_re, o_im = mid[m, 1, r:r + ch, :], mid[m, 1, half + r:half + r + ch, :]
                    for top in range(2):
                        if top == 0:
                            re, im = e_re + o_re, e_im + o_im
                        else:
                            re, im = e_re - o_re, e_im - o_im
                        at = top * half + r
                        for parity in range(2):
                            cols = slice(parity * half, parity * half + half)
                            hi, lo = hi_lo(cat([re[:, cols], im[:, cols]], 1))
                            lhs[m, parity, at:at + ch, :w] = hi
                            lhs[m, parity, at:at + ch, w:] = lo
                for parity in range(2):
                    hi, lo = lhs[m, parity, :, :w], lhs[m, parity, :, w:]
                    near[m, parity] = mm(cat([hi, hi, lo], 1), ri[parity])

            rows_sum = jnp.zeros((8, w), F32)
            cols_sum = jnp.zeros((8, w), F32)
            lanes = lax.broadcasted_iota(jnp.int32, (ch, w), 1)
            inner = (lanes >= 1) & (lanes <= w - 2)

            def near_of(m, r):
                e, o = near[m, 0, pl.ds(r, ch), :], near[m, 1, pl.ds(r, ch), :]
                s, d = e + o, e - o
                return cat([s[:, :half], d[:, :half]], 1), cat([s[:, half:], d[:, half:]], 1)

            for r in range(0, w, ch):
                gre = gim = None
                for m in range(modes):
                    nre, nim = near_of(m, r)
                    pre, pim = probe[0, m, r:r + ch, :], probe[1, m, r:r + ch, :]
                    tre = pre * nre + pim * nim
                    tim = pre * nim - pim * nre
                    gre = tre if gre is None else gre + tre
                    gim = tim if gim is None else gim + tim
                for c, g in ((0, gre), (1, gim)):
                    spread = pltpu.roll(cat([g, jnp.zeros((ch, 128), F32)], 1), off, 1)
                    for t in range(3):
                        grad[tile_at + t, c, pl.ds(row + r, ch), :] += spread[:, 128 * t:128 * t + 128]
                vre, vim = win[0, r:r + ch, :], win[1, r:r + ch, :]
                nre, nim = near_of(mine, r)
                pg[0, r:r + ch, :] += vre * nre + vim * nim
                pg[1, r:r + ch, :] += vre * nim - vim * nre
                dre = pltpu.roll(vre, w - 1, 1) - pltpu.roll(vre, 1, 1)
                dim = pltpu.roll(vim, w - 1, 1) - pltpu.roll(vim, 1, 1)
                t = jnp.where(inner, gre * dre + gim * dim, 0.0)
                cols_sum = cols_sum + jnp.sum(t.reshape(ch // 8, 8, w), axis=0)
                lo_r, hi_r = max(r, 1), min(r + ch, w - 1)
                up = [ext_rows_slice(win, c, r + 1, ch, w) for c in range(2)]
                dn = [ext_rows_slice(win, c, r - 1, ch, w) for c in range(2)]
                t = gre * (up[0] - dn[0]) + gim * (up[1] - dn[1])
                if lo_r != r or hi_r != r + ch:
                    idx = lax.broadcasted_iota(jnp.int32, (ch, w), 0) + r
                    t = jnp.where((idx >= lo_r) & (idx < hi_r), t, 0.0)
                rows_sum = rows_sum + jnp.sum(t.reshape(ch // 8, 8, w), axis=0)
            along[0, slot] = jnp.sum(rows_sum) * (0.5 / w)
            along[1, slot] = jnp.sum(cols_sum) * (0.5 / w)
            return carry

        def ext_rows_slice(ref, c, start, size, width):
            if start < 0:
                return cat([ref[c, 0:1, :], ref[c, 0:size - 1, :]], 0)
            if start + size > w:
                return cat([ref[c, start:w, :], ref[c, w - 1:w, :]], 0)
            return ref[c, start:start + size, :]

        lax.fori_loop(0, count, do_slot, 0)
        stores = [
            pltpu.make_async_copy(inside, part, sem.at[k])
            for k, (inside, part) in enumerate(quarters(grad, (g_own, g_right, g_low, g_diag)))
        ]
        for copy in stores:
            copy.start()
        for copy in stores:
            copy.wait()

    hbm = pl.BlockSpec(memory_space=pl.ANY)
    vmem = pl.BlockSpec(memory_space=pltpu.VMEM)
    smem = pl.BlockSpec(memory_space=pltpu.SMEM)
    shape = jax.ShapeDtypeStruct
    return pl.pallas_call(
        kernel,
        name="slots",
        in_specs=[smem, smem, hbm, hbm, hbm, hbm, vmem, hbm, vmem, vmem, vmem, vmem, vmem],
        out_specs=[hbm, hbm, hbm, hbm, vmem, smem],
        out_shape=[
            shape((2, tile_rows, tile_cols), F32),
            shape((2, tile_rows, w), F32),
            shape((2, w, tile_cols), F32),
            shape((2, w, w), F32),
            shape((2, w, w), F32),
            shape((2, slots), F32),
        ],
        scratch_shapes=[
            pltpu.VMEM((ext_cols // 128, 2, ext_rows, 128), F32),
            pltpu.VMEM((ext_cols // 128, 2, ext_rows, 128), F32),
            pltpu.VMEM((2, 2, w, 128), F32),
            pltpu.VMEM((2, w, w), F32),
            pltpu.VMEM((2, half, w), F32),
            pltpu.VMEM((modes, 2, w, 2 * w), BF),
            pltpu.VMEM((modes, 2, 2, w, w), BF),
            pltpu.VMEM((modes, 2, w, w), F32),
            pltpu.VMEM((modes, 2, w, w), F32),
            pltpu.VMEM((modes, 2, w, w), F32),
            pltpu.SemaphoreType.DMA((2, 2)),
            pltpu.SemaphoreType.DMA((8,)),
        ],
        compiler_params=pltpu.CompilerParams(vmem_limit_bytes=60 << 20),
        cost_estimate=pl.CostEstimate(flops=10**11, bytes_accessed=10**7, transcendentals=0),
    )


MESH = pl.DeviceIdType.MESH


def place():
    return lax.axis_index("row"), lax.axis_index("col"), lax.axis_index("mode")


def device(r, c, m):
    return {"row": r, "col": c, "mode": m}


def remote(src, dst, send, recv, to):
    return pltpu.make_async_remote_copy(
        src_ref=src, dst_ref=dst, send_sem=send, recv_sem=recv, device_id=to, device_id_type=MESH
    )


def greet(to):
    pl.semaphore_signal(pltpu.get_barrier_semaphore(), inc=1, device_id=to, device_id_type=MESH)


class Quarters:
    def __init__(self, src, dst, modes, rows, r, c, chunks, sems):
        me_r, me_c, m = place()
        self.m, self.modes, self.chunks = m, modes, chunks
        self.rows = rows // modes // chunks
        self.src, self.dst = src, dst
        self.ys, self.yr, self.zs, self.zr, self.ts, self.tr = sems
        self.peer = device(r, c, m)
        self.next = device(me_r, me_c, lax.rem(m + 1, modes))
        self.prev = device(me_r, me_c, lax.rem(m + modes - 1, modes))

    def part(self, ref, owner, i):
        at = pl.multiple_of((owner * self.chunks + i) * self.rows, self.rows)
        return ref.at[:, pl.ds(at, self.rows), :]

    def first(self, i):
        mine = self.part(self.src, self.m, i)
        return remote(mine, self.part(self.dst, self.m, i), self.ys.at[i], self.yr.at[i], self.peer)

    def ring(self, i, way):
        mine = self.part(self.dst, self.m, i)
        return remote(mine, mine, self.zs.at[way, i], self.zr.at[way, i], self.next if way == 0 else self.prev)

    def way(self, i):
        return 0 if i < self.chunks // 2 else 1

    def relay(self, i):
        back = self.modes - 1 if self.way(i) == 0 else 1
        block = self.part(self.dst, lax.rem(self.m + back, self.modes), i)
        return remote(block, block, self.ts.at[i], self.tr.at[i], self.next if self.way(i) == 0 else self.prev)

    def start(self):
        for i in range(self.chunks):
            self.first(i).start()

    def sent(self):
        for i in range(self.chunks):
            self.first(i).wait_send()

    def take(self, some=None):
        for i in range(self.chunks) if some is None else some:
            self.first(i).wait_recv()
            self.ring(i, 0).start()
            self.ring(i, 1).start()

    def turn(self):
        for i in range(self.chunks):
            self.ring(i, self.way(i)).wait_recv()
            self.relay(i).start()

    def finish(self):
        for i in range(self.chunks):
            self.ring(i, 1 - self.way(i)).wait_recv()
            self.relay(i).wait_recv()
        for i in range(self.chunks):
            self.ring(i, 0).wait_send()
            self.ring(i, 1).wait_send()
            self.relay(i).wait_send()


STRIP, EDGE = 4, 2


def quarter_sems(chunks):
    one = pltpu.SemaphoreType.DMA((chunks,))
    two = pltpu.SemaphoreType.DMA((2, chunks))
    return [one, one, two, two, one, one]


def when(cond, *steps):
    @pl.when(cond)
    def _():
        for step in steps:
            step()


def make_spread(window, modes, tile_rows, tile_cols, rows_n, cols_n):
    w = window

    def kernel(tile, probe, right, low, diag, gathered, *sems):
        strip_sems, low_sems, diag_sems = sems[:6], sems[6:12], sems[12:18]
        one_s, one_r, p_s, p_r, x_s, x_r, own_sem = sems[18:]
        r, c, m = place()
        core = lax.rem(c, 2)
        other = c + 1 - 2 * core
        odd, even = core == 1, core == 0
        away = jnp.where(odd, jnp.minimum(c + 1, cols_n - 1), jnp.maximum(c - 1, 0))
        has_away = jnp.where(odd, c < cols_n - 1, c > 0)
        has_diag = has_away & jnp.where(odd, r == 0, r == 1)
        flip = rows_n - 1 - r

        for k in range(1, modes):
            greet(device(r, c, lax.rem(m + k, modes)))
        greet(device(r, other, m))
        greet(device(flip, c, m))
        when(has_away, lambda: greet(device(r, away, m)))
        when(has_diag, lambda: greet(device(flip, away, m)))
        pl.semaphore_wait(
            pltpu.get_barrier_semaphore(),
            modes + 1 + has_away.astype(jnp.int32) + has_diag.astype(jnp.int32),
        )

        strip = Quarters(tile, right, modes, tile_rows, r, away, STRIP, strip_sems)
        down = Quarters(tile, low, modes, w, flip, c, EDGE, low_sems)
        corner = Quarters(tile, diag, modes, w, flip, away, EDGE, diag_sems)
        whole = remote(tile, right, one_s.at[0], one_r.at[0], device(r, other, m))
        corner_on = remote(low, diag, one_s.at[1], one_r.at[1], device(r, other, m))

        def probe_copy(k):
            half = gathered.at[pl.ds(core, 1), pl.ds(m, 1)]
            return remote(
                probe.at[pl.ds(core, 1)], half, p_s.at[k], p_r.at[k], device(r, c, lax.rem(m + k, modes))
            )

        def probe_pass(k):
            half = gathered.at[pl.ds(core, 1), pl.ds(lax.rem(m + modes - k, modes), 1)]
            return remote(half, half, x_s.at[k], x_r.at[k], device(r, other, m))

        far = (1, modes - 1, 2)
        when(even & has_away, strip.start)
        when(r == 1, down.start)
        when(even & has_diag, corner.start)
        for k in far:
            probe_copy(k).start()
        when(odd, whole.start)
        keep = pltpu.make_async_copy(probe, gathered.at[:, pl.ds(m, 1)], own_sem)
        keep.start()

        when(odd & has_away, lambda: strip.take([0]))
        when(r == 0, down.take)
        when(odd & has_diag, corner.take)
        when(odd & has_away, lambda: strip.take([1, 2, 3]))
        when(r == 0, down.turn)
        when(odd & has_diag, corner.turn)
        when(odd & has_away, strip.turn)
        when(r == 0, down.finish)
        when(odd & (r == 0), corner_on.start)
        for k in far:
            probe_copy(k).wait_recv()
            probe_pass(k).start()
        when(odd & has_diag, corner.finish)
        when(odd & has_away, strip.finish)
        when(even, whole.wait_recv)
        when(even & (r == 0), corner_on.wait_recv)
        for k in far:
            probe_pass(k).wait_recv()
            probe_pass(k).wait_send()
            probe_copy(k).wait_send()
        keep.wait()
        when(odd, whole.wait_send)
        when(odd & (r == 0), corner_on.wait_send)
        when(even & has_away, strip.sent)
        when(r == 1, down.sent)
        when(even & has_diag, corner.sent)

    hbm = pl.BlockSpec(memory_space=pl.ANY)
    shape = jax.ShapeDtypeStruct
    dma = pltpu.SemaphoreType.DMA
    return pl.pallas_call(
        kernel,
        name="spread",
        in_specs=[hbm, hbm],
        out_specs=[hbm] * 4,
        out_shape=[
            shape((2, tile_rows, tile_cols), F32),
            shape((2, w, tile_cols), F32),
            shape((2, w, tile_cols), F32),
            shape((2, modes, w, w), F32),
        ],
        scratch_shapes=quarter_sems(STRIP) + quarter_sems(EDGE) + quarter_sems(EDGE)
        + [dma((2,))] * 2 + [dma((modes,))] * 4 + [dma],
        compiler_params=pltpu.CompilerParams(collective_id=0, has_side_effects=True),
    )


def make_collect(window, modes, tile_rows, tile_cols, rows_n, cols_n):
    w = window
    chips = rows_n * cols_n // 2
    piece = w // chips

    def kernel(g_right, g_low, g_diag, pg, right, low, diag, total, *sems):
        strip_sems, low_sems, diag_sems = sems[:6], sems[6:12], sems[12:18]
        one_s, one_r, x_s, x_r, y_s, y_r, a_s, a_r, b_s, b_r, in_sem, pair, got, mine = sems[18:]
        r, c, m = place()
        core = lax.rem(c, 2)
        chip = r * (cols_n // 2) + c // 2
        other = c + 1 - 2 * core
        odd, even = core == 1, core == 0
        away = jnp.where(odd, jnp.minimum(c + 1, cols_n - 1), jnp.maximum(c - 1, 0))
        has_away = jnp.where(odd, c < cols_n - 1, c > 0)
        flip = rows_n - 1 - r
        over = jnp.where(r == 0, jnp.minimum(c + 1, cols_n - 1), jnp.maximum(c - 1, 0))
        has_over = jnp.where(r == 0, c < cols_n - 1, c > 0)

        def partner(k):
            p = lax.rem(chip + k, chips)
            return device(p // (cols_n // 2), 2 * lax.rem(p, cols_n // 2) + core, m)

        def hello(k, carry):
            greet(partner(k))
            return carry

        lax.fori_loop(1, chips, hello, 0)
        greet(device(r, other, m))
        for k in (1, modes - 1):
            greet(device(r, c, lax.rem(m + k, modes)))
        when(has_away, lambda: greet(device(r, away, m)))
        when(has_over, lambda: greet(device(flip, over, m)))
        pl.semaphore_wait(
            pltpu.get_barrier_semaphore(),
            chips + 2 + has_away.astype(jnp.int32) + has_over.astype(jnp.int32),
        )

        strip = Quarters(g_right, right, modes, tile_rows, r, away, STRIP, strip_sems)
        down = Quarters(g_low, low, modes, w, flip, c, EDGE, low_sems)
        corner = Quarters(g_diag, diag, modes, w, flip, over, EDGE, diag_sems)
        whole = remote(g_right, right, one_s, one_r, device(r, other, m))
        my_half = pl.ds(pl.multiple_of(core * w, w), w)
        its_half = pl.ds(pl.multiple_of((1 - core) * w, w), w)

        swap = remote(pg.at[its_half, :], pair.at[0], x_s, x_r, device(r, other, m))
        swap.start()
        own = pltpu.make_async_copy(pg.at[my_half, :], pair.at[1], in_sem)
        own.start()
        when(odd & has_away, strip.start)
        when(r == 0, down.start)
        when((r == 0) & has_over, corner.start)

        own.wait()
        swap.wait_recv()
        pair[1] = pair[0] + pair[1]
        when(even, whole.start)

        def scatter(k):
            p = lax.rem(chip + k, chips)
            rows = pl.ds(pl.multiple_of(p * piece, piece), piece)
            return remote(pair.at[1, rows, :], got.at[k], a_s, a_r, partner(k))

        def scatter_go(k, carry):
            scatter(k).start()
            return carry

        lax.fori_loop(1, chips, scatter_go, 0)
        when(even & has_away, lambda: strip.take([0]))
        when(r == 1, down.take)
        when((r == 1) & has_over, corner.take)

        rest = got.at[pl.ds(1, chips - 1)]
        pltpu.make_async_copy(rest, rest, a_r).wait()
        at_chip = pl.ds(pl.multiple_of(chip * piece, piece), piece)

        def add(k, acc):
            return acc + got[k]

        mine[...] = lax.fori_loop(1, chips, add, pair[1, at_chip, :]) * (1.0 / 16.0)
        at_me = pl.ds(pl.multiple_of(core * w + chip * piece, piece), piece)

        def share(k):
            return remote(mine, total.at[at_me, :], b_s, b_r, partner(k))

        def share_go(k, carry):
            share(k).start()
            return carry

        keep = pltpu.make_async_copy(mine, total.at[at_me, :], in_sem)
        keep.start()
        lax.fori_loop(1, chips, share_go, 0)

        when(even & has_away, lambda: strip.take([1, 2, 3]))
        when(r == 1, down.turn)
        when((r == 1) & has_over, corner.turn)
        when(even & has_away, strip.turn)

        keep.wait()
        many = total.at[pl.ds(0, (chips - 1) * piece), :]
        pltpu.make_async_copy(many, many, b_r).wait()
        give = remote(total.at[my_half, :], total.at[my_half, :], y_s, y_r, device(r, other, m))
        give.start()

        when(r == 1, down.finish)
        when((r == 1) & has_over, corner.finish)
        when(even & has_away, strip.finish)
        when(odd, whole.wait_recv)
        give.wait_recv()
        give.wait_send()
        swap.wait_send()
        pltpu.make_async_copy(rest, rest, a_s).wait()
        pltpu.make_async_copy(many, many, b_s).wait()
        when(odd & has_away, strip.sent)
        when(r == 0, down.sent)
        when((r == 0) & has_over, corner.sent)
        when(even, whole.wait_send)

    hbm = pl.BlockSpec(memory_space=pl.ANY)
    shape = jax.ShapeDtypeStruct
    dma = pltpu.SemaphoreType.DMA
    return pl.pallas_call(
        kernel,
        name="collect",
        in_specs=[hbm] * 4,
        out_specs=[hbm] * 4,
        out_shape=[
            shape((2, tile_rows, tile_cols), F32),
            shape((2, w, tile_cols), F32),
            shape((2, w, tile_cols), F32),
            shape((2 * w, w), F32),
        ],
        scratch_shapes=quarter_sems(STRIP) + quarter_sems(EDGE) + quarter_sems(EDGE) + [dma] * 11
        + [pltpu.VMEM((2, w, w), F32), pltpu.VMEM((chips, piece, w), F32), pltpu.VMEM((piece, w), F32)],
        compiler_params=pltpu.CompilerParams(collective_id=1, has_side_effects=True),
    )


def make_finish(window, tile_rows, tile_cols):
    w = window

    def kernel(own, strip, low, diag, total, grad, probe):
        r, c, m = place()
        below, inner = r > 0, c > 0
        first = pl.program_id(0) == 0
        when(inner, lambda: grad.__setitem__(..., own[...] + strip[...]))
        when(jnp.logical_not(inner), lambda: grad.__setitem__(..., own[...]))
        when(first & below, lambda: grad.__setitem__(..., grad[...] + low[...]))
        when(first & below & inner, lambda: grad.__setitem__(..., grad[...] + diag[...]))
        when(first, lambda: probe.__setitem__(..., total[...]))

    block = pl.BlockSpec((2, w, tile_cols), lambda i: (0, i, 0))
    once = pl.BlockSpec((2, w, tile_cols), lambda i: (0, 0, 0))
    return pl.pallas_call(
        kernel,
        name="finish",
        grid=(tile_rows // w,),
        in_specs=[block, block, once, once, once],
        out_specs=[block, once],
        out_shape=[
            jax.ShapeDtypeStruct((2, tile_rows, tile_cols), F32),
            jax.ShapeDtypeStruct((2, w, w), F32),
        ],
    )


def per_device(object_slab, probe_modes, amplitudes, scan_counts, scan_positions):
    window = probe_modes.shape[-1]
    tile_rows, tile_cols = object_slab.shape[1:]
    slots = amplitudes.shape[0]
    modes, cols_n, rows_n = (lax.axis_size(a) for a in ("mode", "col", "row"))
    sizes = (window, modes, tile_rows, tile_cols, rows_n, cols_n)
    right, low, diag, probe = make_spread(*sizes)(object_slab, probe_modes)
    consts = [jnp.asarray(t) for t in tables(window)]
    compute = make_compute(window, modes, slots, tile_rows, tile_cols, cols_n)
    g_own, g_right, g_low, g_diag, pg, shift = compute(
        scan_positions, scan_counts, object_slab, right, low, diag, probe, amplitudes, *consts
    )
    from_left, from_up, from_diag, total = make_collect(*sizes)(
        g_right, g_low, g_diag, pg.reshape(2 * window, window)
    )
    grad, probe_grad = make_finish(window, tile_rows, tile_cols)(
        g_own, from_left, from_up, from_diag, total.reshape(2, window, window)
    )
    return (grad, probe_grad.reshape(2, 1, window, window), shift)


def solution(mesh):
    in_specs = (
        P(None, "row", "col"),
        P(None, "mode", None, None),
        P(("row", "col"), None, None),
        P(),
        P(None, ("row", "col")),
    )
    out_specs = (P(None, "row", "col"), P(None, "mode", None, None), P(None, ("row", "col")))
    return jax.shard_map(
        per_device, mesh=mesh, in_specs=in_specs, out_specs=out_specs, check_vma=False
    )
```

```python
import math
import functools
import numpy as np
import jax
import jax.numpy as jnp
from jax import lax
from jax.experimental import pallas as pl
from jax.experimental.pallas import tpu as pltpu
from jax.sharding import PartitionSpec as P

BF = jnp.bfloat16
F32 = jnp.float32
BATCH = 4
CH = 32


def hi_lo(x):
    hi = x.astype(BF)
    lo = (x - hi.astype(F32)).astype(BF)
    return hi, lo


def halves(table):
    table = table.astype(np.float32)
    hi = table.astype(BF)
    return hi, (table - hi.astype(np.float32)).astype(BF)


def angles(window, radix, q):
    part = window // radix
    n, j = np.arange(part)[:, None], np.arange(part)[None, :]
    angle = 2.0 * math.pi * ((n * (radix * j + q)) % window) / window
    return np.cos(angle) / math.sqrt(window), np.sin(angle) / math.sqrt(window)


def tables(window):
    right_f, right_i, left_f, left_i = [], [], [], []
    for q in range(2):
        c, s = angles(window, 2, q)
        for table, into in ((np.block([[c, -s], [s, c]]), right_f), (np.block([[c.T, s.T], [-s.T, c.T]]), right_i)):
            hi, lo = halves(table)
            into.append(np.concatenate([hi, lo, hi], axis=0))
    for q in range(4):
        c, s = angles(window, 4, q)
        for table, into in ((np.block([[c.T, s.T], [-s.T, c.T]]), left_f), (np.block([[c, -s], [s, c]]), left_i)):
            hi, lo = halves(table)
            top = np.concatenate([hi, hi], axis=1)
            into.append(np.concatenate([top, np.concatenate([lo, np.zeros_like(lo)], axis=1)], axis=0))
    order = np.concatenate([np.arange(0, window, 2), np.arange(1, window, 2)])
    shuffle = np.zeros((window, window), np.float32)
    shuffle[order, np.arange(window)] = 1.0
    return np.stack(right_f), np.stack(right_i), np.stack(left_f), np.stack(left_i), shuffle.astype(BF)


def cat(parts, axis):
    return jnp.concatenate(parts, axis=axis)


def mm(a, b):
    return jnp.dot(a, b, preferred_element_type=F32)


def make_compute(window, modes, slots, tile_rows, tile_cols, cols_n):
    w, half, quart = window, window // 2, window // 4
    ch = CH
    ext_rows, ext_cols = tile_rows + w, tile_cols + w

    def kernel(positions, counts, own, right, low, diag, probe, amps, rf, ri, lf, li, shuffle,
               g_own, g_right, g_low, g_diag, pg, along,
               ext, grad, amp_buf, win, fac, lhs, rhs, mid, far, near, amp_sem, sem):
        row_id, col_id, mine = place()
        count = counts[row_id * cols_n + col_id]
        def quarters(whole, parts):
            pairs = []
            for k in range(4):
                for t in range(2):
                    down = slice(tile_rows, ext_rows) if k >= 2 else slice(0, tile_rows)
                    pairs.append((whole.at[2 * (k % 2) + t, :, down, :], parts[k].at[:, :, 128 * t:128 * t + 128]))
            return pairs

        loads = [
            pltpu.make_async_copy(part, inside, sem.at[k])
            for k, (inside, part) in enumerate(quarters(ext, (own, right, low, diag)))
        ]
        for copy in loads:
            copy.start()

        def amp_copies(slot, place):
            return [
                pltpu.make_async_copy(
                    amps.at[slot, :, 128 * t:128 * t + 128], amp_buf.at[place, t], amp_sem.at[place, t]
                )
                for t in range(2)
            ]

        for copy in amp_copies(0, 0):
            copy.start()

        def clear(i, carry):
            at = pl.multiple_of(i * ch, ch)
            for c in range(2):
                for t in range(4):
                    grad[t, c, pl.ds(at, ch), :] = jnp.zeros((ch, 128), F32)
            return carry

        lax.fori_loop(0, ext_rows // ch, clear, 0)
        pg[...] = jnp.zeros(pg.shape, F32)

        def no_shift(i, carry):
            along[0, i] = 0.0
            along[1, i] = 0.0
            return carry

        lax.fori_loop(0, slots, no_shift, 0)
        for copy in loads:
            copy.wait()

        def put_lhs(parity, at, x):
            hi, lo = hi_lo(x)
            lhs[parity, at:at + ch, :w] = hi
            lhs[parity, at:at + ch, w:] = lo

        def put_rhs(m, q, at, x):
            hi, lo = hi_lo(x)
            rhs[m, q, at:at + ch, :] = hi
            rhs[m, q, half + at:half + at + ch, :] = lo

        def right_apply(m, table, into):
            rows = slice(m * w, (m + BATCH) * w)
            for parity in range(2):
                hi, lo = lhs[parity, rows, :w], lhs[parity, rows, w:]
                into[parity, rows, :] = mm(cat([hi, hi, lo], 1), table[parity])

        def left_apply(m, q, table):
            both = mm(table[q], rhs[m, q])
            return both[:half] + both[half:]

        def forward_rows(m):
            for r in range(0, quart, ch):
                y = [[], [], [], []]
                for parity in range(2):
                    x = [mid[parity, m * w + p * quart + r:m * w + p * quart + r + ch, :] for p in range(4)]
                    a, b, c, d = x[0] + x[2], x[1] + x[3], x[0] - x[2], x[1] - x[3]
                    y[0].append(a + b)
                    y[2].append(a - b)
                    turned = cat([d[:, half:], -d[:, :half]], 1)
                    y[1].append(c + turned)
                    y[3].append(c - turned)
                for q in range(4):
                    e, o = y[q]
                    put_rhs(m, q, r, cat([e[:, :half], o[:, :half]], 1))
                    put_rhs(m, q, quart + r, cat([e[:, half:], o[:, half:]], 1))
            for q in range(4):
                far[m, q] = left_apply(m, q, lf)

        def inverse_rows(m):
            for q in range(4):
                for r in range(0, quart, ch):
                    f = fac[q, r:r + ch, :]
                    for at in (r, quart + r):
                        put_rhs(m, q, at, f * far[m, q, at:at + ch, :])
            for q in range(4):
                far[m, q] = left_apply(m, q, li)
            for r in range(0, quart, ch):
                re = [far[m, q, r:r + ch, :] for q in range(4)]
                im = [far[m, q, quart + r:quart + r + ch, :] for q in range(4)]
                are, aim, bre, bim = re[0] + re[2], im[0] + im[2], re[1] + re[3], im[1] + im[3]
                cre, cim, dre, dim = re[0] - re[2], im[0] - im[2], re[1] - re[3], im[1] - im[3]
                outs = (
                    (are + bre, aim + bim), (cre - dim, cim + dre),
                    (are - bre, aim - bim), (cre + dim, cim - dre),
                )
                for p, (xre, xim) in enumerate(outs):
                    for parity in range(2):
                        cols = slice(parity * half, parity * half + half)
                        put_lhs(parity, m * w + p * quart + r, cat([xre[:, cols], xim[:, cols]], 1))

        def do_slot(slot, carry):
            row = positions[0, slot] - row_id * tile_rows
            col = positions[1, slot] - col_id * tile_cols
            tile_at = col // 128
            off = lax.rem(col, 128)
            back = lax.rem(w + 128 - off, w + 128)
            place_at = lax.rem(slot, 2)
            for copy in amp_copies(slot, place_at):
                copy.wait()

            @pl.when(slot + 1 < count)
            def _():
                for copy in amp_copies(slot + 1, 1 - place_at):
                    copy.start()

            for c in range(2):
                for r in range(0, w, ch):
                    wide = cat([ext[tile_at + t, c, pl.ds(row + r, ch), :] for t in range(3)], 1)
                    win[c, r:r + ch, :] = pltpu.roll(wide, back, 1)[:, :w]

            for q in range(4):
                a = cat([amp_buf[place_at, t, pl.ds(q, quart, stride=4), :] for t in range(2)], 1)
                a0, a1 = hi_lo(a)
                a2 = (a - a0.astype(F32) - a1.astype(F32)).astype(BF)
                stack = mm(cat([a0, a1, a2], 0), shuffle[...])
                fac[q] = stack[:quart] + stack[quart:2 * quart] + stack[2 * quart:]

            for m in range(modes):
                for r in range(0, w, ch):
                    vre, vim = win[0, r:r + ch, :], win[1, r:r + ch, :]
                    pre, pim = probe[0, m, r:r + ch, :], probe[1, m, r:r + ch, :]
                    are = pre * vre - pim * vim
                    aim = pre * vim + pim * vre
                    for parity in range(2):
                        if parity == 0:
                            x = cat([are[:, :half] + are[:, half:], aim[:, :half] + aim[:, half:]], 1)
                        else:
                            x = cat([are[:, :half] - are[:, half:], aim[:, :half] - aim[:, half:]], 1)
                        put_lhs(parity, m * w + r, x)
                if (m + 1) % BATCH == 0:
                    right_apply(m + 1 - BATCH, rf, mid)
                    for n in range(m + 1 - BATCH, m + 1):
                        forward_rows(n)

            for q in range(4):
                for r in range(0, quart, ch):
                    total = None
                    for m in range(modes):
                        re = far[m, q, r:r + ch, :]
                        im = far[m, q, quart + r:quart + r + ch, :]
                        term = re * re + im * im
                        total = term if total is None else total + term
                    fac[q, r:r + ch, :] = 0.25 * (1.0 - fac[q, r:r + ch, :] * lax.rsqrt(total + 0.5))

            for m in range(modes):
                inverse_rows(m)
                if (m + 1) % BATCH == 0:
                    right_apply(m + 1 - BATCH, ri, near)

            rows_sum = jnp.zeros((8, w), F32)
            cols_sum = jnp.zeros((8, w), F32)
            lanes = lax.broadcasted_iota(jnp.int32, (ch, w), 1)
            inner = (lanes >= 1) & (lanes <= w - 2)

            def near_of(m, r):
                at = m * w + r
                if not isinstance(m, int):
                    at = pl.multiple_of(at, ch)
                e, o = near[0, pl.ds(at, ch), :], near[1, pl.ds(at, ch), :]
                s, d = e + o, e - o
                return cat([s[:, :half], d[:, :half]], 1), cat([s[:, half:], d[:, half:]], 1)

            for r in range(0, w, ch):
                gre = gim = None
                for m in range(modes):
                    nre, nim = near_of(m, r)
                    pre, pim = probe[0, m, r:r + ch, :], probe[1, m, r:r + ch, :]
                    tre = pre * nre + pim * nim
                    tim = pre * nim - pim * nre
                    gre = tre if gre is None else gre + tre
                    gim = tim if gim is None else gim + tim
                for c, g in ((0, gre), (1, gim)):
                    spread = pltpu.roll(cat([g, jnp.zeros((ch, 128), F32)], 1), off, 1)
                    for t in range(3):
                        grad[tile_at + t, c, pl.ds(row + r, ch), :] += spread[:, 128 * t:128 * t + 128]
                vre, vim = win[0, r:r + ch, :], win[1, r:r + ch, :]
                nre, nim = near_of(mine, r)
                pg[0, r:r + ch, :] += vre * nre + vim * nim
                pg[1, r:r + ch, :] += vre * nim - vim * nre
                dre = pltpu.roll(vre, w - 1, 1) - pltpu.roll(vre, 1, 1)
                dim = pltpu.roll(vim, w - 1, 1) - pltpu.roll(vim, 1, 1)
                t = jnp.where(inner, gre * dre + gim * dim, 0.0)
                cols_sum = cols_sum + jnp.sum(t.reshape(ch // 8, 8, w), axis=0)
                lo_r, hi_r = max(r, 1), min(r + ch, w - 1)
                up = [ext_rows_slice(win, c, r + 1, ch, w) for c in range(2)]
                dn = [ext_rows_slice(win, c, r - 1, ch, w) for c in range(2)]
                t = gre * (up[0] - dn[0]) + gim * (up[1] - dn[1])
                if lo_r != r or hi_r != r + ch:
                    idx = lax.broadcasted_iota(jnp.int32, (ch, w), 0) + r
                    t = jnp.where((idx >= lo_r) & (idx < hi_r), t, 0.0)
                rows_sum = rows_sum + jnp.sum(t.reshape(ch // 8, 8, w), axis=0)
            along[0, slot] = jnp.sum(rows_sum) * (0.5 / w)
            along[1, slot] = jnp.sum(cols_sum) * (0.5 / w)
            return carry

        def ext_rows_slice(ref, c, start, size, width):
            if start < 0:
                return cat([ref[c, 0:1, :], ref[c, 0:size - 1, :]], 0)
            if start + size > w:
                return cat([ref[c, start:w, :], ref[c, w - 1:w, :]], 0)
            return ref[c, start:start + size, :]

        lax.fori_loop(0, count, do_slot, 0)
        stores = [
            pltpu.make_async_copy(inside, part, sem.at[k])
            for k, (inside, part) in enumerate(quarters(grad, (g_own, g_right, g_low, g_diag)))
        ]
        for copy in stores:
            copy.start()
        for copy in stores:
            copy.wait()

    hbm = pl.BlockSpec(memory_space=pl.ANY)
    vmem = pl.BlockSpec(memory_space=pltpu.VMEM)
    smem = pl.BlockSpec(memory_space=pltpu.SMEM)
    shape = jax.ShapeDtypeStruct
    return pl.pallas_call(
        kernel,
        name="slots",
        in_specs=[smem, smem, hbm, hbm, hbm, hbm, vmem, hbm, vmem, vmem, vmem, vmem, vmem],
        out_specs=[hbm, hbm, hbm, hbm, vmem, smem],
        out_shape=[
            shape((2, tile_rows, tile_cols), F32),
            shape((2, tile_rows, w), F32),
            shape((2, w, tile_cols), F32),
            shape((2, w, w), F32),
            shape((2, w, w), F32),
            shape((2, slots), F32),
        ],
        scratch_shapes=[
            pltpu.VMEM((ext_cols // 128, 2, ext_rows, 128), F32),
            pltpu.VMEM((ext_cols // 128, 2, ext_rows, 128), F32),
            pltpu.VMEM((2, 2, w, 128), F32),
            pltpu.VMEM((2, w, w), F32),
            pltpu.VMEM((4, quart, w), F32),
            pltpu.VMEM((2, modes * w, 2 * w), BF),
            pltpu.VMEM((modes, 4, w, w), BF),
            pltpu.VMEM((2, modes * w, w), F32),
            pltpu.VMEM((modes, 4, half, w), F32),
            pltpu.VMEM((2, modes * w, w), F32),
            pltpu.SemaphoreType.DMA((2, 2)),
            pltpu.SemaphoreType.DMA((8,)),
        ],
        compiler_params=pltpu.CompilerParams(vmem_limit_bytes=60 << 20),
        cost_estimate=pl.CostEstimate(flops=10**11, bytes_accessed=10**7, transcendentals=0),
    )


MESH = pl.DeviceIdType.MESH


def place():
    return lax.axis_index("row"), lax.axis_index("col"), lax.axis_index("mode")


def device(r, c, m):
    return {"row": r, "col": c, "mode": m}


def remote(src, dst, send, recv, to):
    return pltpu.make_async_remote_copy(
        src_ref=src, dst_ref=dst, send_sem=send, recv_sem=recv, device_id=to, device_id_type=MESH
    )


def greet(to):
    pl.semaphore_signal(pltpu.get_barrier_semaphore(), inc=1, device_id=to, device_id_type=MESH)


class Quarters:
    def __init__(self, src, dst, modes, rows, r, c, chunks, sems):
        me_r, me_c, m = place()
        self.m, self.modes, self.chunks = m, modes, chunks
        self.rows = rows // modes // chunks
        self.src, self.dst = src, dst
        self.ys, self.yr, self.zs, self.zr, self.ts, self.tr = sems
        self.peer = device(r, c, m)
        self.next = device(me_r, me_c, lax.rem(m + 1, modes))
        self.prev = device(me_r, me_c, lax.rem(m + modes - 1, modes))

    def part(self, ref, owner, i):
        at = pl.multiple_of((owner * self.chunks + i) * self.rows, self.rows)
        return ref.at[:, pl.ds(at, self.rows), :]

    def first(self, i):
        mine = self.part(self.src, self.m, i)
        return remote(mine, self.part(self.dst, self.m, i), self.ys.at[i], self.yr.at[i], self.peer)

    def ring(self, i, way):
        mine = self.part(self.dst, self.m, i)
        return remote(mine, mine, self.zs.at[way, i], self.zr.at[way, i], self.next if way == 0 else self.prev)

    def way(self, i):
        return 0 if i < self.chunks // 2 else 1

    def relay(self, i):
        back = self.modes - 1 if self.way(i) == 0 else 1
        block = self.part(self.dst, lax.rem(self.m + back, self.modes), i)
        return remote(block, block, self.ts.at[i], self.tr.at[i], self.next if self.way(i) == 0 else self.prev)

    def start(self):
        for i in range(self.chunks):
            self.first(i).start()

    def sent(self):
        for i in range(self.chunks):
            self.first(i).wait_send()

    def take(self, some=None):
        for i in range(self.chunks) if some is None else some:
            self.first(i).wait_recv()
            self.ring(i, 0).start()
            self.ring(i, 1).start()

    def turn(self):
        for i in range(self.chunks):
            self.ring(i, self.way(i)).wait_recv()
            self.relay(i).start()

    def finish(self):
        for i in range(self.chunks):
            self.ring(i, 1 - self.way(i)).wait_recv()
            self.relay(i).wait_recv()
        for i in range(self.chunks):
            self.ring(i, 0).wait_send()
            self.ring(i, 1).wait_send()
            self.relay(i).wait_send()


STRIP, EDGE = 4, 2


def quarter_sems(chunks):
    one = pltpu.SemaphoreType.DMA((chunks,))
    two = pltpu.SemaphoreType.DMA((2, chunks))
    return [one, one, two, two, one, one]


def when(cond, *steps):
    @pl.when(cond)
    def _():
        for step in steps:
            step()


def make_spread(window, modes, tile_rows, tile_cols, rows_n, cols_n):
    w = window

    def kernel(tile, probe, right, low, diag, gathered, *sems):
        strip_sems, low_sems, diag_sems = sems[:6], sems[6:12], sems[12:18]
        one_s, one_r, p_s, p_r, x_s, x_r, own_sem = sems[18:]
        r, c, m = place()
        core = lax.rem(c, 2)
        other = c + 1 - 2 * core
        odd, even = core == 1, core == 0
        away = jnp.where(odd, jnp.minimum(c + 1, cols_n - 1), jnp.maximum(c - 1, 0))
        has_away = jnp.where(odd, c < cols_n - 1, c > 0)
        has_diag = has_away & jnp.where(odd, r == 0, r == 1)
        flip = rows_n - 1 - r

        for k in range(1, modes):
            greet(device(r, c, lax.rem(m + k, modes)))
        greet(device(r, other, m))
        greet(device(flip, c, m))
        when(has_away, lambda: greet(device(r, away, m)))
        when(has_diag, lambda: greet(device(flip, away, m)))
        pl.semaphore_wait(
            pltpu.get_barrier_semaphore(),
            modes + 1 + has_away.astype(jnp.int32) + has_diag.astype(jnp.int32),
        )

        strip = Quarters(tile, right, modes, tile_rows, r, away, STRIP, strip_sems)
        down = Quarters(tile, low, modes, w, flip, c, EDGE, low_sems)
        corner = Quarters(tile, diag, modes, w, flip, away, EDGE, diag_sems)
        whole = remote(tile, right, one_s.at[0], one_r.at[0], device(r, other, m))
        corner_on = remote(low, diag, one_s.at[1], one_r.at[1], device(r, other, m))

        def probe_copy(k):
            to = device(r, c, lax.rem(m + k, modes))
            return remote(probe, gathered.at[:, pl.ds(m, 1)], p_s.at[k], p_r.at[k], to)

        def probe_pass(k):
            one = gathered.at[:, pl.ds(lax.rem(m + modes - k, modes), 1)]
            return remote(one, one, x_s.at[k], x_r.at[k], device(r, other, m))

        def probe_start():
            for k in far:
                probe_copy(k).start()

        def probe_turn():
            for k in far:
                probe_copy(k).wait_recv()
                probe_pass(k).start()

        def probe_finish():
            for k in far:
                probe_pass(k).wait_send()
                probe_copy(k).wait_send()

        def probe_take():
            for k in far:
                probe_pass(k).wait_recv()

        far = (1, modes - 1, 2)
        when(even & has_away, strip.start)
        when(r == 1, down.start)
        when(even & has_diag, corner.start)
        when(even, probe_start)
        when(odd, whole.start)
        keep = pltpu.make_async_copy(probe, gathered.at[:, pl.ds(m, 1)], own_sem)
        keep.start()

        when(odd & has_away, lambda: strip.take([0]))
        when(r == 0, down.take)
        when(odd & has_diag, corner.take)
        when(odd & has_away, lambda: strip.take([1, 2, 3]))
        when(r == 0, down.turn)
        when(odd & has_diag, corner.turn)
        when(odd & has_away, strip.turn)
        when(r == 0, down.finish)
        when(odd & (r == 0), corner_on.start)
        when(even, probe_turn)
        when(odd & has_diag, corner.finish)
        when(odd & has_away, strip.finish)
        when(even, whole.wait_recv)
        when(even & (r == 0), corner_on.wait_recv)
        when(odd, probe_take)
        when(even, probe_finish)
        keep.wait()
        when(odd, whole.wait_send)
        when(odd & (r == 0), corner_on.wait_send)
        when(even & has_away, strip.sent)
        when(r == 1, down.sent)
        when(even & has_diag, corner.sent)

    hbm = pl.BlockSpec(memory_space=pl.ANY)
    shape = jax.ShapeDtypeStruct
    dma = pltpu.SemaphoreType.DMA
    return pl.pallas_call(
        kernel,
        name="spread",
        in_specs=[hbm, hbm],
        out_specs=[hbm] * 4,
        out_shape=[
            shape((2, tile_rows, tile_cols), F32),
            shape((2, w, tile_cols), F32),
            shape((2, w, tile_cols), F32),
            shape((2, modes, w, w), F32),
        ],
        scratch_shapes=quarter_sems(STRIP) + quarter_sems(EDGE) + quarter_sems(EDGE)
        + [dma((2,))] * 2 + [dma((modes,))] * 4 + [dma],
        compiler_params=pltpu.CompilerParams(collective_id=0, has_side_effects=True),
    )


def make_collect(window, modes, tile_rows, tile_cols, rows_n, cols_n):
    w = window
    chips = rows_n * cols_n // 2
    piece = 2 * w // chips

    def kernel(g_right, g_low, g_diag, pg, right, low, diag, total, *sems):
        strip_sems, low_sems, diag_sems = sems[:6], sems[6:12], sems[12:18]
        one_s, one_r, x_s, x_r, y_s, y_r, a_s, a_r, b_s, b_r, in_sem, pair, got, mine = sems[18:]
        r, c, m = place()
        core = lax.rem(c, 2)
        chip = r * (cols_n // 2) + c // 2
        other = c + 1 - 2 * core
        odd, even = core == 1, core == 0
        away = jnp.where(odd, jnp.minimum(c + 1, cols_n - 1), jnp.maximum(c - 1, 0))
        has_away = jnp.where(odd, c < cols_n - 1, c > 0)
        flip = rows_n - 1 - r
        over = jnp.where(r == 0, jnp.minimum(c + 1, cols_n - 1), jnp.maximum(c - 1, 0))
        has_over = jnp.where(r == 0, c < cols_n - 1, c > 0)

        def partner(k):
            p = lax.rem(chip + k, chips)
            return device(p // (cols_n // 2), 2 * lax.rem(p, cols_n // 2) + core, m)

        def hello(k, carry):
            greet(partner(k))
            return carry

        greet(device(r, other, m))
        for k in (1, modes - 1):
            greet(device(r, c, lax.rem(m + k, modes)))
        when(has_away, lambda: greet(device(r, away, m)))
        when(has_over, lambda: greet(device(flip, over, m)))
        when(even, lambda: greet(device(flip, c, m)))
        when(odd, lambda: lax.fori_loop(1, chips, hello, 0))
        pl.semaphore_wait(
            pltpu.get_barrier_semaphore(),
            3 + jnp.where(odd, chips - 1, 1) + has_away.astype(jnp.int32) + has_over.astype(jnp.int32),
        )

        strip = Quarters(g_right, right, modes, tile_rows, r, away, STRIP, strip_sems)
        down = Quarters(g_low, low, modes, w, flip, c, EDGE, low_sems)
        corner = Quarters(g_diag, diag, modes, w, flip, over, EDGE, diag_sems)
        whole = remote(g_right, right, one_s, one_r, device(r, other, m))
        swap = remote(pg, pair.at[0], x_s, x_r, device(r, other, m))
        own = pltpu.make_async_copy(pg, pair.at[1], in_sem)
        at_chip = pl.ds(pl.multiple_of(chip * piece, piece), piece)
        rest = got.at[pl.ds(1, chips - 1)]
        many = total.at[pl.ds(0, (chips - 1) * piece), :]
        keep = pltpu.make_async_copy(mine, total.at[at_chip, :], in_sem)
        give = remote(total, total, y_s, y_r, device(r, other, m))

        def scatter_go(k, carry):
            p = lax.rem(chip + k, chips)
            rows = pl.ds(pl.multiple_of(p * piece, piece), piece)
            remote(pair.at[1, rows, :], got.at[k], a_s, a_r, partner(k)).start()
            return carry

        def share_go(k, carry):
            remote(mine, total.at[at_chip, :], b_s, b_r, partner(k)).start()
            return carry

        def add(k, acc):
            return acc + got[k]

        def sum_pair():
            own.wait()
            swap.wait_recv()
            pair[1] = pair[0] + pair[1]
            lax.fori_loop(1, chips, scatter_go, 0)

        def sum_plane():
            pltpu.make_async_copy(rest, rest, a_r).wait()
            mine[...] = lax.fori_loop(1, chips, add, pair[1, at_chip, :]) * (1.0 / 16.0)
            keep.start()
            lax.fori_loop(1, chips, share_go, 0)

        def sum_give():
            keep.wait()
            pltpu.make_async_copy(many, many, b_r).wait()
            give.start()

        def sum_end():
            pltpu.make_async_copy(rest, rest, a_s).wait()
            pltpu.make_async_copy(many, many, b_s).wait()
            give.wait_send()

        when(even, swap.start)
        when(odd, own.start)
        when(odd & has_away, strip.start)
        when(r == 0, down.start)
        when((r == 0) & has_over, corner.start)
        when(even, whole.start)
        when(odd, sum_pair)
        when(even & has_away, strip.take)
        when(r == 1, down.take)
        when((r == 1) & has_over, corner.take)
        when(odd, sum_plane)
        when(even & has_away, strip.turn)
        when(r == 1, down.turn)
        when((r == 1) & has_over, corner.turn)
        when(odd, sum_give)
        when(even & has_away, strip.finish)
        when(r == 1, down.finish)
        when((r == 1) & has_over, corner.finish)
        when(odd, whole.wait_recv)
        when(even, give.wait_recv)
        when(even, swap.wait_send)
        when(odd, sum_end)
        when(odd & has_away, strip.sent)
        when(r == 0, down.sent)
        when((r == 0) & has_over, corner.sent)
        when(even, whole.wait_send)

    hbm = pl.BlockSpec(memory_space=pl.ANY)
    shape = jax.ShapeDtypeStruct
    dma = pltpu.SemaphoreType.DMA
    return pl.pallas_call(
        kernel,
        name="collect",
        in_specs=[hbm] * 4,
        out_specs=[hbm] * 4,
        out_shape=[
            shape((2, tile_rows, tile_cols), F32),
            shape((2, w, tile_cols), F32),
            shape((2, w, tile_cols), F32),
            shape((2 * w, w), F32),
        ],
        scratch_shapes=quarter_sems(STRIP) + quarter_sems(EDGE) + quarter_sems(EDGE) + [dma] * 11
        + [pltpu.VMEM((2, 2 * w, w), F32), pltpu.VMEM((chips, piece, w), F32), pltpu.VMEM((piece, w), F32)],
        compiler_params=pltpu.CompilerParams(collective_id=1, has_side_effects=True),
    )


def make_finish(window, tile_rows, tile_cols):
    w = window

    def kernel(own, strip, low, diag, total, grad, probe):
        r, c, m = place()
        below, inner = r > 0, c > 0
        first = pl.program_id(0) == 0
        when(inner, lambda: grad.__setitem__(..., own[...] + strip[...]))
        when(jnp.logical_not(inner), lambda: grad.__setitem__(..., own[...]))
        when(first & below, lambda: grad.__setitem__(..., grad[...] + low[...]))
        when(first & below & inner, lambda: grad.__setitem__(..., grad[...] + diag[...]))
        when(first, lambda: probe.__setitem__(..., total[...]))

    block = pl.BlockSpec((2, w, tile_cols), lambda i: (0, i, 0))
    once = pl.BlockSpec((2, w, tile_cols), lambda i: (0, 0, 0))
    return pl.pallas_call(
        kernel,
        name="finish",
        grid=(tile_rows // w,),
        in_specs=[block, block, once, once, once],
        out_specs=[block, once],
        out_shape=[
            jax.ShapeDtypeStruct((2, tile_rows, tile_cols), F32),
            jax.ShapeDtypeStruct((2, w, w), F32),
        ],
    )


def per_device(object_slab, probe_modes, amplitudes, scan_counts, scan_positions):
    window = probe_modes.shape[-1]
    tile_rows, tile_cols = object_slab.shape[1:]
    slots = amplitudes.shape[0]
    modes, cols_n, rows_n = (lax.axis_size(a) for a in ("mode", "col", "row"))
    sizes = (window, modes, tile_rows, tile_cols, rows_n, cols_n)
    right, low, diag, probe = make_spread(*sizes)(object_slab, probe_modes)
    consts = [jnp.asarray(t) for t in tables(window)]
    compute = make_compute(window, modes, slots, tile_rows, tile_cols, cols_n)
    g_own, g_right, g_low, g_diag, pg, shift = compute(
        scan_positions, scan_counts, object_slab, right, low, diag, probe, amplitudes, *consts
    )
    from_left, from_up, from_diag, total = make_collect(*sizes)(
        g_right, g_low, g_diag, pg.reshape(2 * window, window)
    )
    grad, probe_grad = make_finish(window, tile_rows, tile_cols)(
        g_own, from_left, from_up, from_diag, total.reshape(2, window, window)
    )
    return (grad, probe_grad.reshape(2, 1, window, window), shift)


def solution(mesh):
    in_specs = (
        P(None, "row", "col"),
        P(None, "mode", None, None),
        P(("row", "col"), None, None),
        P(),
        P(None, ("row", "col")),
    )
    out_specs = (P(None, "row", "col"), P(None, "mode", None, None), P(None, ("row", "col")))
    return jax.shard_map(
        per_device, mesh=mesh, in_specs=in_specs, out_specs=out_specs, check_vma=False
    )
```

```python
import math
import functools
import numpy as np
import jax
import jax.numpy as jnp
from jax import lax
from jax.experimental import pallas as pl
from jax.experimental.pallas import tpu as pltpu
from jax.sharding import PartitionSpec as P

BF = jnp.bfloat16
F32 = jnp.float32
BATCH = 4
CH = 32


def hi_lo(x):
    hi = x.astype(BF)
    lo = (x - hi.astype(F32)).astype(BF)
    return hi, lo


def halves(table):
    table = table.astype(np.float32)
    hi = table.astype(BF)
    return hi, (table - hi.astype(np.float32)).astype(BF)


def angles(window, radix, q):
    part = window // radix
    n, j = np.arange(part)[:, None], np.arange(part)[None, :]
    angle = 2.0 * math.pi * ((n * (radix * j + q)) % window) / window
    return np.cos(angle) / math.sqrt(window), np.sin(angle) / math.sqrt(window)


def tables(window):
    right_f, right_i, left_f, left_i = [], [], [], []
    for q in range(2):
        c, s = angles(window, 2, q)
        for table, into in ((np.block([[c, -s], [s, c]]), right_f), (np.block([[c.T, s.T], [-s.T, c.T]]), right_i)):
            hi, lo = halves(table)
            into.append(np.concatenate([hi, lo, hi], axis=0))
    for q in range(4):
        c, s = angles(window, 4, q)
        for table, into in ((np.block([[c.T, s.T], [-s.T, c.T]]), left_f), (np.block([[c, -s], [s, c]]), left_i)):
            hi, lo = halves(table)
            top = np.concatenate([hi, hi], axis=1)
            into.append(np.concatenate([top, np.concatenate([lo, np.zeros_like(lo)], axis=1)], axis=0))
    order = np.concatenate([np.arange(0, window, 2), np.arange(1, window, 2)])
    shuffle = np.zeros((window, window), np.float32)
    shuffle[order, np.arange(window)] = 1.0
    return np.stack(right_f), np.stack(right_i), np.stack(left_f), np.stack(left_i), shuffle.astype(BF)


def cat(parts, axis):
    return jnp.concatenate(parts, axis=axis)


def mm(a, b):
    return jnp.dot(a, b, preferred_element_type=F32)


def make_compute(window, modes, slots, tile_rows, tile_cols, cols_n):
    w, half, quart = window, window // 2, window // 4
    ch = CH
    ext_rows, ext_cols = tile_rows + w, tile_cols + w

    def kernel(positions, counts, own, right, low, diag, probe, amps, rf, ri, lf, li, shuffle,
               g_own, g_right, g_low, g_diag, pg, along,
               ext, grad, amp_buf, win, fac, lhs, rhs, mid, far, near, amp_sem, sem):
        row_id, col_id, mine = place()
        count = counts[row_id * cols_n + col_id]
        def quarters(whole, parts):
            pairs = []
            for k in range(4):
                for t in range(2):
                    down = slice(tile_rows, ext_rows) if k >= 2 else slice(0, tile_rows)
                    pairs.append((whole.at[2 * (k % 2) + t, :, down, :], parts[k].at[:, :, 128 * t:128 * t + 128]))
            return pairs

        loads = [
            pltpu.make_async_copy(part, inside, sem.at[k])
            for k, (inside, part) in enumerate(quarters(ext, (own, right, low, diag)))
        ]
        for copy in loads:
            copy.start()

        def amp_copies(slot, place):
            return [
                pltpu.make_async_copy(
                    amps.at[slot, :, 128 * t:128 * t + 128], amp_buf.at[place, t], amp_sem.at[place, t]
                )
                for t in range(2)
            ]

        for copy in amp_copies(0, 0):
            copy.start()

        def clear(i, carry):
            at = pl.multiple_of(i * ch, ch)
            for c in range(2):
                for t in range(4):
                    grad[t, c, pl.ds(at, ch), :] = jnp.zeros((ch, 128), F32)
            return carry

        lax.fori_loop(0, ext_rows // ch, clear, 0)
        pg[...] = jnp.zeros(pg.shape, F32)

        def no_shift(i, carry):
            along[0, i] = 0.0
            along[1, i] = 0.0
            return carry

        lax.fori_loop(0, slots, no_shift, 0)
        for copy in loads:
            copy.wait()

        def put_lhs(parity, at, x):
            hi, lo = hi_lo(x)
            lhs[parity, at:at + ch, :w] = hi
            lhs[parity, at:at + ch, w:] = lo

        def put_rhs(m, q, at, x):
            hi, lo = hi_lo(x)
            rhs[m, q, at:at + ch, :] = hi
            rhs[m, q, half + at:half + at + ch, :] = lo

        def right_apply(m, table, into):
            rows = slice(m * w, (m + BATCH) * w)
            for parity in range(2):
                hi, lo = lhs[parity, rows, :w], lhs[parity, rows, w:]
                into[parity, rows, :] = mm(cat([hi, hi, lo], 1), table[parity])

        def left_apply(m, q, table):
            both = mm(table[q], rhs[m, q])
            return both[:half] + both[half:]

        def forward_rows(m):
            for r in range(0, quart, ch):
                y = [[], [], [], []]
                for parity in range(2):
                    x = [mid[parity, m * w + p * quart + r:m * w + p * quart + r + ch, :] for p in range(4)]
                    a, b, c, d = x[0] + x[2], x[1] + x[3], x[0] - x[2], x[1] - x[3]
                    y[0].append(a + b)
                    y[2].append(a - b)
                    turned = cat([d[:, half:], -d[:, :half]], 1)
                    y[1].append(c + turned)
                    y[3].append(c - turned)
                for q in range(4):
                    e, o = y[q]
                    put_rhs(m, q, r, cat([e[:, :half], o[:, :half]], 1))
                    put_rhs(m, q, quart + r, cat([e[:, half:], o[:, half:]], 1))
            for q in range(4):
                far[m, q] = left_apply(m, q, lf)

        def inverse_rows(m):
            for q in range(4):
                for r in range(0, quart, ch):
                    f = fac[q, r:r + ch, :]
                    for at in (r, quart + r):
                        put_rhs(m, q, at, f * far[m, q, at:at + ch, :])
            for q in range(4):
                far[m, q] = left_apply(m, q, li)
            for r in range(0, quart, ch):
                re = [far[m, q, r:r + ch, :] for q in range(4)]
                im = [far[m, q, quart + r:quart + r + ch, :] for q in range(4)]
                are, aim, bre, bim = re[0] + re[2], im[0] + im[2], re[1] + re[3], im[1] + im[3]
                cre, cim, dre, dim = re[0] - re[2], im[0] - im[2], re[1] - re[3], im[1] - im[3]
                outs = (
                    (are + bre, aim + bim), (cre - dim, cim + dre),
                    (are - bre, aim - bim), (cre + dim, cim - dre),
                )
                for p, (xre, xim) in enumerate(outs):
                    for parity in range(2):
                        cols = slice(parity * half, parity * half + half)
                        put_lhs(parity, m * w + p * quart + r, cat([xre[:, cols], xim[:, cols]], 1))

        def do_slot(slot, carry):
            row = positions[0, slot] - row_id * tile_rows
            col = positions[1, slot] - col_id * tile_cols
            tile_at = col // 128
            off = lax.rem(col, 128)
            back = lax.rem(w + 128 - off, w + 128)
            place_at = lax.rem(slot, 2)
            for copy in amp_copies(slot, place_at):
                copy.wait()

            @pl.when(slot + 1 < count)
            def _():
                for copy in amp_copies(slot + 1, 1 - place_at):
                    copy.start()

            for c in range(2):
                for r in range(0, w, ch):
                    wide = cat([ext[tile_at + t, c, pl.ds(row + r, ch), :] for t in range(3)], 1)
                    win[c, r:r + ch, :] = pltpu.roll(wide, back, 1)[:, :w]

            for q in range(4):
                a = cat([amp_buf[place_at, t, pl.ds(q, quart, stride=4), :] for t in range(2)], 1)
                a0, a1 = hi_lo(a)
                a2 = (a - a0.astype(F32) - a1.astype(F32)).astype(BF)
                stack = mm(cat([a0, a1, a2], 0), shuffle[...])
                fac[q] = stack[:quart] + stack[quart:2 * quart] + stack[2 * quart:]

            for m in range(modes):
                for r in range(0, w, ch):
                    vre, vim = win[0, r:r + ch, :], win[1, r:r + ch, :]
                    pre, pim = probe[0, m, r:r + ch, :], probe[1, m, r:r + ch, :]
                    are = pre * vre - pim * vim
                    aim = pre * vim + pim * vre
                    for parity in range(2):
                        if parity == 0:
                            x = cat([are[:, :half] + are[:, half:], aim[:, :half] + aim[:, half:]], 1)
                        else:
                            x = cat([are[:, :half] - are[:, half:], aim[:, :half] - aim[:, half:]], 1)
                        put_lhs(parity, m * w + r, x)
                if (m + 1) % BATCH == 0:
                    right_apply(m + 1 - BATCH, rf, mid)
                    for n in range(m + 1 - BATCH, m + 1):
                        forward_rows(n)

            for q in range(4):
                for r in range(0, quart, ch):
                    total = None
                    for m in range(modes):
                        re = far[m, q, r:r + ch, :]
                        im = far[m, q, quart + r:quart + r + ch, :]
                        term = re * re + im * im
                        total = term if total is None else total + term
                    fac[q, r:r + ch, :] = 0.25 * (1.0 - fac[q, r:r + ch, :] * lax.rsqrt(total + 0.5))

            for m in range(modes):
                inverse_rows(m)
                if (m + 1) % BATCH == 0:
                    right_apply(m + 1 - BATCH, ri, near)

            rows_sum = jnp.zeros((8, w), F32)
            cols_sum = jnp.zeros((8, w), F32)
            lanes = lax.broadcasted_iota(jnp.int32, (ch, w), 1)
            inner = (lanes >= 1) & (lanes <= w - 2)

            def near_of(m, r):
                at = m * w + r
                if not isinstance(m, int):
                    at = pl.multiple_of(at, ch)
                e, o = near[0, pl.ds(at, ch), :], near[1, pl.ds(at, ch), :]
                s, d = e + o, e - o
                return cat([s[:, :half], d[:, :half]], 1), cat([s[:, half:], d[:, half:]], 1)

            for r in range(0, w, ch):
                gre = gim = None
                for m in range(modes):
                    nre, nim = near_of(m, r)
                    pre, pim = probe[0, m, r:r + ch, :], probe[1, m, r:r + ch, :]
                    tre = pre * nre + pim * nim
                    tim = pre * nim - pim * nre
                    gre = tre if gre is None else gre + tre
                    gim = tim if gim is None else gim + tim
                for c, g in ((0, gre), (1, gim)):
                    spread = pltpu.roll(cat([g, jnp.zeros((ch, 128), F32)], 1), off, 1)
                    for t in range(3):
                        grad[tile_at + t, c, pl.ds(row + r, ch), :] += spread[:, 128 * t:128 * t + 128]
                vre, vim = win[0, r:r + ch, :], win[1, r:r + ch, :]
                nre, nim = near_of(mine, r)
                pg[0, r:r + ch, :] += vre * nre + vim * nim
                pg[1, r:r + ch, :] += vre * nim - vim * nre
                dre = pltpu.roll(vre, w - 1, 1) - pltpu.roll(vre, 1, 1)
                dim = pltpu.roll(vim, w - 1, 1) - pltpu.roll(vim, 1, 1)
                t = jnp.where(inner, gre * dre + gim * dim, 0.0)
                cols_sum = cols_sum + jnp.sum(t.reshape(ch // 8, 8, w), axis=0)
                lo_r, hi_r = max(r, 1), min(r + ch, w - 1)
                up = [ext_rows_slice(win, c, r + 1, ch, w) for c in range(2)]
                dn = [ext_rows_slice(win, c, r - 1, ch, w) for c in range(2)]
                t = gre * (up[0] - dn[0]) + gim * (up[1] - dn[1])
                if lo_r != r or hi_r != r + ch:
                    idx = lax.broadcasted_iota(jnp.int32, (ch, w), 0) + r
                    t = jnp.where((idx >= lo_r) & (idx < hi_r), t, 0.0)
                rows_sum = rows_sum + jnp.sum(t.reshape(ch // 8, 8, w), axis=0)
            along[0, slot] = jnp.sum(rows_sum) * (0.5 / w)
            along[1, slot] = jnp.sum(cols_sum) * (0.5 / w)
            return carry

        def ext_rows_slice(ref, c, start, size, width):
            if start < 0:
                return cat([ref[c, 0:1, :], ref[c, 0:size - 1, :]], 0)
            if start + size > w:
                return cat([ref[c, start:w, :], ref[c, w - 1:w, :]], 0)
            return ref[c, start:start + size, :]

        lax.fori_loop(0, count, do_slot, 0)
        stores = [
            pltpu.make_async_copy(inside, part, sem.at[k])
            for k, (inside, part) in enumerate(quarters(grad, (g_own, g_right, g_low, g_diag)))
        ]
        for copy in stores:
            copy.start()
        for copy in stores:
            copy.wait()

    hbm = pl.BlockSpec(memory_space=pl.ANY)
    vmem = pl.BlockSpec(memory_space=pltpu.VMEM)
    smem = pl.BlockSpec(memory_space=pltpu.SMEM)
    shape = jax.ShapeDtypeStruct
    return pl.pallas_call(
        kernel,
        name="slots",
        in_specs=[smem, smem, hbm, hbm, hbm, hbm, vmem, hbm, vmem, vmem, vmem, vmem, vmem],
        out_specs=[hbm, hbm, hbm, hbm, vmem, smem],
        out_shape=[
            shape((2, tile_rows, tile_cols), F32),
            shape((2, tile_rows, w), F32),
            shape((2, w, tile_cols), F32),
            shape((2, w, w), F32),
            shape((2, w, w), F32),
            shape((2, slots), F32),
        ],
        scratch_shapes=[
            pltpu.VMEM((ext_cols // 128, 2, ext_rows, 128), F32),
            pltpu.VMEM((ext_cols // 128, 2, ext_rows, 128), F32),
            pltpu.VMEM((2, 2, w, 128), F32),
            pltpu.VMEM((2, w, w), F32),
            pltpu.VMEM((4, quart, w), F32),
            pltpu.VMEM((2, modes * w, 2 * w), BF),
            pltpu.VMEM((modes, 4, w, w), BF),
            pltpu.VMEM((2, modes * w, w), F32),
            pltpu.VMEM((modes, 4, half, w), F32),
            pltpu.VMEM((2, modes * w, w), F32),
            pltpu.SemaphoreType.DMA((2, 2)),
            pltpu.SemaphoreType.DMA((8,)),
        ],
        compiler_params=pltpu.CompilerParams(vmem_limit_bytes=60 << 20),
        cost_estimate=pl.CostEstimate(flops=10**11, bytes_accessed=10**7, transcendentals=0),
    )


MESH = pl.DeviceIdType.MESH


def place():
    return lax.axis_index("row"), lax.axis_index("col"), lax.axis_index("mode")


def device(r, c, m):
    return {"row": r, "col": c, "mode": m}


def remote(src, dst, send, recv, to):
    return pltpu.make_async_remote_copy(
        src_ref=src, dst_ref=dst, send_sem=send, recv_sem=recv, device_id=to, device_id_type=MESH
    )


def greet(to):
    pl.semaphore_signal(pltpu.get_barrier_semaphore(), inc=1, device_id=to, device_id_type=MESH)


class Quarters:
    def __init__(self, src, dst, modes, rows, r, c, chunks, sems, direct=False):
        me_r, me_c, m = place()
        self.m, self.modes, self.chunks, self.direct = m, modes, chunks, direct
        self.rows = rows // modes // chunks
        self.src, self.dst = src, dst
        self.ys, self.yr, self.zs, self.zr, self.ts, self.tr = sems
        self.peer = device(r, c, m)
        self.next = device(me_r, me_c, lax.rem(m + 1, modes))
        self.prev = device(me_r, me_c, lax.rem(m + modes - 1, modes))

    def part(self, ref, owner, i):
        at = pl.multiple_of((owner * self.chunks + i) * self.rows, self.rows)
        return ref.at[:, pl.ds(at, self.rows), :]

    def first(self, i):
        mine = self.part(self.src, self.m, i)
        return remote(mine, self.part(self.dst, self.m, i), self.ys.at[i], self.yr.at[i], self.peer)

    def ring(self, i, way):
        mine = self.part(self.dst, self.m, i)
        return remote(mine, mine, self.zs.at[way, i], self.zr.at[way, i], self.next if way == 0 else self.prev)

    def way(self, i):
        return 0 if i < self.chunks // 2 else 1

    def relay(self, i):
        back = self.modes - 1 if self.way(i) == 0 else 1
        block = self.part(self.dst, lax.rem(self.m + back, self.modes), i)
        return remote(block, block, self.ts.at[i], self.tr.at[i], self.next if self.way(i) == 0 else self.prev)

    def second(self, i):
        owner = lax.rem(self.m + self.modes // 2, self.modes)
        return remote(
            self.part(self.src, owner, i), self.part(self.dst, owner, i), self.ts.at[i], self.tr.at[i], self.peer
        )

    def start(self):
        for i in range(self.chunks):
            self.first(i).start()
        for i in range(self.chunks) if self.direct else ():
            self.second(i).start()

    def sent(self):
        for i in range(self.chunks):
            self.first(i).wait_send()
            if self.direct:
                self.second(i).wait_send()

    def take(self, some=None):
        for i in range(self.chunks) if some is None else some:
            self.first(i).wait_recv()
            self.ring(i, 0).start()
            self.ring(i, 1).start()

    def turn(self):
        for i in range(self.chunks):
            self.ring(i, self.way(i)).wait_recv()
            if not self.direct:
                self.relay(i).start()

    def finish(self):
        for i in range(self.chunks):
            self.ring(i, 1 - self.way(i)).wait_recv()
            if self.direct:
                self.second(i).wait_recv()
            else:
                self.relay(i).wait_recv()
        for i in range(self.chunks):
            self.ring(i, 0).wait_send()
            self.ring(i, 1).wait_send()
            if not self.direct:
                self.relay(i).wait_send()


STRIP, EDGE = 4, 2


def quarter_sems(chunks):
    one = pltpu.SemaphoreType.DMA((chunks,))
    two = pltpu.SemaphoreType.DMA((2, chunks))
    return [one, one, two, two, one, one]


def when(cond, *steps):
    @pl.when(cond)
    def _():
        for step in steps:
            step()


def make_spread(window, modes, tile_rows, tile_cols, rows_n, cols_n):
    w = window

    def kernel(tile, probe, right, low, diag, gathered, *sems):
        strip_sems, low_sems, diag_sems = sems[:6], sems[6:12], sems[12:18]
        one_s, one_r, p_s, p_r, x_s, x_r, own_sem = sems[18:]
        r, c, m = place()
        core = lax.rem(c, 2)
        other = c + 1 - 2 * core
        odd, even = core == 1, core == 0
        away = jnp.where(odd, jnp.minimum(c + 1, cols_n - 1), jnp.maximum(c - 1, 0))
        has_away = jnp.where(odd, c < cols_n - 1, c > 0)
        has_diag = has_away & jnp.where(odd, r == 0, r == 1)
        flip = rows_n - 1 - r

        for k in range(1, modes):
            greet(device(r, c, lax.rem(m + k, modes)))
        greet(device(r, other, m))
        greet(device(flip, c, m))
        when(has_away, lambda: greet(device(r, away, m)))
        when(has_diag, lambda: greet(device(flip, away, m)))
        pl.semaphore_wait(
            pltpu.get_barrier_semaphore(),
            modes + 1 + has_away.astype(jnp.int32) + has_diag.astype(jnp.int32),
        )

        strip = Quarters(tile, right, modes, tile_rows, r, away, STRIP, strip_sems, True)
        down = Quarters(tile, low, modes, w, flip, c, EDGE, low_sems)
        corner = Quarters(tile, diag, modes, w, flip, away, EDGE, diag_sems)
        whole = remote(tile, right, one_s.at[0], one_r.at[0], device(r, other, m))
        corner_on = remote(low, diag, one_s.at[1], one_r.at[1], device(r, other, m))

        def probe_of(k, part=None):
            parts = pl.ds(0, 2) if part is None else pl.ds(part, 1)
            return gathered.at[parts, pl.ds(lax.rem(m + modes - k, modes), 1)]

        def probe_copy(k):
            to = device(r, c, lax.rem(m + k, modes))
            return remote(probe, probe_of(0), p_s.at[k], p_r.at[k], to)

        def probe_relay(k):
            block = probe_of(k, 0 if k == 1 else 1)
            at = 0 if k == 1 else 2
            return remote(block, block, p_s.at[at], p_r.at[at], device(r, c, lax.rem(m + k, modes)))

        def probe_pass(k):
            return remote(probe_of(k), probe_of(k), x_s.at[k], x_r.at[k], device(r, other, m))

        def probe_start():
            for k in (1, modes - 1):
                probe_copy(k).start()

        def probe_turn():
            for k in (1, modes - 1):
                probe_copy(k).wait_recv()
                probe_relay(k).start()
                probe_pass(k).start()

        def probe_end():
            for k in (1, modes - 1):
                probe_relay(k).wait_recv()
            probe_pass(2).start()

        def probe_finish():
            for k in (1, modes - 1):
                probe_copy(k).wait_send()
                probe_relay(k).wait_send()
            for k in far:
                probe_pass(k).wait_send()

        def probe_take():
            for k in far:
                probe_pass(k).wait_recv()

        far = (1, modes - 1, 2)
        when(even & has_away, strip.start)
        when(r == 1, down.start)
        when(even & has_diag, corner.start)
        when(even, probe_start)
        when(odd, whole.start)
        keep = pltpu.make_async_copy(probe, gathered.at[:, pl.ds(m, 1)], own_sem)
        keep.start()

        when(odd & has_away, lambda: strip.take([0]))
        when(even, probe_turn)
        when(r == 0, down.take)
        when(odd & has_diag, corner.take)
        when(odd & has_away, lambda: strip.take([1, 2, 3]))
        when(r == 0, down.turn)
        when(odd & has_diag, corner.turn)
        when(odd & has_away, strip.turn)
        when(r == 0, down.finish)
        when(odd & (r == 0), corner_on.start)
        when(even, probe_end)
        when(odd & has_diag, corner.finish)
        when(odd & has_away, strip.finish)
        when(even, whole.wait_recv)
        when(even & (r == 0), corner_on.wait_recv)
        when(odd, probe_take)
        when(even, probe_finish)
        keep.wait()
        when(odd, whole.wait_send)
        when(odd & (r == 0), corner_on.wait_send)
        when(even & has_away, strip.sent)
        when(r == 1, down.sent)
        when(even & has_diag, corner.sent)

    hbm = pl.BlockSpec(memory_space=pl.ANY)
    shape = jax.ShapeDtypeStruct
    dma = pltpu.SemaphoreType.DMA
    return pl.pallas_call(
        kernel,
        name="spread",
        in_specs=[hbm, hbm],
        out_specs=[hbm] * 4,
        out_shape=[
            shape((2, tile_rows, tile_cols), F32),
            shape((2, w, tile_cols), F32),
            shape((2, w, tile_cols), F32),
            shape((2, modes, w, w), F32),
        ],
        scratch_shapes=quarter_sems(STRIP) + quarter_sems(EDGE) + quarter_sems(EDGE)
        + [dma((2,))] * 2 + [dma((modes,))] * 4 + [dma],
        compiler_params=pltpu.CompilerParams(collective_id=0, has_side_effects=True),
    )


def make_collect(window, modes, tile_rows, tile_cols, rows_n, cols_n):
    w = window
    chips = rows_n * cols_n // 2
    piece = 2 * w // chips

    def kernel(g_right, g_low, g_diag, pg, right, low, diag, total, *sems):
        strip_sems, low_sems, diag_sems = sems[:6], sems[6:12], sems[12:18]
        one_s, one_r, x_s, x_r, y_s, y_r, a_s, a_r, b_s, b_r, in_sem, pair, got, mine = sems[18:]
        r, c, m = place()
        core = lax.rem(c, 2)
        chip = r * (cols_n // 2) + c // 2
        other = c + 1 - 2 * core
        odd, even = core == 1, core == 0
        away = jnp.where(odd, jnp.minimum(c + 1, cols_n - 1), jnp.maximum(c - 1, 0))
        has_away = jnp.where(odd, c < cols_n - 1, c > 0)
        flip = rows_n - 1 - r
        over = jnp.where(r == 0, jnp.minimum(c + 1, cols_n - 1), jnp.maximum(c - 1, 0))
        has_over = jnp.where(r == 0, c < cols_n - 1, c > 0)

        def partner(k):
            p = lax.rem(chip + k, chips)
            return device(p // (cols_n // 2), 2 * lax.rem(p, cols_n // 2) + core, m)

        def hello(k, carry):
            greet(partner(k))
            return carry

        greet(device(r, other, m))
        for k in (1, modes - 1):
            greet(device(r, c, lax.rem(m + k, modes)))
        when(has_away, lambda: greet(device(r, away, m)))
        when(has_over, lambda: greet(device(flip, over, m)))
        when(even, lambda: greet(device(flip, c, m)))
        when(odd, lambda: lax.fori_loop(1, chips, hello, 0))
        pl.semaphore_wait(
            pltpu.get_barrier_semaphore(),
            3 + jnp.where(odd, chips - 1, 1) + has_away.astype(jnp.int32) + has_over.astype(jnp.int32),
        )

        strip = Quarters(g_right, right, modes, tile_rows, r, away, STRIP, strip_sems)
        down = Quarters(g_low, low, modes, w, flip, c, EDGE, low_sems)
        corner = Quarters(g_diag, diag, modes, w, flip, over, EDGE, diag_sems)
        whole = remote(g_right, right, one_s, one_r, device(r, other, m))
        swap = remote(pg, pair.at[0], x_s, x_r, device(r, other, m))
        own = pltpu.make_async_copy(pg, pair.at[1], in_sem)
        at_chip = pl.ds(pl.multiple_of(chip * piece, piece), piece)
        rest = got.at[pl.ds(1, chips - 1)]
        many = total.at[pl.ds(0, (chips - 1) * piece), :]
        keep = pltpu.make_async_copy(mine, total.at[at_chip, :], in_sem)
        give = remote(total, total, y_s, y_r, device(r, other, m))

        def scatter_go(k, carry):
            p = lax.rem(chip + k, chips)
            rows = pl.ds(pl.multiple_of(p * piece, piece), piece)
            remote(pair.at[1, rows, :], got.at[k], a_s, a_r, partner(k)).start()
            return carry

        def share_go(k, carry):
            remote(mine, total.at[at_chip, :], b_s, b_r, partner(k)).start()
            return carry

        def add(k, acc):
            return acc + got[k]

        def sum_pair():
            own.wait()
            swap.wait_recv()
            pair[1] = pair[0] + pair[1]
            lax.fori_loop(1, chips, scatter_go, 0)

        def sum_plane():
            pltpu.make_async_copy(rest, rest, a_r).wait()
            mine[...] = lax.fori_loop(1, chips, add, pair[1, at_chip, :]) * (1.0 / 16.0)
            keep.start()
            lax.fori_loop(1, chips, share_go, 0)

        def sum_give():
            keep.wait()
            pltpu.make_async_copy(many, many, b_r).wait()
            give.start()

        def sum_end():
            pltpu.make_async_copy(rest, rest, a_s).wait()
            pltpu.make_async_copy(many, many, b_s).wait()
            give.wait_send()

        when(even, swap.start)
        when(odd, own.start)
        when(odd & has_away, strip.start)
        when(r == 0, down.start)
        when((r == 0) & has_over, corner.start)
        when(even, whole.start)
        when(odd, sum_pair)
        when(even & has_away, strip.take)
        when(r == 1, down.take)
        when((r == 1) & has_over, corner.take)
        when(odd, sum_plane)
        when(even & has_away, strip.turn)
        when(r == 1, down.turn)
        when((r == 1) & has_over, corner.turn)
        when(odd, sum_give)
        when(even & has_away, strip.finish)
        when(r == 1, down.finish)
        when((r == 1) & has_over, corner.finish)
        when(odd, whole.wait_recv)
        when(even, give.wait_recv)
        when(even, swap.wait_send)
        when(odd, sum_end)
        when(odd & has_away, strip.sent)
        when(r == 0, down.sent)
        when((r == 0) & has_over, corner.sent)
        when(even, whole.wait_send)

    hbm = pl.BlockSpec(memory_space=pl.ANY)
    shape = jax.ShapeDtypeStruct
    dma = pltpu.SemaphoreType.DMA
    return pl.pallas_call(
        kernel,
        name="collect",
        in_specs=[hbm] * 4,
        out_specs=[hbm] * 4,
        out_shape=[
            shape((2, tile_rows, tile_cols), F32),
            shape((2, w, tile_cols), F32),
            shape((2, w, tile_cols), F32),
            shape((2 * w, w), F32),
        ],
        scratch_shapes=quarter_sems(STRIP) + quarter_sems(EDGE) + quarter_sems(EDGE) + [dma] * 11
        + [pltpu.VMEM((2, 2 * w, w), F32), pltpu.VMEM((chips, piece, w), F32), pltpu.VMEM((piece, w), F32)],
        compiler_params=pltpu.CompilerParams(collective_id=1, has_side_effects=True),
    )


def make_finish(window, tile_rows, tile_cols):
    w = window
    blocks = tile_rows // w

    def kernel(own, strip, low, diag, total, grad, probe, a, b, e, s_a, s_b, s_e, s_out):
        r, c, m = place()
        below, inner = r > 0, c > 0

        def rows(k):
            return pl.ds(k * w, w)

        loads = [
            [
                pltpu.make_async_copy(own.at[:, rows(k), :], a.at[:, rows(k), :], s_a.at[k]),
                pltpu.make_async_copy(strip.at[:, rows(k), :], b.at[:, rows(k), :], s_b.at[k]),
            ]
            for k in range(blocks)
        ]
        edges = [pltpu.make_async_copy(src, e.at[n], s_e.at[n]) for n, src in enumerate((low, diag, total))]
        for k in reversed(range(blocks)):
            for copy in loads[k]:
                copy.start()
        for copy in edges:
            copy.start()
        stores = [pltpu.make_async_copy(a.at[:, rows(k), :], grad.at[:, rows(k), :], s_out.at[k]) for k in range(blocks)]

        def add(k, x):
            for part in range(2):
                a[part, k * w:k * w + w, :] += x[part]

        for k in reversed(range(blocks)):
            for copy in loads[k]:
                copy.wait()
            when(inner, lambda: add(k, b.at[:, rows(k), :]))
            if k == 0:
                for copy in edges:
                    copy.wait()
                when(below, lambda: add(0, e.at[0]))
                when(below & inner, lambda: add(0, e.at[1]))
                last = pltpu.make_async_copy(e.at[2], probe, s_out.at[blocks])
                last.start()
            stores[k].start()
        for copy in stores + [last]:
            copy.wait()

    hbm = pl.BlockSpec(memory_space=pl.ANY)
    dma = pltpu.SemaphoreType.DMA
    tile = (2, tile_rows, tile_cols)
    return pl.pallas_call(
        kernel,
        name="finish",
        in_specs=[hbm] * 5,
        out_specs=[hbm] * 2,
        out_shape=[jax.ShapeDtypeStruct(tile, F32), jax.ShapeDtypeStruct((2, w, w), F32)],
        scratch_shapes=[
            pltpu.VMEM(tile, F32), pltpu.VMEM(tile, F32), pltpu.VMEM((3, 2, w, w), F32),
            dma((blocks,)), dma((blocks,)), dma((3,)), dma((blocks + 1,)),
        ],
        compiler_params=pltpu.CompilerParams(vmem_limit_bytes=40 << 20),
    )


def per_device(object_slab, probe_modes, amplitudes, scan_counts, scan_positions):
    window = probe_modes.shape[-1]
    tile_rows, tile_cols = object_slab.shape[1:]
    slots = amplitudes.shape[0]
    modes, cols_n, rows_n = (lax.axis_size(a) for a in ("mode", "col", "row"))
    sizes = (window, modes, tile_rows, tile_cols, rows_n, cols_n)
    right, low, diag, probe = make_spread(*sizes)(object_slab, probe_modes)
    consts = [jnp.asarray(t) for t in tables(window)]
    compute = make_compute(window, modes, slots, tile_rows, tile_cols, cols_n)
    g_own, g_right, g_low, g_diag, pg, shift = compute(
        scan_positions, scan_counts, object_slab, right, low, diag, probe, amplitudes, *consts
    )
    from_left, from_up, from_diag, total = make_collect(*sizes)(
        g_right, g_low, g_diag, pg.reshape(2 * window, window)
    )
    grad, probe_grad = make_finish(window, tile_rows, tile_cols)(
        g_own, from_left, from_up, from_diag, total.reshape(2, window, window)
    )
    return (grad, probe_grad.reshape(2, 1, window, window), shift)


def solution(mesh):
    in_specs = (
        P(None, "row", "col"),
        P(None, "mode", None, None),
        P(("row", "col"), None, None),
        P(),
        P(None, ("row", "col")),
    )
    out_specs = (P(None, "row", "col"), P(None, "mode", None, None), P(None, ("row", "col")))
    return jax.shard_map(
        per_device, mesh=mesh, in_specs=in_specs, out_specs=out_specs, check_vma=False
    )
```

```python
import math
import functools
import numpy as np
import jax
import jax.numpy as jnp
from jax import lax
from jax.experimental import pallas as pl
from jax.experimental.pallas import tpu as pltpu
from jax.sharding import PartitionSpec as P

BF = jnp.bfloat16
F32 = jnp.float32
BATCH = 4
CH = 32


def hi_lo(x):
    hi = x.astype(BF)
    lo = (x - hi.astype(F32)).astype(BF)
    return hi, lo


def halves(table):
    table = table.astype(np.float32)
    hi = table.astype(BF)
    return hi, (table - hi.astype(np.float32)).astype(BF)


def angles(window, radix, q):
    part = window // radix
    n, j = np.arange(part)[:, None], np.arange(part)[None, :]
    angle = 2.0 * math.pi * ((n * (radix * j + q)) % window) / window
    return np.cos(angle) / math.sqrt(window), np.sin(angle) / math.sqrt(window)


def tables(window):
    right_f, right_i, left_f, left_i = [], [], [], []
    for q in range(2):
        c, s = angles(window, 2, q)
        for table, into in ((np.block([[c, -s], [s, c]]), right_f), (np.block([[c.T, s.T], [-s.T, c.T]]), right_i)):
            hi, lo = halves(table)
            into.append(np.concatenate([hi, lo, hi], axis=0))
    for q in range(4):
        c, s = angles(window, 4, q)
        for table, into in ((np.block([[c.T, s.T], [-s.T, c.T]]), left_f), (np.block([[c, -s], [s, c]]), left_i)):
            hi, lo = halves(table)
            top = np.concatenate([hi, hi], axis=1)
            into.append(np.concatenate([top, np.concatenate([lo, np.zeros_like(lo)], axis=1)], axis=0))
    order = np.concatenate([np.arange(0, window, 2), np.arange(1, window, 2)])
    shuffle = np.zeros((window, window), np.float32)
    shuffle[order, np.arange(window)] = 1.0
    return np.stack(right_f), np.stack(right_i), np.stack(left_f), np.stack(left_i), shuffle.astype(BF)


def cat(parts, axis):
    return jnp.concatenate(parts, axis=axis)


def mm(a, b):
    return jnp.dot(a, b, preferred_element_type=F32)


def make_compute(window, modes, slots, tile_rows, tile_cols, cols_n):
    w, half, quart = window, window // 2, window // 4
    ch = CH
    ext_rows, ext_cols = tile_rows + w, tile_cols + w

    def kernel(positions, counts, own, right, low, diag, probe, amps, rf, ri, lf, li, shuffle,
               g_own, g_right, g_low, g_diag, pg, along,
               ext, grad, amp_buf, win, fac, lhs, rhs, mid, far, near, amp_sem, sem):
        row_id, col_id, mine = place()
        count = counts[row_id * cols_n + col_id]
        def quarters(whole, parts):
            pairs = []
            for k in range(4):
                for t in range(2):
                    down = slice(tile_rows, ext_rows) if k >= 2 else slice(0, tile_rows)
                    pairs.append((whole.at[2 * (k % 2) + t, :, down, :], parts[k].at[:, :, 128 * t:128 * t + 128]))
            return pairs

        loads = [
            pltpu.make_async_copy(part, inside, sem.at[k])
            for k, (inside, part) in enumerate(quarters(ext, (own, right, low, diag)))
        ]
        for copy in loads:
            copy.start()

        def amp_copies(slot, place):
            return [
                pltpu.make_async_copy(
                    amps.at[slot, :, 128 * t:128 * t + 128], amp_buf.at[place, t], amp_sem.at[place, t]
                )
                for t in range(2)
            ]

        for copy in amp_copies(0, 0):
            copy.start()

        def clear(i, carry):
            at = pl.multiple_of(i * ch, ch)
            for c in range(2):
                for t in range(4):
                    grad[t, c, pl.ds(at, ch), :] = jnp.zeros((ch, 128), F32)
            return carry

        lax.fori_loop(0, ext_rows // ch, clear, 0)
        pg[...] = jnp.zeros(pg.shape, F32)

        def no_shift(i, carry):
            along[0, i] = 0.0
            along[1, i] = 0.0
            return carry

        lax.fori_loop(0, slots, no_shift, 0)
        for copy in loads:
            copy.wait()

        def put_lhs(parity, at, x):
            hi, lo = hi_lo(x)
            lhs[parity, at:at + ch, :w] = hi
            lhs[parity, at:at + ch, w:] = lo

        def put_rhs(m, q, at, x):
            hi, lo = hi_lo(x)
            rhs[m, q, at:at + ch, :] = hi
            rhs[m, q, half + at:half + at + ch, :] = lo

        def right_apply(m, table, into):
            rows = slice(m * w, (m + BATCH) * w)
            for parity in range(2):
                hi, lo = lhs[parity, rows, :w], lhs[parity, rows, w:]
                into[parity, rows, :] = mm(cat([hi, hi, lo], 1), table[parity])

        def left_apply(m, q, table):
            both = mm(table[q], rhs[m, q])
            return both[:half] + both[half:]

        def forward_rows(m):
            for r in range(0, quart, ch):
                y = [[], [], [], []]
                for parity in range(2):
                    x = [mid[parity, m * w + p * quart + r:m * w + p * quart + r + ch, :] for p in range(4)]
                    a, b, c, d = x[0] + x[2], x[1] + x[3], x[0] - x[2], x[1] - x[3]
                    y[0].append(a + b)
                    y[2].append(a - b)
                    turned = cat([d[:, half:], -d[:, :half]], 1)
                    y[1].append(c + turned)
                    y[3].append(c - turned)
                for q in range(4):
                    e, o = y[q]
                    put_rhs(m, q, r, cat([e[:, :half], o[:, :half]], 1))
                    put_rhs(m, q, quart + r, cat([e[:, half:], o[:, half:]], 1))
            for q in range(4):
                far[m, q] = left_apply(m, q, lf)

        def inverse_rows(m):
            for q in range(4):
                for r in range(0, quart, ch):
                    f = fac[q, r:r + ch, :]
                    for at in (r, quart + r):
                        put_rhs(m, q, at, f * far[m, q, at:at + ch, :])
            for q in range(4):
                far[m, q] = left_apply(m, q, li)
            for r in range(0, quart, ch):
                re = [far[m, q, r:r + ch, :] for q in range(4)]
                im = [far[m, q, quart + r:quart + r + ch, :] for q in range(4)]
                are, aim, bre, bim = re[0] + re[2], im[0] + im[2], re[1] + re[3], im[1] + im[3]
                cre, cim, dre, dim = re[0] - re[2], im[0] - im[2], re[1] - re[3], im[1] - im[3]
                outs = (
                    (are + bre, aim + bim), (cre - dim, cim + dre),
                    (are - bre, aim - bim), (cre + dim, cim - dre),
                )
                for p, (xre, xim) in enumerate(outs):
                    for parity in range(2):
                        cols = slice(parity * half, parity * half + half)
                        put_lhs(parity, m * w + p * quart + r, cat([xre[:, cols], xim[:, cols]], 1))

        def do_slot(slot, carry):
            row = positions[0, slot] - row_id * tile_rows
            col = positions[1, slot] - col_id * tile_cols
            tile_at = col // 128
            off = lax.rem(col, 128)
            back = lax.rem(w + 128 - off, w + 128)
            place_at = lax.rem(slot, 2)
            for copy in amp_copies(slot, place_at):
                copy.wait()

            @pl.when(slot + 1 < count)
            def _():
                for copy in amp_copies(slot + 1, 1 - place_at):
                    copy.start()

            for c in range(2):
                for r in range(0, w, ch):
                    wide = cat([ext[tile_at + t, c, pl.ds(row + r, ch), :] for t in range(3)], 1)
                    win[c, r:r + ch, :] = pltpu.roll(wide, back, 1)[:, :w]

            for q in range(4):
                a = cat([amp_buf[place_at, t, pl.ds(q, quart, stride=4), :] for t in range(2)], 1)
                a0, a1 = hi_lo(a)
                a2 = (a - a0.astype(F32) - a1.astype(F32)).astype(BF)
                stack = mm(cat([a0, a1, a2], 0), shuffle[...])
                fac[q] = stack[:quart] + stack[quart:2 * quart] + stack[2 * quart:]

            for m in range(modes):
                for r in range(0, w, ch):
                    vre, vim = win[0, r:r + ch, :], win[1, r:r + ch, :]
                    pre, pim = probe[0, m, r:r + ch, :], probe[1, m, r:r + ch, :]
                    are = pre * vre - pim * vim
                    aim = pre * vim + pim * vre
                    for parity in range(2):
                        if parity == 0:
                            x = cat([are[:, :half] + are[:, half:], aim[:, :half] + aim[:, half:]], 1)
                        else:
                            x = cat([are[:, :half] - are[:, half:], aim[:, :half] - aim[:, half:]], 1)
                        put_lhs(parity, m * w + r, x)
                if (m + 1) % BATCH == 0:
                    right_apply(m + 1 - BATCH, rf, mid)
                    for n in range(m + 1 - BATCH, m + 1):
                        forward_rows(n)

            for q in range(4):
                for r in range(0, quart, ch):
                    total = None
                    for m in range(modes):
                        re = far[m, q, r:r + ch, :]
                        im = far[m, q, quart + r:quart + r + ch, :]
                        term = re * re + im * im
                        total = term if total is None else total + term
                    fac[q, r:r + ch, :] = 0.25 * (1.0 - fac[q, r:r + ch, :] * lax.rsqrt(total + 0.5))

            for m in range(modes):
                inverse_rows(m)
                if (m + 1) % BATCH == 0:
                    right_apply(m + 1 - BATCH, ri, near)

            rows_sum = jnp.zeros((8, w), F32)
            cols_sum = jnp.zeros((8, w), F32)
            lanes = lax.broadcasted_iota(jnp.int32, (ch, w), 1)
            inner = (lanes >= 1) & (lanes <= w - 2)

            def near_of(m, r):
                at = m * w + r
                if not isinstance(m, int):
                    at = pl.multiple_of(at, ch)
                e, o = near[0, pl.ds(at, ch), :], near[1, pl.ds(at, ch), :]
                s, d = e + o, e - o
                return cat([s[:, :half], d[:, :half]], 1), cat([s[:, half:], d[:, half:]], 1)

            for r in range(0, w, ch):
                gre = gim = None
                for m in range(modes):
                    nre, nim = near_of(m, r)
                    pre, pim = probe[0, m, r:r + ch, :], probe[1, m, r:r + ch, :]
                    tre = pre * nre + pim * nim
                    tim = pre * nim - pim * nre
                    gre = tre if gre is None else gre + tre
                    gim = tim if gim is None else gim + tim
                for c, g in ((0, gre), (1, gim)):
                    spread = pltpu.roll(cat([g, jnp.zeros((ch, 128), F32)], 1), off, 1)
                    for t in range(3):
                        grad[tile_at + t, c, pl.ds(row + r, ch), :] += spread[:, 128 * t:128 * t + 128]
                vre, vim = win[0, r:r + ch, :], win[1, r:r + ch, :]
                nre, nim = near_of(mine, r)
                pg[0, r:r + ch, :] += vre * nre + vim * nim
                pg[1, r:r + ch, :] += vre * nim - vim * nre
                dre = pltpu.roll(vre, w - 1, 1) - pltpu.roll(vre, 1, 1)
                dim = pltpu.roll(vim, w - 1, 1) - pltpu.roll(vim, 1, 1)
                t = jnp.where(inner, gre * dre + gim * dim, 0.0)
                cols_sum = cols_sum + jnp.sum(t.reshape(ch // 8, 8, w), axis=0)
                lo_r, hi_r = max(r, 1), min(r + ch, w - 1)
                up = [ext_rows_slice(win, c, r + 1, ch, w) for c in range(2)]
                dn = [ext_rows_slice(win, c, r - 1, ch, w) for c in range(2)]
                t = gre * (up[0] - dn[0]) + gim * (up[1] - dn[1])
                if lo_r != r or hi_r != r + ch:
                    idx = lax.broadcasted_iota(jnp.int32, (ch, w), 0) + r
                    t = jnp.where((idx >= lo_r) & (idx < hi_r), t, 0.0)
                rows_sum = rows_sum + jnp.sum(t.reshape(ch // 8, 8, w), axis=0)
            along[0, slot] = jnp.sum(rows_sum) * (0.5 / w)
            along[1, slot] = jnp.sum(cols_sum) * (0.5 / w)
            return carry

        def ext_rows_slice(ref, c, start, size, width):
            if start < 0:
                return cat([ref[c, 0:1, :], ref[c, 0:size - 1, :]], 0)
            if start + size > w:
                return cat([ref[c, start:w, :], ref[c, w - 1:w, :]], 0)
            return ref[c, start:start + size, :]

        lax.fori_loop(0, count, do_slot, 0)
        stores = [
            pltpu.make_async_copy(inside, part, sem.at[k])
            for k, (inside, part) in enumerate(quarters(grad, (g_own, g_right, g_low, g_diag)))
        ]
        for copy in stores:
            copy.start()
        for copy in stores:
            copy.wait()

    hbm = pl.BlockSpec(memory_space=pl.ANY)
    vmem = pl.BlockSpec(memory_space=pltpu.VMEM)
    smem = pl.BlockSpec(memory_space=pltpu.SMEM)
    shape = jax.ShapeDtypeStruct
    return pl.pallas_call(
        kernel,
        name="slots",
        in_specs=[smem, smem, hbm, hbm, hbm, hbm, vmem, hbm, vmem, vmem, vmem, vmem, vmem],
        out_specs=[hbm, hbm, hbm, hbm, vmem, smem],
        out_shape=[
            shape((2, tile_rows, tile_cols), F32),
            shape((2, tile_rows, w), F32),
            shape((2, w, tile_cols), F32),
            shape((2, w, w), F32),
            shape((2, w, w), F32),
            shape((2, slots), F32),
        ],
        scratch_shapes=[
            pltpu.VMEM((ext_cols // 128, 2, ext_rows, 128), F32),
            pltpu.VMEM((ext_cols // 128, 2, ext_rows, 128), F32),
            pltpu.VMEM((2, 2, w, 128), F32),
            pltpu.VMEM((2, w, w), F32),
            pltpu.VMEM((4, quart, w), F32),
            pltpu.VMEM((2, modes * w, 2 * w), BF),
            pltpu.VMEM((modes, 4, w, w), BF),
            pltpu.VMEM((2, modes * w, w), F32),
            pltpu.VMEM((modes, 4, half, w), F32),
            pltpu.VMEM((2, modes * w, w), F32),
            pltpu.SemaphoreType.DMA((2, 2)),
            pltpu.SemaphoreType.DMA((8,)),
        ],
        compiler_params=pltpu.CompilerParams(vmem_limit_bytes=60 << 20),
        cost_estimate=pl.CostEstimate(flops=10**11, bytes_accessed=10**7, transcendentals=0),
    )


MESH = pl.DeviceIdType.MESH


def place():
    return lax.axis_index("row"), lax.axis_index("col"), lax.axis_index("mode")


def device(r, c, m):
    return {"row": r, "col": c, "mode": m}


def remote(src, dst, send, recv, to):
    return pltpu.make_async_remote_copy(
        src_ref=src, dst_ref=dst, send_sem=send, recv_sem=recv, device_id=to, device_id_type=MESH
    )


def greet(to):
    pl.semaphore_signal(pltpu.get_barrier_semaphore(), inc=1, device_id=to, device_id_type=MESH)


class Quarters:
    def __init__(self, src, dst, modes, rows, r, c, chunks, sems, direct=False):
        me_r, me_c, m = place()
        self.m, self.modes, self.chunks, self.direct = m, modes, chunks, direct
        self.rows = rows // modes // chunks
        self.src, self.dst = src, dst
        self.ys, self.yr, self.zs, self.zr, self.ts, self.tr = sems
        self.peer = device(r, c, m)
        self.next = device(me_r, me_c, lax.rem(m + 1, modes))
        self.prev = device(me_r, me_c, lax.rem(m + modes - 1, modes))

    def part(self, ref, owner, i):
        at = pl.multiple_of((owner * self.chunks + i) * self.rows, self.rows)
        return ref.at[:, pl.ds(at, self.rows), :]

    def first(self, i):
        mine = self.part(self.src, self.m, i)
        return remote(mine, self.part(self.dst, self.m, i), self.ys.at[i], self.yr.at[i], self.peer)

    def ring(self, i, way):
        mine = self.part(self.dst, self.m, i)
        return remote(mine, mine, self.zs.at[way, i], self.zr.at[way, i], self.next if way == 0 else self.prev)

    def way(self, i):
        return 0 if i < self.chunks // 2 else 1

    def relay(self, i):
        back = self.modes - 1 if self.way(i) == 0 else 1
        block = self.part(self.dst, lax.rem(self.m + back, self.modes), i)
        return remote(block, block, self.ts.at[i], self.tr.at[i], self.next if self.way(i) == 0 else self.prev)

    def second(self, i):
        owner = lax.rem(self.m + self.modes // 2, self.modes)
        return remote(
            self.part(self.src, owner, i), self.part(self.dst, owner, i), self.ts.at[i], self.tr.at[i], self.peer
        )

    def start(self):
        for i in range(self.chunks):
            self.first(i).start()
        for i in range(self.chunks) if self.direct else ():
            self.second(i).start()

    def sent(self):
        for i in range(self.chunks):
            self.first(i).wait_send()
            if self.direct:
                self.second(i).wait_send()

    def take(self, some=None):
        for i in range(self.chunks) if some is None else some:
            self.first(i).wait_recv()
            self.ring(i, 0).start()
            self.ring(i, 1).start()

    def turn(self):
        for i in range(self.chunks):
            self.ring(i, self.way(i)).wait_recv()
            if not self.direct:
                self.relay(i).start()

    def finish(self):
        for i in range(self.chunks):
            self.ring(i, 1 - self.way(i)).wait_recv()
            if self.direct:
                self.second(i).wait_recv()
            else:
                self.relay(i).wait_recv()
        for i in range(self.chunks):
            self.ring(i, 0).wait_send()
            self.ring(i, 1).wait_send()
            if not self.direct:
                self.relay(i).wait_send()


STRIP, EDGE = 4, 2


def quarter_sems(chunks):
    one = pltpu.SemaphoreType.DMA((chunks,))
    two = pltpu.SemaphoreType.DMA((2, chunks))
    return [one, one, two, two, one, one]


def when(cond, *steps):
    @pl.when(cond)
    def _():
        for step in steps:
            step()


def make_spread(window, modes, tile_rows, tile_cols, rows_n, cols_n):
    w = window

    def kernel(tile, probe, right, low, diag, gathered, *sems):
        strip_sems, low_sems, diag_sems = sems[:6], sems[6:12], sems[12:18]
        one_s, one_r, p_s, p_r, x_s, x_r, own_sem = sems[18:]
        r, c, m = place()
        core = lax.rem(c, 2)
        other = c + 1 - 2 * core
        odd, even = core == 1, core == 0
        away = jnp.where(odd, jnp.minimum(c + 1, cols_n - 1), jnp.maximum(c - 1, 0))
        has_away = jnp.where(odd, c < cols_n - 1, c > 0)
        has_diag = has_away & jnp.where(odd, r == 0, r == 1)
        flip = rows_n - 1 - r

        for k in range(1, modes):
            greet(device(r, c, lax.rem(m + k, modes)))
        greet(device(r, other, m))
        greet(device(flip, c, m))
        when(has_away, lambda: greet(device(r, away, m)))
        when(has_diag, lambda: greet(device(flip, away, m)))
        pl.semaphore_wait(
            pltpu.get_barrier_semaphore(),
            modes + 1 + has_away.astype(jnp.int32) + has_diag.astype(jnp.int32),
        )

        strip = Quarters(tile, right, modes, tile_rows, r, away, STRIP, strip_sems, True)
        down = Quarters(tile, low, modes, w, flip, c, EDGE, low_sems)
        corner = Quarters(tile, diag, modes, w, flip, away, EDGE, diag_sems)
        whole = remote(tile, right, one_s.at[0], one_r.at[0], device(r, other, m))
        corner_on = remote(low, diag, one_s.at[1], one_r.at[1], device(r, other, m))

        def probe_of(k, part=None):
            parts = pl.ds(0, 2) if part is None else pl.ds(part, 1)
            return gathered.at[parts, pl.ds(lax.rem(m + modes - k, modes), 1)]

        def probe_copy(k):
            to = device(r, c, lax.rem(m + k, modes))
            return remote(probe, probe_of(0), p_s.at[k], p_r.at[k], to)

        def probe_relay(k):
            block = probe_of(k, 0 if k == 1 else 1)
            at = 0 if k == 1 else 2
            return remote(block, block, p_s.at[at], p_r.at[at], device(r, c, lax.rem(m + k, modes)))

        def probe_pass(k):
            return remote(probe_of(k), probe_of(k), x_s.at[k], x_r.at[k], device(r, other, m))

        def probe_start():
            for k in (1, modes - 1):
                probe_copy(k).start()

        def probe_turn():
            for k in (1, modes - 1):
                probe_copy(k).wait_recv()
                probe_relay(k).start()
                probe_pass(k).start()

        def probe_end():
            for k in (1, modes - 1):
                probe_relay(k).wait_recv()
            probe_pass(2).start()

        def probe_finish():
            for k in (1, modes - 1):
                probe_copy(k).wait_send()
                probe_relay(k).wait_send()
            for k in far:
                probe_pass(k).wait_send()

        def probe_take():
            for k in far:
                probe_pass(k).wait_recv()

        far = (1, modes - 1, 2)
        when(r == 1, down.start)
        when(even & has_diag, corner.start)
        when(even & has_away, strip.start)
        when(even, probe_start)
        when(odd, whole.start)
        keep = pltpu.make_async_copy(probe, gathered.at[:, pl.ds(m, 1)], own_sem)
        keep.start()

        when(r == 0, down.take)
        when(odd & has_diag, corner.take)
        when(odd & has_away, lambda: strip.take([0]))
        when(r == 0, down.turn)
        when(odd & has_diag, corner.turn)
        when(even, probe_turn)
        when(odd & has_away, lambda: strip.take([1, 2, 3]))
        when(r == 0, down.finish)
        when(odd & (r == 0), corner_on.start)
        when(odd & has_away, strip.turn)
        when(even, probe_end)
        when(odd & has_diag, corner.finish)
        when(odd & has_away, strip.finish)
        when(even, whole.wait_recv)
        when(even & (r == 0), corner_on.wait_recv)
        when(odd, probe_take)
        when(even, probe_finish)
        keep.wait()
        when(odd, whole.wait_send)
        when(odd & (r == 0), corner_on.wait_send)
        when(even & has_away, strip.sent)
        when(r == 1, down.sent)
        when(even & has_diag, corner.sent)

    hbm = pl.BlockSpec(memory_space=pl.ANY)
    shape = jax.ShapeDtypeStruct
    dma = pltpu.SemaphoreType.DMA
    return pl.pallas_call(
        kernel,
        name="spread",
        in_specs=[hbm, hbm],
        out_specs=[hbm] * 4,
        out_shape=[
            shape((2, tile_rows, tile_cols), F32),
            shape((2, w, tile_cols), F32),
            shape((2, w, tile_cols), F32),
            shape((2, modes, w, w), F32),
        ],
        scratch_shapes=quarter_sems(STRIP) + quarter_sems(EDGE) + quarter_sems(EDGE)
        + [dma((2,))] * 2 + [dma((modes,))] * 4 + [dma],
        compiler_params=pltpu.CompilerParams(collective_id=0, has_side_effects=True),
    )


def make_collect(window, modes, tile_rows, tile_cols, rows_n, cols_n):
    w = window
    chips = rows_n * cols_n // 2
    piece = 2 * w // chips

    def kernel(g_right, g_low, g_diag, pg, right, low, diag, total, *sems):
        strip_sems, low_sems, diag_sems = sems[:6], sems[6:12], sems[12:18]
        one_s, one_r, x_s, x_r, y_s, y_r, a_s, a_r, b_s, b_r, in_sem, pair, got, mine = sems[18:]
        r, c, m = place()
        core = lax.rem(c, 2)
        chip = r * (cols_n // 2) + c // 2
        other = c + 1 - 2 * core
        odd, even = core == 1, core == 0
        away = jnp.where(odd, jnp.minimum(c + 1, cols_n - 1), jnp.maximum(c - 1, 0))
        has_away = jnp.where(odd, c < cols_n - 1, c > 0)
        flip = rows_n - 1 - r
        over = jnp.where(r == 0, jnp.minimum(c + 1, cols_n - 1), jnp.maximum(c - 1, 0))
        has_over = jnp.where(r == 0, c < cols_n - 1, c > 0)

        def partner(k):
            p = lax.rem(chip + k, chips)
            return device(p // (cols_n // 2), 2 * lax.rem(p, cols_n // 2) + core, m)

        def hello(k, carry):
            greet(partner(k))
            return carry

        greet(device(r, other, m))
        for k in (1, modes - 1):
            greet(device(r, c, lax.rem(m + k, modes)))
        when(has_away, lambda: greet(device(r, away, m)))
        when(has_over, lambda: greet(device(flip, over, m)))
        when(even, lambda: greet(device(flip, c, m)))
        when(odd, lambda: lax.fori_loop(1, chips, hello, 0))
        pl.semaphore_wait(
            pltpu.get_barrier_semaphore(),
            3 + jnp.where(odd, chips - 1, 1) + has_away.astype(jnp.int32) + has_over.astype(jnp.int32),
        )

        strip = Quarters(g_right, right, modes, tile_rows, r, away, STRIP, strip_sems)
        down = Quarters(g_low, low, modes, w, flip, c, EDGE, low_sems)
        corner = Quarters(g_diag, diag, modes, w, flip, over, EDGE, diag_sems)
        whole = remote(g_right, right, one_s, one_r, device(r, other, m))
        swap = remote(pg, pair.at[0], x_s, x_r, device(r, other, m))
        own = pltpu.make_async_copy(pg, pair.at[1], in_sem)
        at_chip = pl.ds(pl.multiple_of(chip * piece, piece), piece)
        rest = got.at[pl.ds(1, chips - 1)]
        many = total.at[pl.ds(0, (chips - 1) * piece), :]
        keep = pltpu.make_async_copy(mine, total.at[at_chip, :], in_sem)
        give = remote(total, total, y_s, y_r, device(r, other, m))

        def scatter_go(k, carry):
            p = lax.rem(chip + k, chips)
            rows = pl.ds(pl.multiple_of(p * piece, piece), piece)
            remote(pair.at[1, rows, :], got.at[k], a_s, a_r, partner(k)).start()
            return carry

        def share_go(k, carry):
            remote(mine, total.at[at_chip, :], b_s, b_r, partner(k)).start()
            return carry

        def add(k, acc):
            return acc + got[k]

        def sum_pair():
            own.wait()
            swap.wait_recv()
            pair[1] = pair[0] + pair[1]
            lax.fori_loop(1, chips, scatter_go, 0)

        def sum_plane():
            pltpu.make_async_copy(rest, rest, a_r).wait()
            mine[...] = lax.fori_loop(1, chips, add, pair[1, at_chip, :]) * (1.0 / 16.0)
            keep.start()
            lax.fori_loop(1, chips, share_go, 0)

        def sum_give():
            keep.wait()
            pltpu.make_async_copy(many, many, b_r).wait()
            give.start()

        def sum_end():
            pltpu.make_async_copy(rest, rest, a_s).wait()
            pltpu.make_async_copy(many, many, b_s).wait()
            give.wait_send()

        when(even, swap.start)
        when(odd, own.start)
        when(r == 0, down.start)
        when((r == 0) & has_over, corner.start)
        when(odd & has_away, strip.start)
        when(even, whole.start)
        when(odd, sum_pair)
        when(r == 1, down.take)
        when((r == 1) & has_over, corner.take)
        when(even & has_away, lambda: strip.take([0]))
        when(r == 1, down.turn)
        when((r == 1) & has_over, corner.turn)
        when(odd, sum_plane)
        when(even & has_away, lambda: strip.take([1, 2, 3]))
        when(even & has_away, strip.turn)
        when(odd, sum_give)
        when(even & has_away, strip.finish)
        when(r == 1, down.finish)
        when((r == 1) & has_over, corner.finish)
        when(odd, whole.wait_recv)
        when(even, give.wait_recv)
        when(even, swap.wait_send)
        when(odd, sum_end)
        when(odd & has_away, strip.sent)
        when(r == 0, down.sent)
        when((r == 0) & has_over, corner.sent)
        when(even, whole.wait_send)

    hbm = pl.BlockSpec(memory_space=pl.ANY)
    shape = jax.ShapeDtypeStruct
    dma = pltpu.SemaphoreType.DMA
    return pl.pallas_call(
        kernel,
        name="collect",
        in_specs=[hbm] * 4,
        out_specs=[hbm] * 4,
        out_shape=[
            shape((2, tile_rows, tile_cols), F32),
            shape((2, w, tile_cols), F32),
            shape((2, w, tile_cols), F32),
            shape((2 * w, w), F32),
        ],
        scratch_shapes=quarter_sems(STRIP) + quarter_sems(EDGE) + quarter_sems(EDGE) + [dma] * 11
        + [pltpu.VMEM((2, 2 * w, w), F32), pltpu.VMEM((chips, piece, w), F32), pltpu.VMEM((piece, w), F32)],
        compiler_params=pltpu.CompilerParams(collective_id=1, has_side_effects=True),
    )


def make_finish(window, tile_rows, tile_cols):
    w = window
    blocks = tile_rows // w

    def kernel(own, strip, low, diag, total, grad, probe, a, b, e, s_a, s_b, s_e, s_out):
        r, c, m = place()
        below, inner = r > 0, c > 0

        def rows(k):
            return pl.ds(k * w, w)

        loads = [
            [
                pltpu.make_async_copy(own.at[:, rows(k), :], a.at[:, rows(k), :], s_a.at[k]),
                pltpu.make_async_copy(strip.at[:, rows(k), :], b.at[:, rows(k), :], s_b.at[k]),
            ]
            for k in range(blocks)
        ]
        edges = [pltpu.make_async_copy(src, e.at[n], s_e.at[n]) for n, src in enumerate((low, diag, total))]
        for k in reversed(range(blocks)):
            for copy in loads[k]:
                copy.start()
        for copy in edges:
            copy.start()
        stores = [pltpu.make_async_copy(a.at[:, rows(k), :], grad.at[:, rows(k), :], s_out.at[k]) for k in range(blocks)]

        def add(k, x):
            for part in range(2):
                a[part, k * w:k * w + w, :] += x[part]

        for k in reversed(range(blocks)):
            for copy in loads[k]:
                copy.wait()
            when(inner, lambda: add(k, b.at[:, rows(k), :]))
            if k == 0:
                for copy in edges:
                    copy.wait()
                when(below, lambda: add(0, e.at[0]))
                when(below & inner, lambda: add(0, e.at[1]))
                last = pltpu.make_async_copy(e.at[2], probe, s_out.at[blocks])
                last.start()
            stores[k].start()
        for copy in stores + [last]:
            copy.wait()

    hbm = pl.BlockSpec(memory_space=pl.ANY)
    dma = pltpu.SemaphoreType.DMA
    tile = (2, tile_rows, tile_cols)
    return pl.pallas_call(
        kernel,
        name="finish",
        in_specs=[hbm] * 5,
        out_specs=[hbm] * 2,
        out_shape=[jax.ShapeDtypeStruct(tile, F32), jax.ShapeDtypeStruct((2, w, w), F32)],
        scratch_shapes=[
            pltpu.VMEM(tile, F32), pltpu.VMEM(tile, F32), pltpu.VMEM((3, 2, w, w), F32),
            dma((blocks,)), dma((blocks,)), dma((3,)), dma((blocks + 1,)),
        ],
        compiler_params=pltpu.CompilerParams(vmem_limit_bytes=60 << 20),
    )


def per_device(object_slab, probe_modes, amplitudes, scan_counts, scan_positions):
    window = probe_modes.shape[-1]
    tile_rows, tile_cols = object_slab.shape[1:]
    slots = amplitudes.shape[0]
    modes, cols_n, rows_n = (lax.axis_size(a) for a in ("mode", "col", "row"))
    sizes = (window, modes, tile_rows, tile_cols, rows_n, cols_n)
    right, low, diag, probe = make_spread(*sizes)(object_slab, probe_modes)
    consts = [jnp.asarray(t) for t in tables(window)]
    compute = make_compute(window, modes, slots, tile_rows, tile_cols, cols_n)
    g_own, g_right, g_low, g_diag, pg, shift = compute(
        scan_positions, scan_counts, object_slab, right, low, diag, probe, amplitudes, *consts
    )
    from_left, from_up, from_diag, total = make_collect(*sizes)(
        g_right, g_low, g_diag, pg.reshape(2 * window, window)
    )
    grad, probe_grad = make_finish(window, tile_rows, tile_cols)(
        g_own, from_left, from_up, from_diag, total.reshape(2, window, window)
    )
    return (grad, probe_grad.reshape(2, 1, window, window), shift)


def solution(mesh):
    in_specs = (
        P(None, "row", "col"),
        P(None, "mode", None, None),
        P(("row", "col"), None, None),
        P(),
        P(None, ("row", "col")),
    )
    out_specs = (P(None, "row", "col"), P(None, "mode", None, None), P(None, ("row", "col")))
    return jax.shard_map(
        per_device, mesh=mesh, in_specs=in_specs, out_specs=out_specs, check_vma=False
    )
```

```python
import math
import functools
import numpy as np
import jax
import jax.numpy as jnp
from jax import lax
from jax.experimental import pallas as pl
from jax.experimental.pallas import tpu as pltpu
from jax.sharding import PartitionSpec as P

BF = jnp.bfloat16
F32 = jnp.float32
BATCH = 4
CH = 32


def hi_lo(x):
    hi = x.astype(BF)
    lo = (x - hi.astype(F32)).astype(BF)
    return hi, lo


def halves(table):
    table = table.astype(np.float32)
    hi = table.astype(BF)
    return hi, (table - hi.astype(np.float32)).astype(BF)


def angles(window, radix, q):
    part = window // radix
    n, j = np.arange(part)[:, None], np.arange(part)[None, :]
    angle = 2.0 * math.pi * ((n * (radix * j + q)) % window) / window
    return np.cos(angle) / math.sqrt(window), np.sin(angle) / math.sqrt(window)


def tables(window):
    right_f, right_i, left_f, left_i = [], [], [], []
    for q in range(2):
        c, s = angles(window, 2, q)
        for table, into in ((np.block([[c, -s], [s, c]]), right_f), (np.block([[c.T, s.T], [-s.T, c.T]]), right_i)):
            hi, lo = halves(table)
            into.append(np.concatenate([hi, lo, hi], axis=0))
    for q in range(4):
        c, s = angles(window, 4, q)
        for table, into in ((np.block([[c.T, s.T], [-s.T, c.T]]), left_f), (np.block([[c, -s], [s, c]]), left_i)):
            hi, lo = halves(table)
            top = np.concatenate([hi, hi], axis=1)
            into.append(np.concatenate([top, np.concatenate([lo, np.zeros_like(lo)], axis=1)], axis=0))
    order = np.concatenate([np.arange(0, window, 2), np.arange(1, window, 2)])
    shuffle = np.zeros((window, window), np.float32)
    shuffle[order, np.arange(window)] = 1.0
    return np.stack(right_f), np.stack(right_i), np.stack(left_f), np.stack(left_i), shuffle.astype(BF)


def cat(parts, axis):
    return jnp.concatenate(parts, axis=axis)


def mm(a, b):
    return jnp.dot(a, b, preferred_element_type=F32)


def make_compute(window, modes, slots, tile_rows, tile_cols, cols_n):
    w, half, quart = window, window // 2, window // 4
    ch = CH
    ext_rows, ext_cols = tile_rows + w, tile_cols + w

    def kernel(positions, counts, own, right, low, diag, probe, amps, rf, ri, lf, li, shuffle,
               g_own, g_right, g_low, g_diag, pg, along,
               ext, grad, amp_buf, win, fac, lhs, rhs, mid, far, near, amp_sem, sem):
        row_id, col_id, mine = place()
        count = counts[row_id * cols_n + col_id]
        def quarters(whole, parts):
            pairs = []
            for k in range(4):
                for t in range(2):
                    down = slice(tile_rows, ext_rows) if k >= 2 else slice(0, tile_rows)
                    pairs.append((whole.at[2 * (k % 2) + t, :, down, :], parts[k].at[:, :, 128 * t:128 * t + 128]))
            return pairs

        loads = [
            pltpu.make_async_copy(part, inside, sem.at[k])
            for k, (inside, part) in enumerate(quarters(ext, (own, right, low, diag)))
        ]
        for copy in loads:
            copy.start()

        def amp_copies(slot, place):
            return [
                pltpu.make_async_copy(
                    amps.at[slot, :, 128 * t:128 * t + 128], amp_buf.at[place, t], amp_sem.at[place, t]
                )
                for t in range(2)
            ]

        for copy in amp_copies(0, 0):
            copy.start()

        def clear(i, carry):
            at = pl.multiple_of(i * ch, ch)
            for c in range(2):
                for t in range(4):
                    grad[t, c, pl.ds(at, ch), :] = jnp.zeros((ch, 128), F32)
            return carry

        lax.fori_loop(0, ext_rows // ch, clear, 0)
        pg[...] = jnp.zeros(pg.shape, F32)

        def no_shift(i, carry):
            along[0, i] = 0.0
            along[1, i] = 0.0
            return carry

        lax.fori_loop(0, slots, no_shift, 0)
        for copy in loads:
            copy.wait()

        def put_lhs(parity, at, x):
            hi, lo = hi_lo(x)
            lhs[parity, at:at + ch, :w] = hi
            lhs[parity, at:at + ch, w:] = lo

        def put_rhs(m, q, at, x):
            hi, lo = hi_lo(x)
            rhs[m, q, at:at + ch, :] = hi
            rhs[m, q, half + at:half + at + ch, :] = lo

        def right_apply(m, table, into):
            rows = slice(m * w, (m + BATCH) * w)
            for parity in range(2):
                hi, lo = lhs[parity, rows, :w], lhs[parity, rows, w:]
                into[parity, rows, :] = mm(cat([hi, hi, lo], 1), table[parity])

        def left_apply(m, q, table):
            both = mm(table[q], rhs[m, q])
            return both[:half] + both[half:]

        def forward_rows(m):
            for r in range(0, quart, ch):
                y = [[], [], [], []]
                for parity in range(2):
                    x = [mid[parity, m * w + p * quart + r:m * w + p * quart + r + ch, :] for p in range(4)]
                    a, b, c, d = x[0] + x[2], x[1] + x[3], x[0] - x[2], x[1] - x[3]
                    y[0].append(a + b)
                    y[2].append(a - b)
                    turned = cat([d[:, half:], -d[:, :half]], 1)
                    y[1].append(c + turned)
                    y[3].append(c - turned)
                for q in range(4):
                    e, o = y[q]
                    put_rhs(m, q, r, cat([e[:, :half], o[:, :half]], 1))
                    put_rhs(m, q, quart + r, cat([e[:, half:], o[:, half:]], 1))
            for q in range(4):
                far[m, q] = left_apply(m, q, lf)

        def inverse_rows(m):
            for q in range(4):
                for r in range(0, quart, ch):
                    f = fac[q, r:r + ch, :]
                    for at in (r, quart + r):
                        put_rhs(m, q, at, f * far[m, q, at:at + ch, :])
            for q in range(4):
                far[m, q] = left_apply(m, q, li)
            for r in range(0, quart, ch):
                re = [far[m, q, r:r + ch, :] for q in range(4)]
                im = [far[m, q, quart + r:quart + r + ch, :] for q in range(4)]
                are, aim, bre, bim = re[0] + re[2], im[0] + im[2], re[1] + re[3], im[1] + im[3]
                cre, cim, dre, dim = re[0] - re[2], im[0] - im[2], re[1] - re[3], im[1] - im[3]
                outs = (
                    (are + bre, aim + bim), (cre - dim, cim + dre),
                    (are - bre, aim - bim), (cre + dim, cim - dre),
                )
                for p, (xre, xim) in enumerate(outs):
                    for parity in range(2):
                        cols = slice(parity * half, parity * half + half)
                        put_lhs(parity, m * w + p * quart + r, cat([xre[:, cols], xim[:, cols]], 1))

        def do_slot(slot, carry):
            row = positions[0, slot] - row_id * tile_rows
            col = positions[1, slot] - col_id * tile_cols
            tile_at = col // 128
            off = lax.rem(col, 128)
            back = lax.rem(w + 128 - off, w + 128)
            place_at = lax.rem(slot, 2)
            for copy in amp_copies(slot, place_at):
                copy.wait()

            @pl.when(slot + 1 < count)
            def _():
                for copy in amp_copies(slot + 1, 1 - place_at):
                    copy.start()

            for c in range(2):
                for r in range(0, w, ch):
                    wide = cat([ext[tile_at + t, c, pl.ds(row + r, ch), :] for t in range(3)], 1)
                    win[c, r:r + ch, :] = pltpu.roll(wide, back, 1)[:, :w]

            for q in range(4):
                a = cat([amp_buf[place_at, t, pl.ds(q, quart, stride=4), :] for t in range(2)], 1)
                a0, a1 = hi_lo(a)
                a2 = (a - a0.astype(F32) - a1.astype(F32)).astype(BF)
                stack = mm(cat([a0, a1, a2], 0), shuffle[...])
                fac[q] = stack[:quart] + stack[quart:2 * quart] + stack[2 * quart:]

            for m in range(modes):
                for r in range(0, w, ch):
                    vre, vim = win[0, r:r + ch, :], win[1, r:r + ch, :]
                    pre, pim = probe[0, m, r:r + ch, :], probe[1, m, r:r + ch, :]
                    are = pre * vre - pim * vim
                    aim = pre * vim + pim * vre
                    for parity in range(2):
                        if parity == 0:
                            x = cat([are[:, :half] + are[:, half:], aim[:, :half] + aim[:, half:]], 1)
                        else:
                            x = cat([are[:, :half] - are[:, half:], aim[:, :half] - aim[:, half:]], 1)
                        put_lhs(parity, m * w + r, x)
                if (m + 1) % BATCH == 0:
                    right_apply(m + 1 - BATCH, rf, mid)
                    for n in range(m + 1 - BATCH, m + 1):
                        forward_rows(n)

            for q in range(4):
                for r in range(0, quart, ch):
                    total = None
                    for m in range(modes):
                        re = far[m, q, r:r + ch, :]
                        im = far[m, q, quart + r:quart + r + ch, :]
                        term = re * re + im * im
                        total = term if total is None else total + term
                    fac[q, r:r + ch, :] = 0.25 * (1.0 - fac[q, r:r + ch, :] * lax.rsqrt(total + 0.5))

            for m in range(modes):
                inverse_rows(m)
                if (m + 1) % BATCH == 0:
                    right_apply(m + 1 - BATCH, ri, near)

            rows_sum = jnp.zeros((8, w), F32)
            cols_sum = jnp.zeros((8, w), F32)
            lanes = lax.broadcasted_iota(jnp.int32, (ch, w), 1)
            inner = (lanes >= 1) & (lanes <= w - 2)

            def near_of(m, r):
                at = m * w + r
                if not isinstance(m, int):
                    at = pl.multiple_of(at, ch)
                e, o = near[0, pl.ds(at, ch), :], near[1, pl.ds(at, ch), :]
                s, d = e + o, e - o
                return cat([s[:, :half], d[:, :half]], 1), cat([s[:, half:], d[:, half:]], 1)

            for r in range(0, w, ch):
                gre = gim = None
                for m in range(modes):
                    nre, nim = near_of(m, r)
                    pre, pim = probe[0, m, r:r + ch, :], probe[1, m, r:r + ch, :]
                    tre = pre * nre + pim * nim
                    tim = pre * nim - pim * nre
                    gre = tre if gre is None else gre + tre
                    gim = tim if gim is None else gim + tim
                for c, g in ((0, gre), (1, gim)):
                    spread = pltpu.roll(cat([g, jnp.zeros((ch, 128), F32)], 1), off, 1)
                    for t in range(3):
                        grad[tile_at + t, c, pl.ds(row + r, ch), :] += spread[:, 128 * t:128 * t + 128]
                vre, vim = win[0, r:r + ch, :], win[1, r:r + ch, :]
                nre, nim = near_of(mine, r)
                pg[0, r:r + ch, :] += vre * nre + vim * nim
                pg[1, r:r + ch, :] += vre * nim - vim * nre
                dre = pltpu.roll(vre, w - 1, 1) - pltpu.roll(vre, 1, 1)
                dim = pltpu.roll(vim, w - 1, 1) - pltpu.roll(vim, 1, 1)
                t = jnp.where(inner, gre * dre + gim * dim, 0.0)
                cols_sum = cols_sum + jnp.sum(t.reshape(ch // 8, 8, w), axis=0)
                lo_r, hi_r = max(r, 1), min(r + ch, w - 1)
                up = [ext_rows_slice(win, c, r + 1, ch, w) for c in range(2)]
                dn = [ext_rows_slice(win, c, r - 1, ch, w) for c in range(2)]
                t = gre * (up[0] - dn[0]) + gim * (up[1] - dn[1])
                if lo_r != r or hi_r != r + ch:
                    idx = lax.broadcasted_iota(jnp.int32, (ch, w), 0) + r
                    t = jnp.where((idx >= lo_r) & (idx < hi_r), t, 0.0)
                rows_sum = rows_sum + jnp.sum(t.reshape(ch // 8, 8, w), axis=0)
            along[0, slot] = jnp.sum(rows_sum) * (0.5 / w)
            along[1, slot] = jnp.sum(cols_sum) * (0.5 / w)
            return carry

        def ext_rows_slice(ref, c, start, size, width):
            if start < 0:
                return cat([ref[c, 0:1, :], ref[c, 0:size - 1, :]], 0)
            if start + size > w:
                return cat([ref[c, start:w, :], ref[c, w - 1:w, :]], 0)
            return ref[c, start:start + size, :]

        lax.fori_loop(0, count, do_slot, 0)
        stores = [
            pltpu.make_async_copy(inside, part, sem.at[k])
            for k, (inside, part) in enumerate(quarters(grad, (g_own, g_right, g_low, g_diag)))
        ]
        for copy in stores:
            copy.start()
        for copy in stores:
            copy.wait()

    hbm = pl.BlockSpec(memory_space=pl.ANY)
    vmem = pl.BlockSpec(memory_space=pltpu.VMEM)
    smem = pl.BlockSpec(memory_space=pltpu.SMEM)
    shape = jax.ShapeDtypeStruct
    return pl.pallas_call(
        kernel,
        name="slots",
        in_specs=[smem, smem, hbm, hbm, hbm, hbm, vmem, hbm, vmem, vmem, vmem, vmem, vmem],
        out_specs=[hbm, hbm, hbm, hbm, vmem, smem],
        out_shape=[
            shape((2, tile_rows, tile_cols), F32),
            shape((2, tile_rows, w), F32),
            shape((2, w, tile_cols), F32),
            shape((2, w, w), F32),
            shape((2, w, w), F32),
            shape((2, slots), F32),
        ],
        scratch_shapes=[
            pltpu.VMEM((ext_cols // 128, 2, ext_rows, 128), F32),
            pltpu.VMEM((ext_cols // 128, 2, ext_rows, 128), F32),
            pltpu.VMEM((2, 2, w, 128), F32),
            pltpu.VMEM((2, w, w), F32),
            pltpu.VMEM((4, quart, w), F32),
            pltpu.VMEM((2, modes * w, 2 * w), BF),
            pltpu.VMEM((modes, 4, w, w), BF),
            pltpu.VMEM((2, modes * w, w), F32),
            pltpu.VMEM((modes, 4, half, w), F32),
            pltpu.VMEM((2, modes * w, w), F32),
            pltpu.SemaphoreType.DMA((2, 2)),
            pltpu.SemaphoreType.DMA((8,)),
        ],
        compiler_params=pltpu.CompilerParams(vmem_limit_bytes=60 << 20),
        cost_estimate=pl.CostEstimate(flops=10**11, bytes_accessed=10**7, transcendentals=0),
    )


MESH = pl.DeviceIdType.MESH


def place():
    return lax.axis_index("row"), lax.axis_index("col"), lax.axis_index("mode")


def device(r, c, m):
    return {"row": r, "col": c, "mode": m}


def remote(src, dst, send, recv, to):
    return pltpu.make_async_remote_copy(
        src_ref=src, dst_ref=dst, send_sem=send, recv_sem=recv, device_id=to, device_id_type=MESH
    )


def greet(to):
    pl.semaphore_signal(pltpu.get_barrier_semaphore(), inc=1, device_id=to, device_id_type=MESH)


class Quarters:
    def __init__(self, src, dst, modes, rows, r, c, chunks, sems, direct=False):
        me_r, me_c, m = place()
        self.m, self.modes, self.chunks, self.direct = m, modes, chunks, direct
        self.rows = rows // modes // chunks
        self.src, self.dst = src, dst
        self.ys, self.yr, self.zs, self.zr, self.ts, self.tr = sems
        self.peer = device(r, c, m)
        self.next = device(me_r, me_c, lax.rem(m + 1, modes))
        self.prev = device(me_r, me_c, lax.rem(m + modes - 1, modes))

    def part(self, ref, owner, i):
        at = pl.multiple_of((owner * self.chunks + i) * self.rows, self.rows)
        return ref.at[:, pl.ds(at, self.rows), :]

    def first(self, i):
        mine = self.part(self.src, self.m, i)
        return remote(mine, self.part(self.dst, self.m, i), self.ys.at[i], self.yr.at[i], self.peer)

    def ring(self, i, way):
        mine = self.part(self.dst, self.m, i)
        return remote(mine, mine, self.zs.at[way, i], self.zr.at[way, i], self.next if way == 0 else self.prev)

    def way(self, i):
        return 0 if i < self.chunks // 2 else 1

    def relay(self, i):
        back = self.modes - 1 if self.way(i) == 0 else 1
        block = self.part(self.dst, lax.rem(self.m + back, self.modes), i)
        return remote(block, block, self.ts.at[i], self.tr.at[i], self.next if self.way(i) == 0 else self.prev)

    def second(self, i):
        owner = lax.rem(self.m + self.modes // 2, self.modes)
        return remote(
            self.part(self.src, owner, i), self.part(self.dst, owner, i), self.ts.at[i], self.tr.at[i], self.peer
        )

    def start(self):
        for i in range(self.chunks):
            self.first(i).start()
        for i in range(self.chunks) if self.direct else ():
            self.second(i).start()

    def sent(self):
        for i in range(self.chunks):
            self.first(i).wait_send()
            if self.direct:
                self.second(i).wait_send()

    def take(self, some=None):
        for i in range(self.chunks) if some is None else some:
            self.first(i).wait_recv()
            self.ring(i, 0).start()
            self.ring(i, 1).start()

    def turn(self):
        for i in range(self.chunks):
            self.ring(i, self.way(i)).wait_recv()
            if not self.direct:
                self.relay(i).start()

    def finish(self):
        for i in range(self.chunks):
            self.ring(i, 1 - self.way(i)).wait_recv()
            if self.direct:
                self.second(i).wait_recv()
            else:
                self.relay(i).wait_recv()
        for i in range(self.chunks):
            self.ring(i, 0).wait_send()
            self.ring(i, 1).wait_send()
            if not self.direct:
                self.relay(i).wait_send()


STRIP, EDGE = 4, 2


def quarter_sems(chunks):
    one = pltpu.SemaphoreType.DMA((chunks,))
    two = pltpu.SemaphoreType.DMA((2, chunks))
    return [one, one, two, two, one, one]


def when(cond, *steps):
    @pl.when(cond)
    def _():
        for step in steps:
            step()


def make_spread(window, modes, tile_rows, tile_cols, rows_n, cols_n):
    w = window

    def kernel(tile, probe, right, low, diag, gathered, *sems):
        strip_sems, low_sems, diag_sems = sems[:6], sems[6:12], sems[12:18]
        one_s, one_r, p_s, p_r, x_s, x_r, own_sem = sems[18:]
        r, c, m = place()
        core = lax.rem(c, 2)
        other = c + 1 - 2 * core
        odd, even = core == 1, core == 0
        away = jnp.where(odd, jnp.minimum(c + 1, cols_n - 1), jnp.maximum(c - 1, 0))
        has_away = jnp.where(odd, c < cols_n - 1, c > 0)
        has_diag = has_away & jnp.where(odd, r == 0, r == 1)
        flip = rows_n - 1 - r

        for k in range(1, modes):
            greet(device(r, c, lax.rem(m + k, modes)))
        greet(device(r, other, m))
        greet(device(flip, c, m))
        when(has_away, lambda: greet(device(r, away, m)))
        when(has_diag, lambda: greet(device(flip, away, m)))
        pl.semaphore_wait(
            pltpu.get_barrier_semaphore(),
            modes + 1 + has_away.astype(jnp.int32) + has_diag.astype(jnp.int32),
        )

        strip = Quarters(tile, right, modes, tile_rows, r, away, STRIP, strip_sems)
        down = Quarters(tile, low, modes, w, flip, c, EDGE, low_sems)
        corner = Quarters(tile, diag, modes, w, flip, away, EDGE, diag_sems)
        whole = remote(tile, right, one_s.at[0], one_r.at[0], device(r, other, m))
        corner_on = remote(low, diag, one_s.at[1], one_r.at[1], device(r, other, m))

        def probe_of(k, part=None):
            parts = pl.ds(0, 2) if part is None else pl.ds(part, 1)
            return gathered.at[parts, pl.ds(lax.rem(m + modes - k, modes), 1)]

        def probe_copy(k):
            to = device(r, c, lax.rem(m + k, modes))
            return remote(probe, probe_of(0), p_s.at[k], p_r.at[k], to)

        def probe_relay(k):
            block = probe_of(k, 0 if k == 1 else 1)
            at = 0 if k == 1 else 2
            return remote(block, block, p_s.at[at], p_r.at[at], device(r, c, lax.rem(m + k, modes)))

        def probe_pass(k):
            return remote(probe_of(k), probe_of(k), x_s.at[k], x_r.at[k], device(r, other, m))

        def probe_start():
            for k in (1, modes - 1):
                probe_copy(k).start()

        def probe_turn():
            for k in (1, modes - 1):
                probe_copy(k).wait_recv()
                probe_relay(k).start()
                probe_pass(k).start()

        def probe_end():
            for k in (1, modes - 1):
                probe_relay(k).wait_recv()
            probe_pass(2).start()

        def probe_finish():
            for k in (1, modes - 1):
                probe_copy(k).wait_send()
                probe_relay(k).wait_send()
            for k in far:
                probe_pass(k).wait_send()

        def probe_take():
            for k in far:
                probe_pass(k).wait_recv()

        far = (1, modes - 1, 2)
        when(r == 1, down.start)
        when(even & has_diag, corner.start)
        when(even & has_away, strip.start)
        when(even, probe_start)
        when(odd, whole.start)
        keep = pltpu.make_async_copy(probe, gathered.at[:, pl.ds(m, 1)], own_sem)
        keep.start()

        when(r == 0, down.take)
        when(odd & has_diag, corner.take)
        when(odd & has_away, lambda: strip.take([0]))
        when(r == 0, down.turn)
        when(odd & has_diag, corner.turn)
        when(even, probe_turn)
        when(odd & has_away, lambda: strip.take([1, 2, 3]))
        when(r == 0, down.finish)
        when(odd & (r == 0), corner_on.start)
        when(odd & has_away, strip.turn)
        when(even, probe_end)
        when(odd & has_diag, corner.finish)
        when(odd & has_away, strip.finish)
        when(even, whole.wait_recv)
        when(even & (r == 0), corner_on.wait_recv)
        when(odd, probe_take)
        when(even, probe_finish)
        keep.wait()
        when(odd, whole.wait_send)
        when(odd & (r == 0), corner_on.wait_send)
        when(even & has_away, strip.sent)
        when(r == 1, down.sent)
        when(even & has_diag, corner.sent)

    hbm = pl.BlockSpec(memory_space=pl.ANY)
    shape = jax.ShapeDtypeStruct
    dma = pltpu.SemaphoreType.DMA
    return pl.pallas_call(
        kernel,
        name="spread",
        in_specs=[hbm, hbm],
        out_specs=[hbm] * 4,
        out_shape=[
            shape((2, tile_rows, tile_cols), F32),
            shape((2, w, tile_cols), F32),
            shape((2, w, tile_cols), F32),
            shape((2, modes, w, w), F32),
        ],
        scratch_shapes=quarter_sems(STRIP) + quarter_sems(EDGE) + quarter_sems(EDGE)
        + [dma((2,))] * 2 + [dma((modes,))] * 4 + [dma],
        compiler_params=pltpu.CompilerParams(collective_id=0, has_side_effects=True),
    )


def make_collect(window, modes, tile_rows, tile_cols, rows_n, cols_n):
    w = window
    chips = rows_n * cols_n // 2
    piece = 2 * w // chips

    def kernel(g_right, g_low, g_diag, pg, right, low, diag, total, *sems):
        strip_sems, low_sems, diag_sems = sems[:6], sems[6:12], sems[12:18]
        one_s, one_r, x_s, x_r, y_s, y_r, a_s, a_r, b_s, b_r, in_sem, pair, got, mine = sems[18:]
        r, c, m = place()
        core = lax.rem(c, 2)
        chip = r * (cols_n // 2) + c // 2
        other = c + 1 - 2 * core
        odd, even = core == 1, core == 0
        away = jnp.where(odd, jnp.minimum(c + 1, cols_n - 1), jnp.maximum(c - 1, 0))
        has_away = jnp.where(odd, c < cols_n - 1, c > 0)
        flip = rows_n - 1 - r
        over = jnp.where(r == 0, jnp.minimum(c + 1, cols_n - 1), jnp.maximum(c - 1, 0))
        has_over = jnp.where(r == 0, c < cols_n - 1, c > 0)

        def partner(k):
            p = lax.rem(chip + k, chips)
            return device(p // (cols_n // 2), 2 * lax.rem(p, cols_n // 2) + core, m)

        def hello(k, carry):
            greet(partner(k))
            return carry

        greet(device(r, other, m))
        for k in (1, modes - 1):
            greet(device(r, c, lax.rem(m + k, modes)))
        when(has_away, lambda: greet(device(r, away, m)))
        when(has_over, lambda: greet(device(flip, over, m)))
        when(even, lambda: greet(device(flip, c, m)))
        when(odd, lambda: lax.fori_loop(1, chips, hello, 0))
        pl.semaphore_wait(
            pltpu.get_barrier_semaphore(),
            3 + jnp.where(odd, chips - 1, 1) + has_away.astype(jnp.int32) + has_over.astype(jnp.int32),
        )

        strip = Quarters(g_right, right, modes, tile_rows, r, away, STRIP, strip_sems)
        down = Quarters(g_low, low, modes, w, flip, c, EDGE, low_sems)
        corner = Quarters(g_diag, diag, modes, w, flip, over, EDGE, diag_sems)
        whole = remote(g_right, right, one_s, one_r, device(r, other, m))
        swap = remote(pg, pair.at[0], x_s, x_r, device(r, other, m))
        own = pltpu.make_async_copy(pg, pair.at[1], in_sem)
        at_chip = pl.ds(pl.multiple_of(chip * piece, piece), piece)
        rest = got.at[pl.ds(1, chips - 1)]
        many = total.at[pl.ds(0, (chips - 1) * piece), :]
        keep = pltpu.make_async_copy(mine, total.at[at_chip, :], in_sem)
        give = remote(total, total, y_s, y_r, device(r, other, m))

        def scatter_go(k, carry):
            p = lax.rem(chip + k, chips)
            rows = pl.ds(pl.multiple_of(p * piece, piece), piece)
            remote(pair.at[1, rows, :], got.at[k], a_s, a_r, partner(k)).start()
            return carry

        def share_go(k, carry):
            remote(mine, total.at[at_chip, :], b_s, b_r, partner(k)).start()
            return carry

        def add(k, acc):
            return acc + got[k]

        def sum_pair():
            own.wait()
            swap.wait_recv()
            pair[1] = pair[0] + pair[1]
            lax.fori_loop(1, chips, scatter_go, 0)

        def sum_plane():
            pltpu.make_async_copy(rest, rest, a_r).wait()
            mine[...] = lax.fori_loop(1, chips, add, pair[1, at_chip, :]) * (1.0 / 16.0)
            keep.start()
            lax.fori_loop(1, chips, share_go, 0)

        def sum_give():
            keep.wait()
            pltpu.make_async_copy(many, many, b_r).wait()
            give.start()

        def sum_end():
            pltpu.make_async_copy(rest, rest, a_s).wait()
            pltpu.make_async_copy(many, many, b_s).wait()
            give.wait_send()

        when(even, swap.start)
        when(odd, own.start)
        when(odd & has_away, strip.start)
        when(r == 0, down.start)
        when((r == 0) & has_over, corner.start)
        when(even, whole.start)
        when(odd, sum_pair)
        when(even & has_away, strip.take)
        when(r == 1, down.take)
        when((r == 1) & has_over, corner.take)
        when(odd, sum_plane)
        when(even & has_away, strip.turn)
        when(r == 1, down.turn)
        when((r == 1) & has_over, corner.turn)
        when(odd, sum_give)
        when(even & has_away, strip.finish)
        when(r == 1, down.finish)
        when((r == 1) & has_over, corner.finish)
        when(odd, whole.wait_recv)
        when(even, give.wait_recv)
        when(even, swap.wait_send)
        when(odd, sum_end)
        when(odd & has_away, strip.sent)
        when(r == 0, down.sent)
        when((r == 0) & has_over, corner.sent)
        when(even, whole.wait_send)

    hbm = pl.BlockSpec(memory_space=pl.ANY)
    shape = jax.ShapeDtypeStruct
    dma = pltpu.SemaphoreType.DMA
    return pl.pallas_call(
        kernel,
        name="collect",
        in_specs=[hbm] * 4,
        out_specs=[hbm] * 4,
        out_shape=[
            shape((2, tile_rows, tile_cols), F32),
            shape((2, w, tile_cols), F32),
            shape((2, w, tile_cols), F32),
            shape((2 * w, w), F32),
        ],
        scratch_shapes=quarter_sems(STRIP) + quarter_sems(EDGE) + quarter_sems(EDGE) + [dma] * 11
        + [pltpu.VMEM((2, 2 * w, w), F32), pltpu.VMEM((chips, piece, w), F32), pltpu.VMEM((piece, w), F32)],
        compiler_params=pltpu.CompilerParams(collective_id=1, has_side_effects=True),
    )


def make_finish(window, tile_rows, tile_cols):
    w = window
    blocks = tile_rows // w

    def kernel(own, strip, low, diag, total, grad, probe, a, b, e, s_a, s_b, s_e, s_out):
        r, c, m = place()
        below, inner = r > 0, c > 0

        def rows(k):
            return pl.ds(k * w, w)

        loads = [
            [
                pltpu.make_async_copy(own.at[:, rows(k), :], a.at[:, rows(k), :], s_a.at[k]),
                pltpu.make_async_copy(strip.at[:, rows(k), :], b.at[:, rows(k), :], s_b.at[k]),
            ]
            for k in range(blocks)
        ]
        edges = [pltpu.make_async_copy(src, e.at[n], s_e.at[n]) for n, src in enumerate((low, diag, total))]
        for k in reversed(range(blocks)):
            for copy in loads[k]:
                copy.start()
        for copy in edges:
            copy.start()
        stores = [pltpu.make_async_copy(a.at[:, rows(k), :], grad.at[:, rows(k), :], s_out.at[k]) for k in range(blocks)]

        def add(k, x):
            for part in range(2):
                a[part, k * w:k * w + w, :] += x[part]

        for k in reversed(range(blocks)):
            for copy in loads[k]:
                copy.wait()
            when(inner, lambda: add(k, b.at[:, rows(k), :]))
            if k == 0:
                for copy in edges:
                    copy.wait()
                when(below, lambda: add(0, e.at[0]))
                when(below & inner, lambda: add(0, e.at[1]))
                last = pltpu.make_async_copy(e.at[2], probe, s_out.at[blocks])
                last.start()
            stores[k].start()
        for copy in stores + [last]:
            copy.wait()

    hbm = pl.BlockSpec(memory_space=pl.ANY)
    dma = pltpu.SemaphoreType.DMA
    tile = (2, tile_rows, tile_cols)
    return pl.pallas_call(
        kernel,
        name="finish",
        in_specs=[hbm] * 5,
        out_specs=[hbm] * 2,
        out_shape=[jax.ShapeDtypeStruct(tile, F32), jax.ShapeDtypeStruct((2, w, w), F32)],
        scratch_shapes=[
            pltpu.VMEM(tile, F32), pltpu.VMEM(tile, F32), pltpu.VMEM((3, 2, w, w), F32),
            dma((blocks,)), dma((blocks,)), dma((3,)), dma((blocks + 1,)),
        ],
        compiler_params=pltpu.CompilerParams(vmem_limit_bytes=60 << 20),
    )


def per_device(object_slab, probe_modes, amplitudes, scan_counts, scan_positions):
    window = probe_modes.shape[-1]
    tile_rows, tile_cols = object_slab.shape[1:]
    slots = amplitudes.shape[0]
    modes, cols_n, rows_n = (lax.axis_size(a) for a in ("mode", "col", "row"))
    sizes = (window, modes, tile_rows, tile_cols, rows_n, cols_n)
    right, low, diag, probe = make_spread(*sizes)(object_slab, probe_modes)
    consts = [jnp.asarray(t) for t in tables(window)]
    compute = make_compute(window, modes, slots, tile_rows, tile_cols, cols_n)
    g_own, g_right, g_low, g_diag, pg, shift = compute(
        scan_positions, scan_counts, object_slab, right, low, diag, probe, amplitudes, *consts
    )
    from_left, from_up, from_diag, total = make_collect(*sizes)(
        g_right, g_low, g_diag, pg.reshape(2 * window, window)
    )
    grad, probe_grad = make_finish(window, tile_rows, tile_cols)(
        g_own, from_left, from_up, from_diag, total.reshape(2, window, window)
    )
    return (grad, probe_grad.reshape(2, 1, window, window), shift)


def solution(mesh):
    in_specs = (
        P(None, "row", "col"),
        P(None, "mode", None, None),
        P(("row", "col"), None, None),
        P(),
        P(None, ("row", "col")),
    )
    out_specs = (P(None, "row", "col"), P(None, "mode", None, None), P(None, ("row", "col")))
    return jax.shard_map(
        per_device, mesh=mesh, in_specs=in_specs, out_specs=out_specs, check_vma=False
    )
```

```python
import math
import functools
import numpy as np
import jax
import jax.numpy as jnp
from jax import lax
from jax.experimental import pallas as pl
from jax.experimental.pallas import tpu as pltpu
from jax.sharding import PartitionSpec as P

BF = jnp.bfloat16
F32 = jnp.float32
BATCH = 4
CH = 32


def hi_lo(x):
    hi = x.astype(BF)
    lo = (x - hi.astype(F32)).astype(BF)
    return hi, lo


def halves(table):
    table = table.astype(np.float32)
    hi = table.astype(BF)
    return hi, (table - hi.astype(np.float32)).astype(BF)


def angles(window, radix, q):
    part = window // radix
    n, j = np.arange(part)[:, None], np.arange(part)[None, :]
    angle = 2.0 * math.pi * ((n * (radix * j + q)) % window) / window
    return np.cos(angle) / math.sqrt(window), np.sin(angle) / math.sqrt(window)


def tables(window):
    right_f, right_i, left_f, left_i = [], [], [], []
    for q in range(2):
        c, s = angles(window, 2, q)
        for table, into in ((np.block([[c, -s], [s, c]]), right_f), (np.block([[c.T, s.T], [-s.T, c.T]]), right_i)):
            hi, lo = halves(table)
            into.append(np.concatenate([hi, lo, hi], axis=0))
    for q in range(4):
        c, s = angles(window, 4, q)
        for table, into in ((np.block([[c.T, s.T], [-s.T, c.T]]), left_f), (np.block([[c, -s], [s, c]]), left_i)):
            hi, lo = halves(table)
            top = np.concatenate([hi, hi], axis=1)
            into.append(np.concatenate([top, np.concatenate([lo, np.zeros_like(lo)], axis=1)], axis=0))
    order = np.concatenate([np.arange(0, window, 2), np.arange(1, window, 2)])
    shuffle = np.zeros((window, window), np.float32)
    shuffle[order, np.arange(window)] = 1.0
    return np.stack(right_f), np.stack(right_i), np.stack(left_f), np.stack(left_i), shuffle.astype(BF)


def cat(parts, axis):
    return jnp.concatenate(parts, axis=axis)


def mm(a, b):
    return jnp.dot(a, b, preferred_element_type=F32)


def make_compute(window, modes, slots, tile_rows, tile_cols, cols_n):
    w, half, quart = window, window // 2, window // 4
    ch = CH
    ext_rows, ext_cols = tile_rows + w, tile_cols + w

    def kernel(positions, counts, own, right, low, diag, probe, amps, rf, ri, lf, li, shuffle,
               g_own, g_right, g_low, g_diag, pg, along,
               ext, grad, amp_buf, win, fac, lhs, rhs, mid, far, near, amp_sem, sem):
        row_id, col_id, mine = place()
        count = counts[row_id * cols_n + col_id]
        def quarters(whole, parts):
            pairs = []
            for k in range(4):
                for t in range(2):
                    down = slice(tile_rows, ext_rows) if k >= 2 else slice(0, tile_rows)
                    pairs.append((whole.at[2 * (k % 2) + t, :, down, :], parts[k].at[:, :, 128 * t:128 * t + 128]))
            return pairs

        loads = [
            pltpu.make_async_copy(part, inside, sem.at[k])
            for k, (inside, part) in enumerate(quarters(ext, (own, right, low, diag)))
        ]
        for copy in loads:
            copy.start()

        def amp_copies(slot, place):
            return [
                pltpu.make_async_copy(
                    amps.at[slot, :, 128 * t:128 * t + 128], amp_buf.at[place, t], amp_sem.at[place, t]
                )
                for t in range(2)
            ]

        for copy in amp_copies(0, 0):
            copy.start()

        def clear(i, carry):
            at = pl.multiple_of(i * ch, ch)
            for c in range(2):
                for t in range(4):
                    grad[t, c, pl.ds(at, ch), :] = jnp.zeros((ch, 128), F32)
            return carry

        lax.fori_loop(0, ext_rows // ch, clear, 0)
        pg[...] = jnp.zeros(pg.shape, F32)

        def no_shift(i, carry):
            along[0, i] = 0.0
            along[1, i] = 0.0
            return carry

        lax.fori_loop(0, slots, no_shift, 0)
        for copy in loads:
            copy.wait()

        def put_lhs(parity, at, x):
            hi, lo = hi_lo(x)
            lhs[parity, at:at + ch, :w] = hi
            lhs[parity, at:at + ch, w:] = lo

        def put_rhs(m, q, at, x):
            hi, lo = hi_lo(x)
            rhs[m, q, at:at + ch, :] = hi
            rhs[m, q, half + at:half + at + ch, :] = lo

        def right_apply(m, table, into):
            rows = slice(m * w, (m + BATCH) * w)
            for parity in range(2):
                hi, lo = lhs[parity, rows, :w], lhs[parity, rows, w:]
                into[parity, rows, :] = mm(cat([hi, hi, lo], 1), table[parity])

        def left_apply(m, q, table):
            both = mm(table[q], rhs[m, q])
            return both[:half] + both[half:]

        def forward_rows(m):
            for r in range(0, quart, ch):
                y = [[], [], [], []]
                for parity in range(2):
                    x = [mid[parity, m * w + p * quart + r:m * w + p * quart + r + ch, :] for p in range(4)]
                    a, b, c, d = x[0] + x[2], x[1] + x[3], x[0] - x[2], x[1] - x[3]
                    y[0].append(a + b)
                    y[2].append(a - b)
                    turned = cat([d[:, half:], -d[:, :half]], 1)
                    y[1].append(c + turned)
                    y[3].append(c - turned)
                for q in range(4):
                    e, o = y[q]
                    put_rhs(m, q, r, cat([e[:, :half], o[:, :half]], 1))
                    put_rhs(m, q, quart + r, cat([e[:, half:], o[:, half:]], 1))
            for q in range(4):
                far[m, q] = left_apply(m, q, lf)

        def inverse_rows(m):
            for q in range(4):
                for r in range(0, quart, ch):
                    f = fac[q, r:r + ch, :]
                    for at in (r, quart + r):
                        put_rhs(m, q, at, f * far[m, q, at:at + ch, :])
            for q in range(4):
                far[m, q] = left_apply(m, q, li)
            for r in range(0, quart, ch):
                re = [far[m, q, r:r + ch, :] for q in range(4)]
                im = [far[m, q, quart + r:quart + r + ch, :] for q in range(4)]
                are, aim, bre, bim = re[0] + re[2], im[0] + im[2], re[1] + re[3], im[1] + im[3]
                cre, cim, dre, dim = re[0] - re[2], im[0] - im[2], re[1] - re[3], im[1] - im[3]
                outs = (
                    (are + bre, aim + bim), (cre - dim, cim + dre),
                    (are - bre, aim - bim), (cre + dim, cim - dre),
                )
                for p, (xre, xim) in enumerate(outs):
                    for parity in range(2):
                        cols = slice(parity * half, parity * half + half)
                        put_lhs(parity, m * w + p * quart + r, cat([xre[:, cols], xim[:, cols]], 1))

        def do_slot(slot, carry):
            row = positions[0, slot] - row_id * tile_rows
            col = positions[1, slot] - col_id * tile_cols
            tile_at = col // 128
            off = lax.rem(col, 128)
            back = lax.rem(w + 128 - off, w + 128)
            place_at = lax.rem(slot, 2)
            for copy in amp_copies(slot, place_at):
                copy.wait()

            @pl.when(slot + 1 < count)
            def _():
                for copy in amp_copies(slot + 1, 1 - place_at):
                    copy.start()

            for c in range(2):
                for r in range(0, w, ch):
                    wide = cat([ext[tile_at + t, c, pl.ds(row + r, ch), :] for t in range(3)], 1)
                    win[c, r:r + ch, :] = pltpu.roll(wide, back, 1)[:, :w]

            for q in range(4):
                a = cat([amp_buf[place_at, t, pl.ds(q, quart, stride=4), :] for t in range(2)], 1)
                a0, a1 = hi_lo(a)
                a2 = (a - a0.astype(F32) - a1.astype(F32)).astype(BF)
                stack = mm(cat([a0, a1, a2], 0), shuffle[...])
                fac[q] = stack[:quart] + stack[quart:2 * quart] + stack[2 * quart:]

            for m in range(modes):
                for r in range(0, w, ch):
                    vre, vim = win[0, r:r + ch, :], win[1, r:r + ch, :]
                    pre, pim = probe[0, m, r:r + ch, :], probe[1, m, r:r + ch, :]
                    are = pre * vre - pim * vim
                    aim = pre * vim + pim * vre
                    for parity in range(2):
                        if parity == 0:
                            x = cat([are[:, :half] + are[:, half:], aim[:, :half] + aim[:, half:]], 1)
                        else:
                            x = cat([are[:, :half] - are[:, half:], aim[:, :half] - aim[:, half:]], 1)
                        put_lhs(parity, m * w + r, x)
                if (m + 1) % BATCH == 0:
                    right_apply(m + 1 - BATCH, rf, mid)
                    for n in range(m + 1 - BATCH, m + 1):
                        forward_rows(n)

            for q in range(4):
                for r in range(0, quart, ch):
                    total = None
                    for m in range(modes):
                        re = far[m, q, r:r + ch, :]
                        im = far[m, q, quart + r:quart + r + ch, :]
                        term = re * re + im * im
                        total = term if total is None else total + term
                    fac[q, r:r + ch, :] = 0.25 * (1.0 - fac[q, r:r + ch, :] * lax.rsqrt(total + 0.5))

            for m in range(modes):
                inverse_rows(m)
                if (m + 1) % BATCH == 0:
                    right_apply(m + 1 - BATCH, ri, near)

            rows_sum = jnp.zeros((8, w), F32)
            cols_sum = jnp.zeros((8, w), F32)
            lanes = lax.broadcasted_iota(jnp.int32, (ch, w), 1)
            inner = (lanes >= 1) & (lanes <= w - 2)

            def near_of(m, r):
                at = m * w + r
                if not isinstance(m, int):
                    at = pl.multiple_of(at, ch)
                e, o = near[0, pl.ds(at, ch), :], near[1, pl.ds(at, ch), :]
                s, d = e + o, e - o
                return cat([s[:, :half], d[:, :half]], 1), cat([s[:, half:], d[:, half:]], 1)

            for r in range(0, w, ch):
                gre = gim = None
                for m in range(modes):
                    nre, nim = near_of(m, r)
                    pre, pim = probe[0, m, r:r + ch, :], probe[1, m, r:r + ch, :]
                    tre = pre * nre + pim * nim
                    tim = pre * nim - pim * nre
                    gre = tre if gre is None else gre + tre
                    gim = tim if gim is None else gim + tim
                for c, g in ((0, gre), (1, gim)):
                    spread = pltpu.roll(cat([g, jnp.zeros((ch, 128), F32)], 1), off, 1)
                    for t in range(3):
                        grad[tile_at + t, c, pl.ds(row + r, ch), :] += spread[:, 128 * t:128 * t + 128]
                vre, vim = win[0, r:r + ch, :], win[1, r:r + ch, :]
                nre, nim = near_of(mine, r)
                pg[0, r:r + ch, :] += vre * nre + vim * nim
                pg[1, r:r + ch, :] += vre * nim - vim * nre
                dre = pltpu.roll(vre, w - 1, 1) - pltpu.roll(vre, 1, 1)
                dim = pltpu.roll(vim, w - 1, 1) - pltpu.roll(vim, 1, 1)
                t = jnp.where(inner, gre * dre + gim * dim, 0.0)
                cols_sum = cols_sum + jnp.sum(t.reshape(ch // 8, 8, w), axis=0)
                lo_r, hi_r = max(r, 1), min(r + ch, w - 1)
                up = [ext_rows_slice(win, c, r + 1, ch, w) for c in range(2)]
                dn = [ext_rows_slice(win, c, r - 1, ch, w) for c in range(2)]
                t = gre * (up[0] - dn[0]) + gim * (up[1] - dn[1])
                if lo_r != r or hi_r != r + ch:
                    idx = lax.broadcasted_iota(jnp.int32, (ch, w), 0) + r
                    t = jnp.where((idx >= lo_r) & (idx < hi_r), t, 0.0)
                rows_sum = rows_sum + jnp.sum(t.reshape(ch // 8, 8, w), axis=0)
            along[0, slot] = jnp.sum(rows_sum) * (0.5 / w)
            along[1, slot] = jnp.sum(cols_sum) * (0.5 / w)
            return carry

        def ext_rows_slice(ref, c, start, size, width):
            if start < 0:
                return cat([ref[c, 0:1, :], ref[c, 0:size - 1, :]], 0)
            if start + size > w:
                return cat([ref[c, start:w, :], ref[c, w - 1:w, :]], 0)
            return ref[c, start:start + size, :]

        lax.fori_loop(0, count, do_slot, 0)
        stores = [
            pltpu.make_async_copy(inside, part, sem.at[k])
            for k, (inside, part) in enumerate(quarters(grad, (g_own, g_right, g_low, g_diag)))
        ]
        for copy in stores:
            copy.start()
        for copy in stores:
            copy.wait()

    hbm = pl.BlockSpec(memory_space=pl.ANY)
    vmem = pl.BlockSpec(memory_space=pltpu.VMEM)
    smem = pl.BlockSpec(memory_space=pltpu.SMEM)
    shape = jax.ShapeDtypeStruct
    return pl.pallas_call(
        kernel,
        name="slots",
        in_specs=[smem, smem, hbm, hbm, hbm, hbm, vmem, hbm, vmem, vmem, vmem, vmem, vmem],
        out_specs=[hbm, hbm, hbm, hbm, vmem, smem],
        out_shape=[
            shape((2, tile_rows, tile_cols), F32),
            shape((2, tile_rows, w), F32),
            shape((2, w, tile_cols), F32),
            shape((2, w, w), F32),
            shape((2, w, w), F32),
            shape((2, slots), F32),
        ],
        scratch_shapes=[
            pltpu.VMEM((ext_cols // 128, 2, ext_rows, 128), F32),
            pltpu.VMEM((ext_cols // 128, 2, ext_rows, 128), F32),
            pltpu.VMEM((2, 2, w, 128), F32),
            pltpu.VMEM((2, w, w), F32),
            pltpu.VMEM((4, quart, w), F32),
            pltpu.VMEM((2, modes * w, 2 * w), BF),
            pltpu.VMEM((modes, 4, w, w), BF),
            pltpu.VMEM((2, modes * w, w), F32),
            pltpu.VMEM((modes, 4, half, w), F32),
            pltpu.VMEM((2, modes * w, w), F32),
            pltpu.SemaphoreType.DMA((2, 2)),
            pltpu.SemaphoreType.DMA((8,)),
        ],
        compiler_params=pltpu.CompilerParams(vmem_limit_bytes=60 << 20),
        cost_estimate=pl.CostEstimate(flops=10**11, bytes_accessed=10**7, transcendentals=0),
    )


MESH = pl.DeviceIdType.MESH


def place():
    return lax.axis_index("row"), lax.axis_index("col"), lax.axis_index("mode")


def device(r, c, m):
    return {"row": r, "col": c, "mode": m}


def remote(src, dst, send, recv, to):
    return pltpu.make_async_remote_copy(
        src_ref=src, dst_ref=dst, send_sem=send, recv_sem=recv, device_id=to, device_id_type=MESH
    )


def greet(to):
    pl.semaphore_signal(pltpu.get_barrier_semaphore(), inc=1, device_id=to, device_id_type=MESH)


class Quarters:
    def __init__(self, src, dst, modes, rows, r, c, chunks, sems, held=False):
        me_r, me_c, m = place()
        self.m, self.modes, self.chunks, self.held = m, modes, chunks, held
        self.rows = rows // modes // chunks
        self.src, self.dst = src, dst
        self.ys, self.yr, self.zs, self.zr, self.ts, self.tr = sems
        self.peer = device(r, c, m)
        self.next = device(me_r, me_c, lax.rem(m + 1, modes))
        self.prev = device(me_r, me_c, lax.rem(m + modes - 1, modes))

    def part(self, ref, owner, i):
        at = pl.multiple_of((owner * self.chunks + i) * self.rows, self.rows)
        return ref.at[:, pl.ds(at, self.rows), :]

    def first(self, i):
        mine = self.part(self.src, 0 if self.held else self.m, i)
        return remote(mine, self.part(self.dst, self.m, i), self.ys.at[i], self.yr.at[i], self.peer)

    def ring(self, i, way):
        mine = self.part(self.dst, self.m, i)
        return remote(mine, mine, self.zs.at[way, i], self.zr.at[way, i], self.next if way == 0 else self.prev)

    def way(self, i):
        return 0 if i < self.chunks // 2 else 1

    def relay(self, i):
        back = self.modes - 1 if self.way(i) == 0 else 1
        block = self.part(self.dst, lax.rem(self.m + back, self.modes), i)
        return remote(block, block, self.ts.at[i], self.tr.at[i], self.next if self.way(i) == 0 else self.prev)

    def start(self):
        for i in range(self.chunks):
            self.first(i).start()

    def sent(self):
        for i in range(self.chunks):
            self.first(i).wait_send()

    def take(self, some=None):
        for i in range(self.chunks) if some is None else some:
            self.first(i).wait_recv()
            self.ring(i, 0).start()
            self.ring(i, 1).start()

    def turn(self):
        for i in range(self.chunks):
            self.ring(i, self.way(i)).wait_recv()
            self.relay(i).start()

    def finish(self):
        for i in range(self.chunks):
            self.ring(i, 1 - self.way(i)).wait_recv()
            self.relay(i).wait_recv()
        for i in range(self.chunks):
            self.ring(i, 0).wait_send()
            self.ring(i, 1).wait_send()
            self.relay(i).wait_send()


STRIP, EDGE = 4, 2


def quarter_sems(chunks):
    one = pltpu.SemaphoreType.DMA((chunks,))
    two = pltpu.SemaphoreType.DMA((2, chunks))
    return [one, one, two, two, one, one]


def when(cond, *steps):
    @pl.when(cond)
    def _():
        for step in steps:
            step()


def make_spread(window, modes, tile_rows, tile_cols, rows_n, cols_n):
    w = window

    def kernel(tile, probe, right, low, diag, gathered, *sems):
        strip_sems, low_sems, diag_sems = sems[:6], sems[6:12], sems[12:18]
        one_s, one_r, p_s, p_r, x_s, x_r, h_s, h_r, own_sem, held = sems[18:]
        r, c, m = place()
        core = lax.rem(c, 2)
        other = c + 1 - 2 * core
        odd, even = core == 1, core == 0
        away = jnp.where(odd, jnp.minimum(c + 1, cols_n - 1), jnp.maximum(c - 1, 0))
        has_away = jnp.where(odd, c < cols_n - 1, c > 0)
        flip = rows_n - 1 - r

        for k in range(1, modes):
            greet(device(r, c, lax.rem(m + k, modes)))
        greet(device(r, other, m))
        greet(device(flip, c, m))
        when(has_away, lambda: greet(device(r, away, m)))
        pl.semaphore_wait(pltpu.get_barrier_semaphore(), modes + 1 + has_away.astype(jnp.int32))

        strip = Quarters(tile, right, modes, tile_rows, r, away, STRIP, strip_sems)
        down = Quarters(tile, low, modes, w, flip, c, EDGE, low_sems)
        corner = Quarters(held, diag, modes, w, flip, c, EDGE, diag_sems, True)
        top = tile.at[:, pl.ds(pl.multiple_of(m * (w // modes), w // modes), w // modes), :]
        hop = remote(top, held, h_s, h_r, device(r, away, m))
        whole = remote(tile, right, one_s.at[0], one_r.at[0], device(r, other, m))
        corner_on = remote(low, diag, one_s.at[1], one_r.at[1], device(r, other, m))

        def probe_of(k, part=None):
            parts = pl.ds(0, 2) if part is None else pl.ds(part, 1)
            return gathered.at[parts, pl.ds(lax.rem(m + modes - k, modes), 1)]

        def probe_copy(k):
            to = device(r, c, lax.rem(m + k, modes))
            return remote(probe, probe_of(0), p_s.at[k], p_r.at[k], to)

        def probe_relay(k):
            block = probe_of(k, 0 if k == 1 else 1)
            at = 0 if k == 1 else 2
            return remote(block, block, p_s.at[at], p_r.at[at], device(r, c, lax.rem(m + k, modes)))

        def probe_pass(k):
            return remote(probe_of(k), probe_of(k), x_s.at[k], x_r.at[k], device(r, other, m))

        def probe_start():
            for k in (1, modes - 1):
                probe_copy(k).start()

        def probe_turn():
            for k in (1, modes - 1):
                probe_copy(k).wait_recv()
                probe_relay(k).start()
                probe_pass(k).start()

        def probe_end():
            for k in (1, modes - 1):
                probe_relay(k).wait_recv()
            probe_pass(2).start()

        def probe_finish():
            for k in (1, modes - 1):
                probe_copy(k).wait_send()
                probe_relay(k).wait_send()
            for k in far:
                probe_pass(k).wait_send()

        def probe_take():
            for k in far:
                probe_pass(k).wait_recv()

        far = (1, modes - 1, 2)
        when((r == 1) & even & has_away, hop.start)
        when(r == 1, down.start)
        when(even & has_away, strip.start)
        when(even, probe_start)
        when(odd, whole.start)
        keep = pltpu.make_async_copy(probe, gathered.at[:, pl.ds(m, 1)], own_sem)
        keep.start()

        when((r == 1) & odd & has_away, hop.wait_recv, corner.start)
        when(r == 0, down.take)
        when((r == 0) & odd & has_away, corner.take)
        when(odd & has_away, lambda: strip.take([0]))
        when(r == 0, down.turn)
        when((r == 0) & odd & has_away, corner.turn)
        when(even, probe_turn)
        when(odd & has_away, lambda: strip.take([1, 2, 3]))
        when(r == 0, down.finish)
        when(odd & (r == 0), corner_on.start)
        when(odd & has_away, strip.turn)
        when(even, probe_end)
        when((r == 0) & odd & has_away, corner.finish)
        when(odd & has_away, strip.finish)
        when(even, whole.wait_recv)
        when(even & (r == 0), corner_on.wait_recv)
        when(odd, probe_take)
        when(even, probe_finish)
        keep.wait()
        when(odd, whole.wait_send)
        when(odd & (r == 0), corner_on.wait_send)
        when(even & has_away, strip.sent)
        when(r == 1, down.sent)
        when((r == 1) & even & has_away, hop.wait_send)
        when((r == 1) & odd & has_away, corner.sent)

    hbm = pl.BlockSpec(memory_space=pl.ANY)
    shape = jax.ShapeDtypeStruct
    dma = pltpu.SemaphoreType.DMA
    return pl.pallas_call(
        kernel,
        name="spread",
        in_specs=[hbm, hbm],
        out_specs=[hbm] * 4,
        out_shape=[
            shape((2, tile_rows, tile_cols), F32),
            shape((2, w, tile_cols), F32),
            shape((2, w, tile_cols), F32),
            shape((2, modes, w, w), F32),
        ],
        scratch_shapes=quarter_sems(STRIP) + quarter_sems(EDGE) + quarter_sems(EDGE)
        + [dma((2,))] * 2 + [dma((modes,))] * 4 + [dma] * 3
        + [pltpu.VMEM((2, w // modes, tile_cols), F32)],
        compiler_params=pltpu.CompilerParams(collective_id=0, has_side_effects=True),
    )


def make_collect(window, modes, tile_rows, tile_cols, rows_n, cols_n):
    w = window
    chips = rows_n * cols_n // 2
    piece = 2 * w // chips

    def kernel(g_right, g_low, g_diag, pg, right, low, diag, total, *sems):
        strip_sems, low_sems, diag_sems = sems[:6], sems[6:12], sems[12:18]
        one_s, one_r, x_s, x_r, y_s, y_r, a_s, a_r, b_s, b_r, h_s, h_r, in_sem, pair, got, mine, held = sems[18:]
        r, c, m = place()
        core = lax.rem(c, 2)
        chip = r * (cols_n // 2) + c // 2
        other = c + 1 - 2 * core
        odd, even = core == 1, core == 0
        away = jnp.where(odd, jnp.minimum(c + 1, cols_n - 1), jnp.maximum(c - 1, 0))
        has_away = jnp.where(odd, c < cols_n - 1, c > 0)
        flip = rows_n - 1 - r

        def partner(k):
            p = lax.rem(chip + k, chips)
            return device(p // (cols_n // 2), 2 * lax.rem(p, cols_n // 2) + core, m)

        def hello(k, carry):
            greet(partner(k))
            return carry

        greet(device(r, other, m))
        for k in (1, modes - 1):
            greet(device(r, c, lax.rem(m + k, modes)))
        when(has_away, lambda: greet(device(r, away, m)))
        when(even, lambda: greet(device(flip, c, m)))
        when(odd, lambda: lax.fori_loop(1, chips, hello, 0))
        pl.semaphore_wait(
            pltpu.get_barrier_semaphore(),
            3 + jnp.where(odd, chips - 1, 1) + has_away.astype(jnp.int32),
        )

        strip = Quarters(g_right, right, modes, tile_rows, r, away, STRIP, strip_sems)
        down = Quarters(g_low, low, modes, w, flip, c, EDGE, low_sems)
        corner = Quarters(held, diag, modes, w, flip, c, EDGE, diag_sems, True)
        top = g_diag.at[:, pl.ds(pl.multiple_of(m * (w // modes), w // modes), w // modes), :]
        hop = remote(top, held, h_s, h_r, device(r, jnp.minimum(c + 1, cols_n - 1), m))
        whole = remote(g_right, right, one_s, one_r, device(r, other, m))
        swap = remote(pg, pair.at[0], x_s, x_r, device(r, other, m))
        own = pltpu.make_async_copy(pg, pair.at[1], in_sem)
        at_chip = pl.ds(pl.multiple_of(chip * piece, piece), piece)
        rest = got.at[pl.ds(1, chips - 1)]
        many = total.at[pl.ds(0, (chips - 1) * piece), :]
        keep = pltpu.make_async_copy(mine, total.at[at_chip, :], in_sem)
        give = remote(total, total, y_s, y_r, device(r, other, m))

        def scatter_go(k, carry):
            p = lax.rem(chip + k, chips)
            rows = pl.ds(pl.multiple_of(p * piece, piece), piece)
            remote(pair.at[1, rows, :], got.at[k], a_s, a_r, partner(k)).start()
            return carry

        def share_go(k, carry):
            remote(mine, total.at[at_chip, :], b_s, b_r, partner(k)).start()
            return carry

        def add(k, acc):
            return acc + got[k]

        def sum_pair():
            own.wait()
            swap.wait_recv()
            pair[1] = pair[0] + pair[1]
            lax.fori_loop(1, chips, scatter_go, 0)

        def sum_plane():
            pltpu.make_async_copy(rest, rest, a_r).wait()
            mine[...] = lax.fori_loop(1, chips, add, pair[1, at_chip, :]) * (1.0 / 16.0)
            keep.start()
            lax.fori_loop(1, chips, share_go, 0)

        def sum_give():
            keep.wait()
            pltpu.make_async_copy(many, many, b_r).wait()
            give.start()

        def sum_end():
            pltpu.make_async_copy(rest, rest, a_s).wait()
            pltpu.make_async_copy(many, many, b_s).wait()
            give.wait_send()

        when(even, swap.start)
        when(odd, own.start)
        when((r == 0) & (c < cols_n - 1), hop.start)
        when(r == 0, down.start)
        when((r == 0) & (c > 0), hop.wait_recv, corner.start)
        when(odd & has_away, strip.start)
        when(even, whole.start)
        when(odd, sum_pair)
        when(r == 1, down.take)
        when((r == 1) & (c > 0), corner.take)
        when(even & has_away, lambda: strip.take([0]))
        when(r == 1, down.turn)
        when((r == 1) & (c > 0), corner.turn)
        when(odd, sum_plane)
        when(even & has_away, lambda: strip.take([1, 2, 3]))
        when(even & has_away, strip.turn)
        when(odd, sum_give)
        when(even & has_away, strip.finish)
        when(r == 1, down.finish)
        when((r == 1) & (c > 0), corner.finish)
        when(odd, whole.wait_recv)
        when(even, give.wait_recv)
        when(even, swap.wait_send)
        when(odd, sum_end)
        when(odd & has_away, strip.sent)
        when(r == 0, down.sent)
        when((r == 0) & (c < cols_n - 1), hop.wait_send)
        when((r == 0) & (c > 0), corner.sent)
        when(even, whole.wait_send)

    hbm = pl.BlockSpec(memory_space=pl.ANY)
    shape = jax.ShapeDtypeStruct
    dma = pltpu.SemaphoreType.DMA
    return pl.pallas_call(
        kernel,
        name="collect",
        in_specs=[hbm] * 4,
        out_specs=[hbm] * 4,
        out_shape=[
            shape((2, tile_rows, tile_cols), F32),
            shape((2, w, tile_cols), F32),
            shape((2, w, tile_cols), F32),
            shape((2 * w, w), F32),
        ],
        scratch_shapes=quarter_sems(STRIP) + quarter_sems(EDGE) + quarter_sems(EDGE) + [dma] * 13
        + [pltpu.VMEM((2, 2 * w, w), F32), pltpu.VMEM((chips, piece, w), F32), pltpu.VMEM((piece, w), F32), pltpu.VMEM((2, w // modes, w), F32)],
        compiler_params=pltpu.CompilerParams(collective_id=1, has_side_effects=True),
    )


def make_finish(window, tile_rows, tile_cols):
    w = window
    blocks = tile_rows // w

    def kernel(own, strip, low, diag, total, grad, probe, a, b, e, s_a, s_b, s_e, s_out):
        r, c, m = place()
        below, inner = r > 0, c > 0

        def rows(k):
            return pl.ds(k * w, w)

        loads = [
            [
                pltpu.make_async_copy(own.at[:, rows(k), :], a.at[:, rows(k), :], s_a.at[k]),
                pltpu.make_async_copy(strip.at[:, rows(k), :], b.at[:, rows(k), :], s_b.at[k]),
            ]
            for k in range(blocks)
        ]
        edges = [pltpu.make_async_copy(src, e.at[n], s_e.at[n]) for n, src in enumerate((low, diag, total))]
        for k in reversed(range(blocks)):
            for copy in loads[k]:
                copy.start()
        for copy in edges:
            copy.start()
        stores = [pltpu.make_async_copy(a.at[:, rows(k), :], grad.at[:, rows(k), :], s_out.at[k]) for k in range(blocks)]

        def add(k, x):
            for part in range(2):
                a[part, k * w:k * w + w, :] += x[part]

        for k in reversed(range(blocks)):
            for copy in loads[k]:
                copy.wait()
            when(inner, lambda: add(k, b.at[:, rows(k), :]))
            if k == 0:
                for copy in edges:
                    copy.wait()
                when(below, lambda: add(0, e.at[0]))
                when(below & inner, lambda: add(0, e.at[1]))
                last = pltpu.make_async_copy(e.at[2], probe, s_out.at[blocks])
                last.start()
            stores[k].start()
        for copy in stores + [last]:
            copy.wait()

    hbm = pl.BlockSpec(memory_space=pl.ANY)
    dma = pltpu.SemaphoreType.DMA
    tile = (2, tile_rows, tile_cols)
    return pl.pallas_call(
        kernel,
        name="finish",
        in_specs=[hbm] * 5,
        out_specs=[hbm] * 2,
        out_shape=[jax.ShapeDtypeStruct(tile, F32), jax.ShapeDtypeStruct((2, w, w), F32)],
        scratch_shapes=[
            pltpu.VMEM(tile, F32), pltpu.VMEM(tile, F32), pltpu.VMEM((3, 2, w, w), F32),
            dma((blocks,)), dma((blocks,)), dma((3,)), dma((blocks + 1,)),
        ],
        compiler_params=pltpu.CompilerParams(vmem_limit_bytes=60 << 20),
    )


def per_device(object_slab, probe_modes, amplitudes, scan_counts, scan_positions):
    window = probe_modes.shape[-1]
    tile_rows, tile_cols = object_slab.shape[1:]
    slots = amplitudes.shape[0]
    modes, cols_n, rows_n = (lax.axis_size(a) for a in ("mode", "col", "row"))
    sizes = (window, modes, tile_rows, tile_cols, rows_n, cols_n)
    right, low, diag, probe = make_spread(*sizes)(object_slab, probe_modes)
    consts = [jnp.asarray(t) for t in tables(window)]
    compute = make_compute(window, modes, slots, tile_rows, tile_cols, cols_n)
    g_own, g_right, g_low, g_diag, pg, shift = compute(
        scan_positions, scan_counts, object_slab, right, low, diag, probe, amplitudes, *consts
    )
    from_left, from_up, from_diag, total = make_collect(*sizes)(
        g_right, g_low, g_diag, pg.reshape(2 * window, window)
    )
    grad, probe_grad = make_finish(window, tile_rows, tile_cols)(
        g_own, from_left, from_up, from_diag, total.reshape(2, window, window)
    )
    return (grad, probe_grad.reshape(2, 1, window, window), shift)


def solution(mesh):
    in_specs = (
        P(None, "row", "col"),
        P(None, "mode", None, None),
        P(("row", "col"), None, None),
        P(),
        P(None, ("row", "col")),
    )
    out_specs = (P(None, "row", "col"), P(None, "mode", None, None), P(None, ("row", "col")))
    return jax.shard_map(
        per_device, mesh=mesh, in_specs=in_specs, out_specs=out_specs, check_vma=False
    )
```

```python
import math
import functools
import numpy as np
import jax
import jax.numpy as jnp
from jax import lax
from jax.experimental import pallas as pl
from jax.experimental.pallas import tpu as pltpu
from jax.sharding import PartitionSpec as P

BF = jnp.bfloat16
F32 = jnp.float32
BATCH = 4
CH = 32


def hi_lo(x):
    hi = x.astype(BF)
    lo = (x - hi.astype(F32)).astype(BF)
    return hi, lo


def halves(table):
    table = table.astype(np.float32)
    hi = table.astype(BF)
    return hi, (table - hi.astype(np.float32)).astype(BF)


def angles(window, radix, q):
    part = window // radix
    n, j = np.arange(part)[:, None], np.arange(part)[None, :]
    angle = 2.0 * math.pi * ((n * (radix * j + q)) % window) / window
    return np.cos(angle) / math.sqrt(window), np.sin(angle) / math.sqrt(window)


def tables(window):
    right_f, right_i, left_f, left_i = [], [], [], []
    for q in range(2):
        c, s = angles(window, 2, q)
        for table, into in ((np.block([[c, -s], [s, c]]), right_f), (np.block([[c.T, s.T], [-s.T, c.T]]), right_i)):
            hi, lo = halves(table)
            into.append(np.concatenate([hi, lo, hi], axis=0))
    for q in range(4):
        c, s = angles(window, 4, q)
        for table, into in ((np.block([[c.T, s.T], [-s.T, c.T]]), left_f), (np.block([[c, -s], [s, c]]), left_i)):
            hi, lo = halves(table)
            top = np.concatenate([hi, hi], axis=1)
            into.append(np.concatenate([top, np.concatenate([lo, np.zeros_like(lo)], axis=1)], axis=0))
    order = np.concatenate([np.arange(0, window, 2), np.arange(1, window, 2)])
    shuffle = np.zeros((window, window), np.float32)
    shuffle[order, np.arange(window)] = 1.0
    return np.stack(right_f), np.stack(right_i), np.stack(left_f), np.stack(left_i), shuffle.astype(BF)


def cat(parts, axis):
    return jnp.concatenate(parts, axis=axis)


def mm(a, b):
    return jnp.dot(a, b, preferred_element_type=F32)


def make_compute(window, modes, slots, tile_rows, tile_cols, cols_n):
    w, half, quart = window, window // 2, window // 4
    ch = CH
    ext_rows, ext_cols = tile_rows + w, tile_cols + w

    def kernel(positions, counts, own, right, low, diag, probe, amps, rf, ri, lf, li, shuffle,
               g_own, g_right, g_low, g_diag, pg, along,
               ext, grad, amp_buf, win, fac, lhs, rhs, mid, far, near, amp_sem, sem):
        row_id, col_id, mine = place()
        count = counts[row_id * cols_n + col_id]
        def quarters(whole, parts):
            pairs = []
            for k in range(4):
                for t in range(2):
                    down = slice(tile_rows, ext_rows) if k >= 2 else slice(0, tile_rows)
                    pairs.append((whole.at[2 * (k % 2) + t, :, down, :], parts[k].at[:, :, 128 * t:128 * t + 128]))
            return pairs

        loads = [
            pltpu.make_async_copy(part, inside, sem.at[k])
            for k, (inside, part) in enumerate(quarters(ext, (own, right, low, diag)))
        ]
        for copy in loads:
            copy.start()

        def amp_copies(slot, place):
            return [
                pltpu.make_async_copy(
                    amps.at[slot, :, 128 * t:128 * t + 128], amp_buf.at[place, t], amp_sem.at[place, t]
                )
                for t in range(2)
            ]

        for copy in amp_copies(0, 0):
            copy.start()

        def clear(i, carry):
            at = pl.multiple_of(i * ch, ch)
            for c in range(2):
                for t in range(4):
                    grad[t, c, pl.ds(at, ch), :] = jnp.zeros((ch, 128), F32)
            return carry

        lax.fori_loop(0, ext_rows // ch, clear, 0)
        pg[...] = jnp.zeros(pg.shape, F32)

        def no_shift(i, carry):
            along[0, i] = 0.0
            along[1, i] = 0.0
            return carry

        lax.fori_loop(0, slots, no_shift, 0)
        for copy in loads:
            copy.wait()

        def put_lhs(parity, at, x):
            hi, lo = hi_lo(x)
            lhs[parity, at:at + ch, :w] = hi
            lhs[parity, at:at + ch, w:] = lo

        def put_rhs(m, q, at, x):
            hi, lo = hi_lo(x)
            rhs[m, q, at:at + ch, :] = hi
            rhs[m, q, half + at:half + at + ch, :] = lo

        def right_apply(m, table, into):
            rows = slice(m * w, (m + BATCH) * w)
            for parity in range(2):
                hi, lo = lhs[parity, rows, :w], lhs[parity, rows, w:]
                into[parity, rows, :] = mm(cat([hi, hi, lo], 1), table[parity])

        def left_apply(m, q, table):
            both = mm(table[q], rhs[m, q])
            return both[:half] + both[half:]

        def forward_rows(m):
            for r in range(0, quart, ch):
                y = [[], [], [], []]
                for parity in range(2):
                    x = [mid[parity, m * w + p * quart + r:m * w + p * quart + r + ch, :] for p in range(4)]
                    a, b, c, d = x[0] + x[2], x[1] + x[3], x[0] - x[2], x[1] - x[3]
                    y[0].append(a + b)
                    y[2].append(a - b)
                    turned = cat([d[:, half:], -d[:, :half]], 1)
                    y[1].append(c + turned)
                    y[3].append(c - turned)
                for q in range(4):
                    e, o = y[q]
                    put_rhs(m, q, r, cat([e[:, :half], o[:, :half]], 1))
                    put_rhs(m, q, quart + r, cat([e[:, half:], o[:, half:]], 1))
            for q in range(4):
                far[m, q] = left_apply(m, q, lf)

        def inverse_rows(m):
            for q in range(4):
                for r in range(0, quart, ch):
                    f = fac[q, r:r + ch, :]
                    for at in (r, quart + r):
                        put_rhs(m, q, at, f * far[m, q, at:at + ch, :])
            for q in range(4):
                far[m, q] = left_apply(m, q, li)
            for r in range(0, quart, ch):
                re = [far[m, q, r:r + ch, :] for q in range(4)]
                im = [far[m, q, quart + r:quart + r + ch, :] for q in range(4)]
                are, aim, bre, bim = re[0] + re[2], im[0] + im[2], re[1] + re[3], im[1] + im[3]
                cre, cim, dre, dim = re[0] - re[2], im[0] - im[2], re[1] - re[3], im[1] - im[3]
                outs = (
                    (are + bre, aim + bim), (cre - dim, cim + dre),
                    (are - bre, aim - bim), (cre + dim, cim - dre),
                )
                for p, (xre, xim) in enumerate(outs):
                    for parity in range(2):
                        cols = slice(parity * half, parity * half + half)
                        put_lhs(parity, m * w + p * quart + r, cat([xre[:, cols], xim[:, cols]], 1))

        def do_slot(slot, carry):
            row = positions[0, slot] - row_id * tile_rows
            col = positions[1, slot] - col_id * tile_cols
            tile_at = col // 128
            off = lax.rem(col, 128)
            back = lax.rem(w + 128 - off, w + 128)
            place_at = lax.rem(slot, 2)
            for copy in amp_copies(slot, place_at):
                copy.wait()

            @pl.when(slot + 1 < count)
            def _():
                for copy in amp_copies(slot + 1, 1 - place_at):
                    copy.start()

            for c in range(2):
                for r in range(0, w, ch):
                    wide = cat([ext[tile_at + t, c, pl.ds(row + r, ch), :] for t in range(3)], 1)
                    win[c, r:r + ch, :] = pltpu.roll(wide, back, 1)[:, :w]

            for q in range(4):
                a = cat([amp_buf[place_at, t, pl.ds(q, quart, stride=4), :] for t in range(2)], 1)
                a0, a1 = hi_lo(a)
                a2 = (a - a0.astype(F32) - a1.astype(F32)).astype(BF)
                stack = mm(cat([a0, a1, a2], 0), shuffle[...])
                fac[q] = stack[:quart] + stack[quart:2 * quart] + stack[2 * quart:]

            for m in range(modes):
                for r in range(0, w, ch):
                    vre, vim = win[0, r:r + ch, :], win[1, r:r + ch, :]
                    pre, pim = probe[0, m, r:r + ch, :], probe[1, m, r:r + ch, :]
                    are = pre * vre - pim * vim
                    aim = pre * vim + pim * vre
                    for parity in range(2):
                        if parity == 0:
                            x = cat([are[:, :half] + are[:, half:], aim[:, :half] + aim[:, half:]], 1)
                        else:
                            x = cat([are[:, :half] - are[:, half:], aim[:, :half] - aim[:, half:]], 1)
                        put_lhs(parity, m * w + r, x)
                if (m + 1) % BATCH == 0:
                    right_apply(m + 1 - BATCH, rf, mid)
                    for n in range(m + 1 - BATCH, m + 1):
                        forward_rows(n)

            for q in range(4):
                for r in range(0, quart, ch):
                    total = None
                    for m in range(modes):
                        re = far[m, q, r:r + ch, :]
                        im = far[m, q, quart + r:quart + r + ch, :]
                        term = re * re + im * im
                        total = term if total is None else total + term
                    fac[q, r:r + ch, :] = 0.25 * (1.0 - fac[q, r:r + ch, :] * lax.rsqrt(total + 0.5))

            for m in range(modes):
                inverse_rows(m)
                if (m + 1) % BATCH == 0:
                    right_apply(m + 1 - BATCH, ri, near)

            rows_sum = jnp.zeros((8, w), F32)
            cols_sum = jnp.zeros((8, w), F32)
            lanes = lax.broadcasted_iota(jnp.int32, (ch, w), 1)
            inner = (lanes >= 1) & (lanes <= w - 2)

            def near_of(m, r):
                at = m * w + r
                if not isinstance(m, int):
                    at = pl.multiple_of(at, ch)
                e, o = near[0, pl.ds(at, ch), :], near[1, pl.ds(at, ch), :]
                s, d = e + o, e - o
                return cat([s[:, :half], d[:, :half]], 1), cat([s[:, half:], d[:, half:]], 1)

            for r in range(0, w, ch):
                gre = gim = None
                for m in range(modes):
                    nre, nim = near_of(m, r)
                    pre, pim = probe[0, m, r:r + ch, :], probe[1, m, r:r + ch, :]
                    tre = pre * nre + pim * nim
                    tim = pre * nim - pim * nre
                    gre = tre if gre is None else gre + tre
                    gim = tim if gim is None else gim + tim
                for c, g in ((0, gre), (1, gim)):
                    spread = pltpu.roll(cat([g, jnp.zeros((ch, 128), F32)], 1), off, 1)
                    for t in range(3):
                        grad[tile_at + t, c, pl.ds(row + r, ch), :] += spread[:, 128 * t:128 * t + 128]
                vre, vim = win[0, r:r + ch, :], win[1, r:r + ch, :]
                nre, nim = near_of(mine, r)
                pg[0, r:r + ch, :] += vre * nre + vim * nim
                pg[1, r:r + ch, :] += vre * nim - vim * nre
                dre = pltpu.roll(vre, w - 1, 1) - pltpu.roll(vre, 1, 1)
                dim = pltpu.roll(vim, w - 1, 1) - pltpu.roll(vim, 1, 1)
                t = jnp.where(inner, gre * dre + gim * dim, 0.0)
                cols_sum = cols_sum + jnp.sum(t.reshape(ch // 8, 8, w), axis=0)
                lo_r, hi_r = max(r, 1), min(r + ch, w - 1)
                up = [ext_rows_slice(win, c, r + 1, ch, w) for c in range(2)]
                dn = [ext_rows_slice(win, c, r - 1, ch, w) for c in range(2)]
                t = gre * (up[0] - dn[0]) + gim * (up[1] - dn[1])
                if lo_r != r or hi_r != r + ch:
                    idx = lax.broadcasted_iota(jnp.int32, (ch, w), 0) + r
                    t = jnp.where((idx >= lo_r) & (idx < hi_r), t, 0.0)
                rows_sum = rows_sum + jnp.sum(t.reshape(ch // 8, 8, w), axis=0)
            along[0, slot] = jnp.sum(rows_sum) * (0.5 / w)
            along[1, slot] = jnp.sum(cols_sum) * (0.5 / w)
            return carry

        def ext_rows_slice(ref, c, start, size, width):
            if start < 0:
                return cat([ref[c, 0:1, :], ref[c, 0:size - 1, :]], 0)
            if start + size > w:
                return cat([ref[c, start:w, :], ref[c, w - 1:w, :]], 0)
            return ref[c, start:start + size, :]

        lax.fori_loop(0, count, do_slot, 0)
        stores = [
            pltpu.make_async_copy(inside, part, sem.at[k])
            for k, (inside, part) in enumerate(quarters(grad, (g_own, g_right, g_low, g_diag)))
        ]
        for copy in stores:
            copy.start()
        for copy in stores:
            copy.wait()

    hbm = pl.BlockSpec(memory_space=pl.ANY)
    vmem = pl.BlockSpec(memory_space=pltpu.VMEM)
    smem = pl.BlockSpec(memory_space=pltpu.SMEM)
    shape = jax.ShapeDtypeStruct
    return pl.pallas_call(
        kernel,
        name="slots",
        in_specs=[smem, smem, hbm, hbm, hbm, hbm, vmem, hbm, vmem, vmem, vmem, vmem, vmem],
        out_specs=[hbm, hbm, hbm, hbm, vmem, smem],
        out_shape=[
            shape((2, tile_rows, tile_cols), F32),
            shape((2, tile_rows, w), F32),
            shape((2, w, tile_cols), F32),
            shape((2, w, w), F32),
            shape((2, w, w), F32),
            shape((2, slots), F32),
        ],
        scratch_shapes=[
            pltpu.VMEM((ext_cols // 128, 2, ext_rows, 128), F32),
            pltpu.VMEM((ext_cols // 128, 2, ext_rows, 128), F32),
            pltpu.VMEM((2, 2, w, 128), F32),
            pltpu.VMEM((2, w, w), F32),
            pltpu.VMEM((4, quart, w), F32),
            pltpu.VMEM((2, modes * w, 2 * w), BF),
            pltpu.VMEM((modes, 4, w, w), BF),
            pltpu.VMEM((2, modes * w, w), F32),
            pltpu.VMEM((modes, 4, half, w), F32),
            pltpu.VMEM((2, modes * w, w), F32),
            pltpu.SemaphoreType.DMA((2, 2)),
            pltpu.SemaphoreType.DMA((8,)),
        ],
        compiler_params=pltpu.CompilerParams(vmem_limit_bytes=60 << 20),
        cost_estimate=pl.CostEstimate(flops=10**11, bytes_accessed=10**7, transcendentals=0),
    )


MESH = pl.DeviceIdType.MESH


def place():
    return lax.axis_index("row"), lax.axis_index("col"), lax.axis_index("mode")


def device(r, c, m):
    return {"row": r, "col": c, "mode": m}


def remote(src, dst, send, recv, to):
    return pltpu.make_async_remote_copy(
        src_ref=src, dst_ref=dst, send_sem=send, recv_sem=recv, device_id=to, device_id_type=MESH
    )


def greet(to):
    pl.semaphore_signal(pltpu.get_barrier_semaphore(), inc=1, device_id=to, device_id_type=MESH)


class Quarters:
    def __init__(self, src, dst, modes, rows, r, c, chunks, sems):
        me_r, me_c, m = place()
        self.m, self.modes, self.chunks = m, modes, chunks
        self.rows = rows // modes // chunks
        self.src, self.dst = src, dst
        self.ys, self.yr, self.zs, self.zr, self.ts, self.tr = sems
        self.peer = device(r, c, m)
        self.next = device(me_r, me_c, lax.rem(m + 1, modes))
        self.prev = device(me_r, me_c, lax.rem(m + modes - 1, modes))

    def part(self, ref, owner, i):
        at = pl.multiple_of((owner * self.chunks + i) * self.rows, self.rows)
        return ref.at[:, pl.ds(at, self.rows), :]

    def first(self, i):
        mine = self.part(self.src, self.m, i)
        return remote(mine, self.part(self.dst, self.m, i), self.ys.at[i], self.yr.at[i], self.peer)

    def ring(self, i, way):
        mine = self.part(self.dst, self.m, i)
        return remote(mine, mine, self.zs.at[way, i], self.zr.at[way, i], self.next if way == 0 else self.prev)

    def way(self, i):
        return 0 if i < self.chunks // 2 else 1

    def relay(self, i):
        back = self.modes - 1 if self.way(i) == 0 else 1
        block = self.part(self.dst, lax.rem(self.m + back, self.modes), i)
        return remote(block, block, self.ts.at[i], self.tr.at[i], self.next if self.way(i) == 0 else self.prev)

    def start(self):
        for i in range(self.chunks):
            self.first(i).start()

    def sent(self):
        for i in range(self.chunks):
            self.first(i).wait_send()

    def take(self, some=None):
        for i in range(self.chunks) if some is None else some:
            self.first(i).wait_recv()
            self.ring(i, 0).start()
            self.ring(i, 1).start()

    def turn(self):
        for i in range(self.chunks):
            self.ring(i, self.way(i)).wait_recv()
            self.relay(i).start()

    def finish(self):
        for i in range(self.chunks):
            self.ring(i, 1 - self.way(i)).wait_recv()
            self.relay(i).wait_recv()
        for i in range(self.chunks):
            self.ring(i, 0).wait_send()
            self.ring(i, 1).wait_send()
            self.relay(i).wait_send()


STRIP, EDGE = 4, 2


def quarter_sems(chunks):
    one = pltpu.SemaphoreType.DMA((chunks,))
    two = pltpu.SemaphoreType.DMA((2, chunks))
    return [one, one, two, two, one, one]


def when(cond, *steps):
    @pl.when(cond)
    def _():
        for step in steps:
            step()


def make_spread(window, modes, tile_rows, tile_cols, rows_n, cols_n):
    w = window

    def kernel(tile, probe, right, low, diag, gathered, *sems):
        quarter, (one_s, one_r, p_s, p_r, x_s, x_r, own_sem) = sems[:6], sems[6:]
        r, c, m = place()
        core = lax.rem(c, 2)
        other = c + 1 - 2 * core
        odd, even = core == 1, core == 0
        has_left, has_right = c > 0, c < cols_n - 1
        top = tile.at[:, pl.ds(0, w), :]

        for k in range(1, modes):
            greet(device(r, c, lax.rem(m + k, modes)))
        greet(device(r, other, m))
        greet(device(rows_n - 1 - r, c, m))
        count = modes + 1
        away = jnp.where(odd, jnp.minimum(c + 1, cols_n - 1), jnp.maximum(c - 1, 0))
        has_away = jnp.where(odd, has_right, has_left)

        @pl.when(has_away)
        def _():
            greet(device(r, away, m))

        has_diag = has_away & jnp.where(odd, r == 0, r == 1)

        @pl.when(has_diag)
        def _():
            greet(device(rows_n - 1 - r, away, m))

        pl.semaphore_wait(
            pltpu.get_barrier_semaphore(),
            count + has_away.astype(jnp.int32) + has_diag.astype(jnp.int32),
        )

        strip = Quarters(tile, right, modes, tile_rows, r, away, STRIP, quarter)
        whole = remote(tile, right, one_s.at[0], one_r.at[0], device(r, other, m))
        down = remote(top, low, one_s.at[1], one_r.at[1], device(rows_n - 1 - r, c, m))
        corner = remote(top, diag, one_s.at[2], one_r.at[2], device(rows_n - 1 - r, away, m))
        corner_on = remote(low, diag, one_s.at[2], one_r.at[2], device(r, other, m))

        def probe_copy(k):
            half = gathered.at[pl.ds(core, 1), pl.ds(m, 1)]
            return remote(
                probe.at[pl.ds(core, 1)], half, p_s.at[k], p_r.at[k], device(r, c, lax.rem(m + k, modes))
            )

        def probe_pass(k):
            half = gathered.at[pl.ds(core, 1), pl.ds(lax.rem(m + modes - k, modes), 1)]
            return remote(half, half, x_s.at[k], x_r.at[k], device(r, other, m))

        @pl.when(even & has_left)
        def _():
            strip.start()

        @pl.when(r == 1)
        def _():
            down.start()

        @pl.when(even & has_diag)
        def _():
            corner.start()

        for k in (1, 3, 2):
            probe_copy(k).start()

        @pl.when(odd)
        def _():
            whole.start()

        keep = pltpu.make_async_copy(probe, gathered.at[:, pl.ds(m, 1)], own_sem)
        keep.start()

        @pl.when(odd & has_right)
        def _():
            strip.take()

        @pl.when(r == 0)
        def _():
            down.wait_recv()

        @pl.when(odd & (r == 0))
        def _():
            corner_on.start()

        for k in (1, 3, 2):
            probe_copy(k).wait_recv()
            probe_pass(k).start()

        @pl.when(odd & has_right)
        def _():
            strip.turn()
            strip.finish()

        @pl.when(odd & has_diag)
        def _():
            corner.wait_recv()

        @pl.when(even)
        def _():
            whole.wait_recv()

        @pl.when(even & (r == 0))
        def _():
            corner_on.wait_recv()

        for k in (1, 3, 2):
            probe_pass(k).wait_recv()
            probe_pass(k).wait_send()
            probe_copy(k).wait_send()
        keep.wait()

        @pl.when(odd)
        def _():
            whole.wait_send()

        @pl.when(odd & (r == 0))
        def _():
            corner_on.wait_send()

        @pl.when(even & has_left)
        def _():
            strip.sent()

        @pl.when(r == 1)
        def _():
            down.wait_send()

        @pl.when(even & has_diag)
        def _():
            corner.wait_send()

    hbm = pl.BlockSpec(memory_space=pl.ANY)
    shape = jax.ShapeDtypeStruct
    return pl.pallas_call(
        kernel,
        name="spread",
        in_specs=[hbm, hbm],
        out_specs=[hbm] * 4,
        out_shape=[
            shape((2, tile_rows, tile_cols), F32),
            shape((2, w, tile_cols), F32),
            shape((2, w, tile_cols), F32),
            shape((2, modes, w, w), F32),
        ],
        scratch_shapes=quarter_sems(STRIP) + [pltpu.SemaphoreType.DMA((3,))] * 2
        + [pltpu.SemaphoreType.DMA((modes,))] * 4 + [pltpu.SemaphoreType.DMA],
        compiler_params=pltpu.CompilerParams(collective_id=0, has_side_effects=True),
    )


def make_collect(window, modes, tile_rows, tile_cols, rows_n, cols_n):
    w = window
    chips = rows_n * cols_n // 2
    piece = 2 * w // chips

    def kernel(g_right, g_low, g_diag, pg, right, low, diag, total, *sems):
        strip_sems, low_sems, diag_sems = sems[:6], sems[6:12], sems[12:18]
        one_s, one_r, x_s, x_r, y_s, y_r, a_s, a_r, b_s, b_r, in_sem, pair, got, mine = sems[18:]
        r, c, m = place()
        core = lax.rem(c, 2)
        chip = r * (cols_n // 2) + c // 2
        other = c + 1 - 2 * core
        odd, even = core == 1, core == 0
        away = jnp.where(odd, jnp.minimum(c + 1, cols_n - 1), jnp.maximum(c - 1, 0))
        has_away = jnp.where(odd, c < cols_n - 1, c > 0)
        flip = rows_n - 1 - r
        over = jnp.where(r == 0, jnp.minimum(c + 1, cols_n - 1), jnp.maximum(c - 1, 0))
        has_over = jnp.where(r == 0, c < cols_n - 1, c > 0)

        def partner(k):
            p = lax.rem(chip + k, chips)
            return device(p // (cols_n // 2), 2 * lax.rem(p, cols_n // 2) + core, m)

        def hello(k, carry):
            greet(partner(k))
            return carry

        greet(device(r, other, m))
        for k in (1, modes - 1):
            greet(device(r, c, lax.rem(m + k, modes)))
        when(has_away, lambda: greet(device(r, away, m)))
        when(has_over, lambda: greet(device(flip, over, m)))
        when(even, lambda: greet(device(flip, c, m)))
        when(odd, lambda: lax.fori_loop(1, chips, hello, 0))
        pl.semaphore_wait(
            pltpu.get_barrier_semaphore(),
            3 + jnp.where(odd, chips - 1, 1) + has_away.astype(jnp.int32) + has_over.astype(jnp.int32),
        )

        strip = Quarters(g_right, right, modes, tile_rows, r, away, STRIP, strip_sems)
        down = Quarters(g_low, low, modes, w, flip, c, EDGE, low_sems)
        corner = Quarters(g_diag, diag, modes, w, flip, over, EDGE, diag_sems)
        whole = remote(g_right, right, one_s, one_r, device(r, other, m))
        swap = remote(pg, pair.at[0], x_s, x_r, device(r, other, m))
        own = pltpu.make_async_copy(pg, pair.at[1], in_sem)
        at_chip = pl.ds(pl.multiple_of(chip * piece, piece), piece)
        rest = got.at[pl.ds(1, chips - 1)]
        many = total.at[pl.ds(0, (chips - 1) * piece), :]
        keep = pltpu.make_async_copy(mine, total.at[at_chip, :], in_sem)
        give = remote(total, total, y_s, y_r, device(r, other, m))

        def scatter_go(k, carry):
            p = lax.rem(chip + k, chips)
            rows = pl.ds(pl.multiple_of(p * piece, piece), piece)
            remote(pair.at[1, rows, :], got.at[k], a_s, a_r, partner(k)).start()
            return carry

        def share_go(k, carry):
            remote(mine, total.at[at_chip, :], b_s, b_r, partner(k)).start()
            return carry

        def add(k, acc):
            return acc + got[k]

        def sum_pair():
            own.wait()
            swap.wait_recv()
            pair[1] = pair[0] + pair[1]
            lax.fori_loop(1, chips, scatter_go, 0)

        def sum_plane():
            pltpu.make_async_copy(rest, rest, a_r).wait()
            mine[...] = lax.fori_loop(1, chips, add, pair[1, at_chip, :]) * (1.0 / 16.0)
            keep.start()
            lax.fori_loop(1, chips, share_go, 0)

        def sum_give():
            keep.wait()
            pltpu.make_async_copy(many, many, b_r).wait()
            give.start()

        def sum_end():
            pltpu.make_async_copy(rest, rest, a_s).wait()
            pltpu.make_async_copy(many, many, b_s).wait()
            give.wait_send()

        when(even, swap.start)
        when(odd, own.start)
        when(odd & has_away, strip.start)
        when(r == 0, down.start)
        when((r == 0) & has_over, corner.start)
        when(even, whole.start)
        when(odd, sum_pair)
        when(even & has_away, strip.take)
        when(r == 1, down.take)
        when((r == 1) & has_over, corner.take)
        when(odd, sum_plane)
        when(even & has_away, strip.turn)
        when(r == 1, down.turn)
        when((r == 1) & has_over, corner.turn)
        when(odd, sum_give)
        when(even & has_away, strip.finish)
        when(r == 1, down.finish)
        when((r == 1) & has_over, corner.finish)
        when(odd, whole.wait_recv)
        when(even, give.wait_recv)
        when(even, swap.wait_send)
        when(odd, sum_end)
        when(odd & has_away, strip.sent)
        when(r == 0, down.sent)
        when((r == 0) & has_over, corner.sent)
        when(even, whole.wait_send)

    hbm = pl.BlockSpec(memory_space=pl.ANY)
    shape = jax.ShapeDtypeStruct
    dma = pltpu.SemaphoreType.DMA
    return pl.pallas_call(
        kernel,
        name="collect",
        in_specs=[hbm] * 4,
        out_specs=[hbm] * 4,
        out_shape=[
            shape((2, tile_rows, tile_cols), F32),
            shape((2, w, tile_cols), F32),
            shape((2, w, tile_cols), F32),
            shape((2 * w, w), F32),
        ],
        scratch_shapes=quarter_sems(STRIP) + quarter_sems(EDGE) + quarter_sems(EDGE) + [dma] * 11
        + [pltpu.VMEM((2, 2 * w, w), F32), pltpu.VMEM((chips, piece, w), F32), pltpu.VMEM((piece, w), F32)],
        compiler_params=pltpu.CompilerParams(collective_id=1, has_side_effects=True),
    )


def make_finish(window, tile_rows, tile_cols):
    w = window
    blocks = tile_rows // w

    def kernel(own, strip, low, diag, total, grad, probe, a, b, e, s_a, s_b, s_e, s_out):
        r, c, m = place()
        below, inner = r > 0, c > 0

        def rows(k):
            return pl.ds(k * w, w)

        loads = [
            [
                pltpu.make_async_copy(own.at[:, rows(k), :], a.at[:, rows(k), :], s_a.at[k]),
                pltpu.make_async_copy(strip.at[:, rows(k), :], b.at[:, rows(k), :], s_b.at[k]),
            ]
            for k in range(blocks)
        ]
        edges = [pltpu.make_async_copy(src, e.at[n], s_e.at[n]) for n, src in enumerate((low, diag, total))]
        for k in reversed(range(blocks)):
            for copy in loads[k]:
                copy.start()
        for copy in edges:
            copy.start()
        stores = [pltpu.make_async_copy(a.at[:, rows(k), :], grad.at[:, rows(k), :], s_out.at[k]) for k in range(blocks)]

        def add(k, x):
            for part in range(2):
                a[part, k * w:k * w + w, :] += x[part]

        for k in reversed(range(blocks)):
            for copy in loads[k]:
                copy.wait()
            when(inner, lambda: add(k, b.at[:, rows(k), :]))
            if k == 0:
                for copy in edges:
                    copy.wait()
                when(below, lambda: add(0, e.at[0]))
                when(below & inner, lambda: add(0, e.at[1]))
                last = pltpu.make_async_copy(e.at[2], probe, s_out.at[blocks])
                last.start()
            stores[k].start()
        for copy in stores + [last]:
            copy.wait()

    hbm = pl.BlockSpec(memory_space=pl.ANY)
    dma = pltpu.SemaphoreType.DMA
    tile = (2, tile_rows, tile_cols)
    return pl.pallas_call(
        kernel,
        name="finish",
        in_specs=[hbm] * 5,
        out_specs=[hbm] * 2,
        out_shape=[jax.ShapeDtypeStruct(tile, F32), jax.ShapeDtypeStruct((2, w, w), F32)],
        scratch_shapes=[
            pltpu.VMEM(tile, F32), pltpu.VMEM(tile, F32), pltpu.VMEM((3, 2, w, w), F32),
            dma((blocks,)), dma((blocks,)), dma((3,)), dma((blocks + 1,)),
        ],
        compiler_params=pltpu.CompilerParams(vmem_limit_bytes=60 << 20),
    )


def per_device(object_slab, probe_modes, amplitudes, scan_counts, scan_positions):
    window = probe_modes.shape[-1]
    tile_rows, tile_cols = object_slab.shape[1:]
    slots = amplitudes.shape[0]
    modes, cols_n, rows_n = (lax.axis_size(a) for a in ("mode", "col", "row"))
    sizes = (window, modes, tile_rows, tile_cols, rows_n, cols_n)
    right, low, diag, probe = make_spread(*sizes)(object_slab, probe_modes)
    consts = [jnp.asarray(t) for t in tables(window)]
    compute = make_compute(window, modes, slots, tile_rows, tile_cols, cols_n)
    g_own, g_right, g_low, g_diag, pg, shift = compute(
        scan_positions, scan_counts, object_slab, right, low, diag, probe, amplitudes, *consts
    )
    from_left, from_up, from_diag, total = make_collect(*sizes)(
        g_right, g_low, g_diag, pg.reshape(2 * window, window)
    )
    grad, probe_grad = make_finish(window, tile_rows, tile_cols)(
        g_own, from_left, from_up, from_diag, total.reshape(2, window, window)
    )
    return (grad, probe_grad.reshape(2, 1, window, window), shift)


def solution(mesh):
    in_specs = (
        P(None, "row", "col"),
        P(None, "mode", None, None),
        P(("row", "col"), None, None),
        P(),
        P(None, ("row", "col")),
    )
    out_specs = (P(None, "row", "col"), P(None, "mode", None, None), P(None, ("row", "col")))
    return jax.shard_map(
        per_device, mesh=mesh, in_specs=in_specs, out_specs=out_specs, check_vma=False
    )
```

```python
import math
import functools
import numpy as np
import jax
import jax.numpy as jnp
from jax import lax
from jax.experimental import pallas as pl
from jax.experimental.pallas import tpu as pltpu
from jax.sharding import PartitionSpec as P

BF = jnp.bfloat16
F32 = jnp.float32
BATCH = 4
CH = 32


def hi_lo(x):
    hi = x.astype(BF)
    lo = (x - hi.astype(F32)).astype(BF)
    return hi, lo


def halves(table):
    table = table.astype(np.float32)
    hi = table.astype(BF)
    return hi, (table - hi.astype(np.float32)).astype(BF)


def angles(window, radix, q):
    part = window // radix
    n, j = np.arange(part)[:, None], np.arange(part)[None, :]
    angle = 2.0 * math.pi * ((n * (radix * j + q)) % window) / window
    return np.cos(angle) / math.sqrt(window), np.sin(angle) / math.sqrt(window)


def tables(window):
    right_f, right_i, left_f, left_i = [], [], [], []
    for q in range(2):
        c, s = angles(window, 2, q)
        for table, into in ((np.block([[c, -s], [s, c]]), right_f), (np.block([[c.T, s.T], [-s.T, c.T]]), right_i)):
            hi, lo = halves(table)
            into.append(np.concatenate([hi, lo, hi], axis=0))
    for q in range(4):
        c, s = angles(window, 4, q)
        for table, into in ((np.block([[c.T, s.T], [-s.T, c.T]]), left_f), (np.block([[c, -s], [s, c]]), left_i)):
            hi, lo = halves(table)
            top = np.concatenate([hi, hi], axis=1)
            into.append(np.concatenate([top, np.concatenate([lo, np.zeros_like(lo)], axis=1)], axis=0))
    order = np.concatenate([np.arange(0, window, 2), np.arange(1, window, 2)])
    shuffle = np.zeros((window, window), np.float32)
    shuffle[order, np.arange(window)] = 1.0
    return np.stack(right_f), np.stack(right_i), np.stack(left_f), np.stack(left_i), shuffle.astype(BF)


def cat(parts, axis):
    return jnp.concatenate(parts, axis=axis)


def mm(a, b):
    return jnp.dot(a, b, preferred_element_type=F32)


def make_compute(window, modes, slots, tile_rows, tile_cols, cols_n):
    w, half, quart = window, window // 2, window // 4
    ch = CH
    ext_rows, ext_cols = tile_rows + w, tile_cols + w

    def kernel(positions, counts, own, right, low, diag, probe, amps, rf, ri, lf, li, shuffle,
               g_own, g_right, g_low, g_diag, pg, along,
               ext, grad, amp_buf, win, fac, lhs, rhs, mid, far, near, amp_sem, sem):
        row_id, col_id, mine = place()
        count = counts[row_id * cols_n + col_id]
        def quarters(whole, parts):
            pairs = []
            for k in range(4):
                for t in range(2):
                    down = slice(tile_rows, ext_rows) if k >= 2 else slice(0, tile_rows)
                    pairs.append((whole.at[2 * (k % 2) + t, :, down, :], parts[k].at[:, :, 128 * t:128 * t + 128]))
            return pairs

        loads = [
            pltpu.make_async_copy(part, inside, sem.at[k])
            for k, (inside, part) in enumerate(quarters(ext, (own, right, low, diag)))
        ]
        for copy in loads:
            copy.start()

        def amp_copies(slot, place):
            return [
                pltpu.make_async_copy(
                    amps.at[slot, :, 128 * t:128 * t + 128], amp_buf.at[place, t], amp_sem.at[place, t]
                )
                for t in range(2)
            ]

        for copy in amp_copies(0, 0):
            copy.start()

        def clear(i, carry):
            at = pl.multiple_of(i * ch, ch)
            for c in range(2):
                for t in range(4):
                    grad[t, c, pl.ds(at, ch), :] = jnp.zeros((ch, 128), F32)
            return carry

        lax.fori_loop(0, ext_rows // ch, clear, 0)
        pg[...] = jnp.zeros(pg.shape, F32)

        def no_shift(i, carry):
            along[0, i] = 0.0
            along[1, i] = 0.0
            return carry

        lax.fori_loop(0, slots, no_shift, 0)
        for copy in loads:
            copy.wait()

        def put_lhs(parity, at, x):
            hi, lo = hi_lo(x)
            lhs[parity, at:at + ch, :w] = hi
            lhs[parity, at:at + ch, w:] = lo

        def put_rhs(m, q, at, x):
            hi, lo = hi_lo(x)
            rhs[m, q, at:at + ch, :] = hi
            rhs[m, q, half + at:half + at + ch, :] = lo

        def right_apply(m, table, into):
            rows = slice(m * w, (m + BATCH) * w)
            for parity in range(2):
                hi, lo = lhs[parity, rows, :w], lhs[parity, rows, w:]
                into[parity, rows, :] = mm(cat([hi, hi, lo], 1), table[parity])

        def left_apply(m, q, table):
            both = mm(table[q], rhs[m, q])
            return both[:half] + both[half:]

        def forward_rows(m):
            for r in range(0, quart, ch):
                y = [[], [], [], []]
                for parity in range(2):
                    x = [mid[parity, m * w + p * quart + r:m * w + p * quart + r + ch, :] for p in range(4)]
                    a, b, c, d = x[0] + x[2], x[1] + x[3], x[0] - x[2], x[1] - x[3]
                    y[0].append(a + b)
                    y[2].append(a - b)
                    turned = cat([d[:, half:], -d[:, :half]], 1)
                    y[1].append(c + turned)
                    y[3].append(c - turned)
                for q in range(4):
                    e, o = y[q]
                    put_rhs(m, q, r, cat([e[:, :half], o[:, :half]], 1))
                    put_rhs(m, q, quart + r, cat([e[:, half:], o[:, half:]], 1))
            for q in range(4):
                far[m, q] = left_apply(m, q, lf)

        def inverse_rows(m):
            for q in range(4):
                for r in range(0, quart, ch):
                    f = fac[q, r:r + ch, :]
                    for at in (r, quart + r):
                        put_rhs(m, q, at, f * far[m, q, at:at + ch, :])
            for q in range(4):
                far[m, q] = left_apply(m, q, li)
            for r in range(0, quart, ch):
                re = [far[m, q, r:r + ch, :] for q in range(4)]
                im = [far[m, q, quart + r:quart + r + ch, :] for q in range(4)]
                are, aim, bre, bim = re[0] + re[2], im[0] + im[2], re[1] + re[3], im[1] + im[3]
                cre, cim, dre, dim = re[0] - re[2], im[0] - im[2], re[1] - re[3], im[1] - im[3]
                outs = (
                    (are + bre, aim + bim), (cre - dim, cim + dre),
                    (are - bre, aim - bim), (cre + dim, cim - dre),
                )
                for p, (xre, xim) in enumerate(outs):
                    for parity in range(2):
                        cols = slice(parity * half, parity * half + half)
                        put_lhs(parity, m * w + p * quart + r, cat([xre[:, cols], xim[:, cols]], 1))

        def do_slot(slot, carry):
            row = positions[0, slot] - row_id * tile_rows
            col = positions[1, slot] - col_id * tile_cols
            tile_at = col // 128
            off = lax.rem(col, 128)
            back = lax.rem(w + 128 - off, w + 128)
            place_at = lax.rem(slot, 2)
            for copy in amp_copies(slot, place_at):
                copy.wait()

            @pl.when(slot + 1 < count)
            def _():
                for copy in amp_copies(slot + 1, 1 - place_at):
                    copy.start()

            for c in range(2):
                for r in range(0, w, ch):
                    wide = cat([ext[tile_at + t, c, pl.ds(row + r, ch), :] for t in range(3)], 1)
                    win[c, r:r + ch, :] = pltpu.roll(wide, back, 1)[:, :w]

            for q in range(4):
                a = cat([amp_buf[place_at, t, pl.ds(q, quart, stride=4), :] for t in range(2)], 1)
                a0, a1 = hi_lo(a)
                a2 = (a - a0.astype(F32) - a1.astype(F32)).astype(BF)
                stack = mm(cat([a0, a1, a2], 0), shuffle[...])
                fac[q] = stack[:quart] + stack[quart:2 * quart] + stack[2 * quart:]

            for m in range(modes):
                for r in range(0, w, ch):
                    vre, vim = win[0, r:r + ch, :], win[1, r:r + ch, :]
                    pre, pim = probe[0, m, r:r + ch, :], probe[1, m, r:r + ch, :]
                    are = pre * vre - pim * vim
                    aim = pre * vim + pim * vre
                    for parity in range(2):
                        if parity == 0:
                            x = cat([are[:, :half] + are[:, half:], aim[:, :half] + aim[:, half:]], 1)
                        else:
                            x = cat([are[:, :half] - are[:, half:], aim[:, :half] - aim[:, half:]], 1)
                        put_lhs(parity, m * w + r, x)
                if (m + 1) % BATCH == 0:
                    right_apply(m + 1 - BATCH, rf, mid)
                    for n in range(m + 1 - BATCH, m + 1):
                        forward_rows(n)

            for q in range(4):
                for r in range(0, quart, ch):
                    total = None
                    for m in range(modes):
                        re = far[m, q, r:r + ch, :]
                        im = far[m, q, quart + r:quart + r + ch, :]
                        term = re * re + im * im
                        total = term if total is None else total + term
                    fac[q, r:r + ch, :] = 0.25 * (1.0 - fac[q, r:r + ch, :] * lax.rsqrt(total + 0.5))

            for m in range(modes):
                inverse_rows(m)
                if (m + 1) % BATCH == 0:
                    right_apply(m + 1 - BATCH, ri, near)

            rows_sum = jnp.zeros((8, w), F32)
            cols_sum = jnp.zeros((8, w), F32)
            lanes = lax.broadcasted_iota(jnp.int32, (ch, w), 1)
            inner = (lanes >= 1) & (lanes <= w - 2)

            def near_of(m, r):
                at = m * w + r
                if not isinstance(m, int):
                    at = pl.multiple_of(at, ch)
                e, o = near[0, pl.ds(at, ch), :], near[1, pl.ds(at, ch), :]
                s, d = e + o, e - o
                return cat([s[:, :half], d[:, :half]], 1), cat([s[:, half:], d[:, half:]], 1)

            for r in range(0, w, ch):
                gre = gim = None
                for m in range(modes):
                    nre, nim = near_of(m, r)
                    pre, pim = probe[0, m, r:r + ch, :], probe[1, m, r:r + ch, :]
                    tre = pre * nre + pim * nim
                    tim = pre * nim - pim * nre
                    gre = tre if gre is None else gre + tre
                    gim = tim if gim is None else gim + tim
                for c, g in ((0, gre), (1, gim)):
                    spread = pltpu.roll(cat([g, jnp.zeros((ch, 128), F32)], 1), off, 1)
                    for t in range(3):
                        grad[tile_at + t, c, pl.ds(row + r, ch), :] += spread[:, 128 * t:128 * t + 128]
                vre, vim = win[0, r:r + ch, :], win[1, r:r + ch, :]
                nre, nim = near_of(mine, r)
                pg[0, r:r + ch, :] += vre * nre + vim * nim
                pg[1, r:r + ch, :] += vre * nim - vim * nre
                dre = pltpu.roll(vre, w - 1, 1) - pltpu.roll(vre, 1, 1)
                dim = pltpu.roll(vim, w - 1, 1) - pltpu.roll(vim, 1, 1)
                t = jnp.where(inner, gre * dre + gim * dim, 0.0)
                cols_sum = cols_sum + jnp.sum(t.reshape(ch // 8, 8, w), axis=0)
                lo_r, hi_r = max(r, 1), min(r + ch, w - 1)
                up = [ext_rows_slice(win, c, r + 1, ch, w) for c in range(2)]
                dn = [ext_rows_slice(win, c, r - 1, ch, w) for c in range(2)]
                t = gre * (up[0] - dn[0]) + gim * (up[1] - dn[1])
                if lo_r != r or hi_r != r + ch:
                    idx = lax.broadcasted_iota(jnp.int32, (ch, w), 0) + r
                    t = jnp.where((idx >= lo_r) & (idx < hi_r), t, 0.0)
                rows_sum = rows_sum + jnp.sum(t.reshape(ch // 8, 8, w), axis=0)
            along[0, slot] = jnp.sum(rows_sum) * (0.5 / w)
            along[1, slot] = jnp.sum(cols_sum) * (0.5 / w)
            return carry

        def ext_rows_slice(ref, c, start, size, width):
            if start < 0:
                return cat([ref[c, 0:1, :], ref[c, 0:size - 1, :]], 0)
            if start + size > w:
                return cat([ref[c, start:w, :], ref[c, w - 1:w, :]], 0)
            return ref[c, start:start + size, :]

        lax.fori_loop(0, count, do_slot, 0)
        stores = [
            pltpu.make_async_copy(inside, part, sem.at[k])
            for k, (inside, part) in enumerate(quarters(grad, (g_own, g_right, g_low, g_diag)))
        ]
        for copy in stores:
            copy.start()
        for copy in stores:
            copy.wait()

    hbm = pl.BlockSpec(memory_space=pl.ANY)
    vmem = pl.BlockSpec(memory_space=pltpu.VMEM)
    smem = pl.BlockSpec(memory_space=pltpu.SMEM)
    shape = jax.ShapeDtypeStruct
    return pl.pallas_call(
        kernel,
        name="slots",
        in_specs=[smem, smem, hbm, hbm, hbm, hbm, vmem, hbm, vmem, vmem, vmem, vmem, vmem],
        out_specs=[hbm, hbm, hbm, hbm, vmem, smem],
        out_shape=[
            shape((2, tile_rows, tile_cols), F32),
            shape((2, tile_rows, w), F32),
            shape((2, w, tile_cols), F32),
            shape((2, w, w), F32),
            shape((2, w, w), F32),
            shape((2, slots), F32),
        ],
        scratch_shapes=[
            pltpu.VMEM((ext_cols // 128, 2, ext_rows, 128), F32),
            pltpu.VMEM((ext_cols // 128, 2, ext_rows, 128), F32),
            pltpu.VMEM((2, 2, w, 128), F32),
            pltpu.VMEM((2, w, w), F32),
            pltpu.VMEM((4, quart, w), F32),
            pltpu.VMEM((2, modes * w, 2 * w), BF),
            pltpu.VMEM((modes, 4, w, w), BF),
            pltpu.VMEM((2, modes * w, w), F32),
            pltpu.VMEM((modes, 4, half, w), F32),
            pltpu.VMEM((2, modes * w, w), F32),
            pltpu.SemaphoreType.DMA((2, 2)),
            pltpu.SemaphoreType.DMA((8,)),
        ],
        compiler_params=pltpu.CompilerParams(vmem_limit_bytes=60 << 20),
        cost_estimate=pl.CostEstimate(flops=10**11, bytes_accessed=10**7, transcendentals=0),
    )


MESH = pl.DeviceIdType.MESH


def place():
    return lax.axis_index("row"), lax.axis_index("col"), lax.axis_index("mode")


def device(r, c, m):
    return {"row": r, "col": c, "mode": m}


def remote(src, dst, send, recv, to):
    return pltpu.make_async_remote_copy(
        src_ref=src, dst_ref=dst, send_sem=send, recv_sem=recv, device_id=to, device_id_type=MESH
    )


def greet(to):
    pl.semaphore_signal(pltpu.get_barrier_semaphore(), inc=1, device_id=to, device_id_type=MESH)


class Quarters:
    def __init__(self, src, dst, modes, rows, r, c, chunks, sems):
        me_r, me_c, m = place()
        self.m, self.modes, self.chunks = m, modes, chunks
        self.rows = rows // modes // chunks
        self.src, self.dst = src, dst
        self.ys, self.yr, self.zs, self.zr, self.ts, self.tr = sems
        self.peer = device(r, c, m)
        self.next = device(me_r, me_c, lax.rem(m + 1, modes))
        self.prev = device(me_r, me_c, lax.rem(m + modes - 1, modes))

    def part(self, ref, owner, i):
        at = pl.multiple_of((owner * self.chunks + i) * self.rows, self.rows)
        return ref.at[:, pl.ds(at, self.rows), :]

    def first(self, i):
        mine = self.part(self.src, self.m, i)
        return remote(mine, self.part(self.dst, self.m, i), self.ys.at[i], self.yr.at[i], self.peer)

    def ring(self, i, way):
        mine = self.part(self.dst, self.m, i)
        return remote(mine, mine, self.zs.at[way, i], self.zr.at[way, i], self.next if way == 0 else self.prev)

    def way(self, i):
        return 0 if i < self.chunks // 2 else 1

    def relay(self, i):
        back = self.modes - 1 if self.way(i) == 0 else 1
        block = self.part(self.dst, lax.rem(self.m + back, self.modes), i)
        return remote(block, block, self.ts.at[i], self.tr.at[i], self.next if self.way(i) == 0 else self.prev)

    def start(self):
        for i in range(self.chunks):
            self.first(i).start()

    def sent(self):
        for i in range(self.chunks):
            self.first(i).wait_send()

    def take(self, some=None):
        for i in range(self.chunks) if some is None else some:
            self.first(i).wait_recv()
            self.ring(i, 0).start()
            self.ring(i, 1).start()

    def turn(self):
        for i in range(self.chunks):
            self.ring(i, self.way(i)).wait_recv()
            self.relay(i).start()

    def finish(self):
        for i in range(self.chunks):
            self.ring(i, 1 - self.way(i)).wait_recv()
            self.relay(i).wait_recv()
        for i in range(self.chunks):
            self.ring(i, 0).wait_send()
            self.ring(i, 1).wait_send()
            self.relay(i).wait_send()


STRIP, EDGE = 4, 2


def quarter_sems(chunks):
    one = pltpu.SemaphoreType.DMA((chunks,))
    two = pltpu.SemaphoreType.DMA((2, chunks))
    return [one, one, two, two, one, one]


def when(cond, *steps):
    @pl.when(cond)
    def _():
        for step in steps:
            step()


def make_spread(window, modes, tile_rows, tile_cols, rows_n, cols_n):
    w = window

    def kernel(tile, probe, right, low, diag, gathered, *sems):
        quarter, (one_s, one_r, p_s, p_r, x_s, x_r, own_sem) = sems[:6], sems[6:]
        r, c, m = place()
        core = lax.rem(c, 2)
        other = c + 1 - 2 * core
        odd, even = core == 1, core == 0
        has_left, has_right = c > 0, c < cols_n - 1
        top = tile.at[:, pl.ds(0, w), :]

        for k in range(1, modes):
            greet(device(r, c, lax.rem(m + k, modes)))
        greet(device(r, other, m))
        greet(device(rows_n - 1 - r, c, m))
        count = modes + 1
        away = jnp.where(odd, jnp.minimum(c + 1, cols_n - 1), jnp.maximum(c - 1, 0))
        has_away = jnp.where(odd, has_right, has_left)

        @pl.when(has_away)
        def _():
            greet(device(r, away, m))

        has_diag = has_away & jnp.where(odd, r == 0, r == 1)

        @pl.when(has_diag)
        def _():
            greet(device(rows_n - 1 - r, away, m))

        pl.semaphore_wait(
            pltpu.get_barrier_semaphore(),
            count + has_away.astype(jnp.int32) + has_diag.astype(jnp.int32),
        )

        strip = Quarters(tile, right, modes, tile_rows, r, away, STRIP, quarter)
        whole = remote(tile, right, one_s.at[0], one_r.at[0], device(r, other, m))
        down = remote(top, low, one_s.at[1], one_r.at[1], device(rows_n - 1 - r, c, m))
        corner = remote(top, diag, one_s.at[2], one_r.at[2], device(rows_n - 1 - r, away, m))
        corner_on = remote(low, diag, one_s.at[2], one_r.at[2], device(r, other, m))

        def probe_copy(k):
            half = gathered.at[pl.ds(core, 1), pl.ds(m, 1)]
            return remote(
                probe.at[pl.ds(core, 1)], half, p_s.at[k], p_r.at[k], device(r, c, lax.rem(m + k, modes))
            )

        def probe_pass(k):
            half = gathered.at[pl.ds(core, 1), pl.ds(lax.rem(m + modes - k, modes), 1)]
            return remote(half, half, x_s.at[k], x_r.at[k], device(r, other, m))

        @pl.when(even & has_left)
        def _():
            strip.start()

        @pl.when(r == 1)
        def _():
            down.start()

        @pl.when(even & has_diag)
        def _():
            corner.start()

        for k in (1, 3, 2):
            probe_copy(k).start()

        @pl.when(odd)
        def _():
            whole.start()

        keep = pltpu.make_async_copy(probe, gathered.at[:, pl.ds(m, 1)], own_sem)
        keep.start()

        @pl.when(odd & has_right)
        def _():
            strip.take()

        @pl.when(r == 0)
        def _():
            down.wait_recv()

        @pl.when(odd & (r == 0))
        def _():
            corner_on.start()

        for k in (1, 3, 2):
            probe_copy(k).wait_recv()
            probe_pass(k).start()

        @pl.when(odd & has_right)
        def _():
            strip.turn()
            strip.finish()

        @pl.when(odd & has_diag)
        def _():
            corner.wait_recv()

        @pl.when(even)
        def _():
            whole.wait_recv()

        @pl.when(even & (r == 0))
        def _():
            corner_on.wait_recv()

        for k in (1, 3, 2):
            probe_pass(k).wait_recv()
            probe_pass(k).wait_send()
            probe_copy(k).wait_send()
        keep.wait()

        @pl.when(odd)
        def _():
            whole.wait_send()

        @pl.when(odd & (r == 0))
        def _():
            corner_on.wait_send()

        @pl.when(even & has_left)
        def _():
            strip.sent()

        @pl.when(r == 1)
        def _():
            down.wait_send()

        @pl.when(even & has_diag)
        def _():
            corner.wait_send()

    hbm = pl.BlockSpec(memory_space=pl.ANY)
    shape = jax.ShapeDtypeStruct
    return pl.pallas_call(
        kernel,
        name="spread",
        in_specs=[hbm, hbm],
        out_specs=[hbm] * 4,
        out_shape=[
            shape((2, tile_rows, tile_cols), F32),
            shape((2, w, tile_cols), F32),
            shape((2, w, tile_cols), F32),
            shape((2, modes, w, w), F32),
        ],
        scratch_shapes=quarter_sems(STRIP) + [pltpu.SemaphoreType.DMA((3,))] * 2
        + [pltpu.SemaphoreType.DMA((modes,))] * 4 + [pltpu.SemaphoreType.DMA],
        compiler_params=pltpu.CompilerParams(collective_id=0, has_side_effects=True),
    )


def make_collect(window, modes, tile_rows, tile_cols, rows_n, cols_n):
    w = window
    chips = rows_n * cols_n // 2
    piece = 2 * w // chips

    def kernel(g_right, g_low, g_diag, pg, right, low, diag, total, *sems):
        strip_sems = sems[:6]
        one_s, one_r, d_s, d_r, e_s, e_r, x_s, x_r, y_s, y_r, a_s, a_r, b_s, b_r, in_sem, pair, got, mine = sems[6:]
        r, c, m = place()
        core = lax.rem(c, 2)
        chip = r * (cols_n // 2) + c // 2
        other = c + 1 - 2 * core
        odd, even = core == 1, core == 0
        away = jnp.where(odd, jnp.minimum(c + 1, cols_n - 1), jnp.maximum(c - 1, 0))
        has_away = jnp.where(odd, c < cols_n - 1, c > 0)
        flip = rows_n - 1 - r
        over = jnp.where(r == 0, jnp.minimum(c + 1, cols_n - 1), jnp.maximum(c - 1, 0))
        has_over = jnp.where(r == 0, c < cols_n - 1, c > 0)

        def partner(k):
            p = lax.rem(chip + k, chips)
            return device(p // (cols_n // 2), 2 * lax.rem(p, cols_n // 2) + core, m)

        def hello(k, carry):
            greet(partner(k))
            return carry

        greet(device(r, other, m))
        for k in (1, modes - 1):
            greet(device(r, c, lax.rem(m + k, modes)))
        when(has_away, lambda: greet(device(r, away, m)))
        when(has_over, lambda: greet(device(flip, over, m)))
        when(even, lambda: greet(device(flip, c, m)))
        when(odd, lambda: lax.fori_loop(1, chips, hello, 0))
        pl.semaphore_wait(
            pltpu.get_barrier_semaphore(),
            3 + jnp.where(odd, chips - 1, 1) + has_away.astype(jnp.int32) + has_over.astype(jnp.int32),
        )

        strip = Quarters(g_right, right, modes, tile_rows, r, away, STRIP, strip_sems)
        down = remote(g_low, low, d_s, d_r, device(flip, c, m))
        corner = remote(g_diag, diag, e_s, e_r, device(flip, over, m))
        whole = remote(g_right, right, one_s, one_r, device(r, other, m))
        swap = remote(pg, pair.at[0], x_s, x_r, device(r, other, m))
        own = pltpu.make_async_copy(pg, pair.at[1], in_sem)
        at_chip = pl.ds(pl.multiple_of(chip * piece, piece), piece)
        rest = got.at[pl.ds(1, chips - 1)]
        many = total.at[pl.ds(0, (chips - 1) * piece), :]
        keep = pltpu.make_async_copy(mine, total.at[at_chip, :], in_sem)
        give = remote(total, total, y_s, y_r, device(r, other, m))

        def scatter_go(k, carry):
            p = lax.rem(chip + k, chips)
            rows = pl.ds(pl.multiple_of(p * piece, piece), piece)
            remote(pair.at[1, rows, :], got.at[k], a_s, a_r, partner(k)).start()
            return carry

        def share_go(k, carry):
            remote(mine, total.at[at_chip, :], b_s, b_r, partner(k)).start()
            return carry

        def add(k, acc):
            return acc + got[k]

        def sum_pair():
            own.wait()
            swap.wait_recv()
            pair[1] = pair[0] + pair[1]
            lax.fori_loop(1, chips, scatter_go, 0)

        def sum_plane():
            pltpu.make_async_copy(rest, rest, a_r).wait()
            mine[...] = lax.fori_loop(1, chips, add, pair[1, at_chip, :]) * (1.0 / 16.0)
            keep.start()
            lax.fori_loop(1, chips, share_go, 0)

        def sum_give():
            keep.wait()
            pltpu.make_async_copy(many, many, b_r).wait()
            give.start()

        def sum_end():
            pltpu.make_async_copy(rest, rest, a_s).wait()
            pltpu.make_async_copy(many, many, b_s).wait()
            give.wait_send()

        when(even, swap.start)
        when(odd, own.start)
        when(odd & has_away, strip.start)
        when(r == 0, down.start)
        when((r == 0) & has_over, corner.start)
        when(even, whole.start)
        when(odd, sum_pair)
        when(even & has_away, strip.take)
        when(odd, sum_plane)
        when(even & has_away, strip.turn)
        when(odd, sum_give)
        when(even & has_away, strip.finish)
        when(r == 1, down.wait_recv)
        when((r == 1) & has_over, corner.wait_recv)
        when(odd, whole.wait_recv)
        when(even, give.wait_recv)
        when(even, swap.wait_send)
        when(odd, sum_end)
        when(odd & has_away, strip.sent)
        when(r == 0, down.wait_send)
        when((r == 0) & has_over, corner.wait_send)
        when(even, whole.wait_send)

    hbm = pl.BlockSpec(memory_space=pl.ANY)
    shape = jax.ShapeDtypeStruct
    dma = pltpu.SemaphoreType.DMA
    return pl.pallas_call(
        kernel,
        name="collect",
        in_specs=[hbm] * 4,
        out_specs=[hbm] * 4,
        out_shape=[
            shape((2, tile_rows, tile_cols), F32),
            shape((2, w, tile_cols), F32),
            shape((2, w, tile_cols), F32),
            shape((2 * w, w), F32),
        ],
        scratch_shapes=quarter_sems(STRIP) + [dma] * 15
        + [pltpu.VMEM((2, 2 * w, w), F32), pltpu.VMEM((chips, piece, w), F32), pltpu.VMEM((piece, w), F32)],
        compiler_params=pltpu.CompilerParams(collective_id=1, has_side_effects=True),
    )


def make_finish(window, tile_rows, tile_cols):
    w = window
    blocks = tile_rows // w

    def kernel(own, strip, low, diag, total, grad, probe, a, b, e, s_a, s_b, s_e, s_out):
        r, c, m = place()
        below, inner = r > 0, c > 0

        def rows(k):
            return pl.ds(k * w, w)

        loads = [
            [
                pltpu.make_async_copy(own.at[:, rows(k), :], a.at[:, rows(k), :], s_a.at[k]),
                pltpu.make_async_copy(strip.at[:, rows(k), :], b.at[:, rows(k), :], s_b.at[k]),
            ]
            for k in range(blocks)
        ]
        edges = [pltpu.make_async_copy(src, e.at[n], s_e.at[n]) for n, src in enumerate((low, diag, total))]
        for k in reversed(range(blocks)):
            for copy in loads[k]:
                copy.start()
        for copy in edges:
            copy.start()
        stores = [pltpu.make_async_copy(a.at[:, rows(k), :], grad.at[:, rows(k), :], s_out.at[k]) for k in range(blocks)]

        def add(k, x):
            for part in range(2):
                a[part, k * w:k * w + w, :] += x[part]

        for k in reversed(range(blocks)):
            for copy in loads[k]:
                copy.wait()
            when(inner, lambda: add(k, b.at[:, rows(k), :]))
            if k == 0:
                for copy in edges:
                    copy.wait()
                when(below, lambda: add(0, e.at[0]))
                when(below & inner, lambda: add(0, e.at[1]))
                last = pltpu.make_async_copy(e.at[2], probe, s_out.at[blocks])
                last.start()
            stores[k].start()
        for copy in stores + [last]:
            copy.wait()

    hbm = pl.BlockSpec(memory_space=pl.ANY)
    dma = pltpu.SemaphoreType.DMA
    tile = (2, tile_rows, tile_cols)
    return pl.pallas_call(
        kernel,
        name="finish",
        in_specs=[hbm] * 5,
        out_specs=[hbm] * 2,
        out_shape=[jax.ShapeDtypeStruct(tile, F32), jax.ShapeDtypeStruct((2, w, w), F32)],
        scratch_shapes=[
            pltpu.VMEM(tile, F32), pltpu.VMEM(tile, F32), pltpu.VMEM((3, 2, w, w), F32),
            dma((blocks,)), dma((blocks,)), dma((3,)), dma((blocks + 1,)),
        ],
        compiler_params=pltpu.CompilerParams(vmem_limit_bytes=60 << 20),
    )


def per_device(object_slab, probe_modes, amplitudes, scan_counts, scan_positions):
    window = probe_modes.shape[-1]
    tile_rows, tile_cols = object_slab.shape[1:]
    slots = amplitudes.shape[0]
    modes, cols_n, rows_n = (lax.axis_size(a) for a in ("mode", "col", "row"))
    sizes = (window, modes, tile_rows, tile_cols, rows_n, cols_n)
    right, low, diag, probe = make_spread(*sizes)(object_slab, probe_modes)
    consts = [jnp.asarray(t) for t in tables(window)]
    compute = make_compute(window, modes, slots, tile_rows, tile_cols, cols_n)
    g_own, g_right, g_low, g_diag, pg, shift = compute(
        scan_positions, scan_counts, object_slab, right, low, diag, probe, amplitudes, *consts
    )
    from_left, from_up, from_diag, total = make_collect(*sizes)(
        g_right, g_low, g_diag, pg.reshape(2 * window, window)
    )
    grad, probe_grad = make_finish(window, tile_rows, tile_cols)(
        g_own, from_left, from_up, from_diag, total.reshape(2, window, window)
    )
    return (grad, probe_grad.reshape(2, 1, window, window), shift)


def solution(mesh):
    in_specs = (
        P(None, "row", "col"),
        P(None, "mode", None, None),
        P(("row", "col"), None, None),
        P(),
        P(None, ("row", "col")),
    )
    out_specs = (P(None, "row", "col"), P(None, "mode", None, None), P(None, ("row", "col")))
    return jax.shard_map(
        per_device, mesh=mesh, in_specs=in_specs, out_specs=out_specs, check_vma=False
    )
```

```python
import math
import functools
import numpy as np
import jax
import jax.numpy as jnp
from jax import lax
from jax.experimental import pallas as pl
from jax.experimental.pallas import tpu as pltpu
from jax.sharding import PartitionSpec as P

BF = jnp.bfloat16
F32 = jnp.float32
BATCH = 4
CH = 32


def hi_lo(x):
    hi = x.astype(BF)
    lo = (x - hi.astype(F32)).astype(BF)
    return hi, lo


def halves(table):
    table = table.astype(np.float32)
    hi = table.astype(BF)
    return hi, (table - hi.astype(np.float32)).astype(BF)


def angles(window, radix, q):
    part = window // radix
    n, j = np.arange(part)[:, None], np.arange(part)[None, :]
    angle = 2.0 * math.pi * ((n * (radix * j + q)) % window) / window
    return np.cos(angle) / math.sqrt(window), np.sin(angle) / math.sqrt(window)


def tables(window):
    right_f, right_i, left_f, left_i = [], [], [], []
    for q in range(2):
        c, s = angles(window, 2, q)
        for table, into in ((np.block([[c, -s], [s, c]]), right_f), (np.block([[c.T, s.T], [-s.T, c.T]]), right_i)):
            hi, lo = halves(table)
            into.append(np.concatenate([hi, lo, hi], axis=0))
    for q in range(4):
        c, s = angles(window, 4, q)
        for table, into in ((np.block([[c.T, s.T], [-s.T, c.T]]), left_f), (np.block([[c, -s], [s, c]]), left_i)):
            hi, lo = halves(table)
            top = np.concatenate([hi, hi], axis=1)
            into.append(np.concatenate([top, np.concatenate([lo, np.zeros_like(lo)], axis=1)], axis=0))
    order = np.concatenate([np.arange(0, window, 2), np.arange(1, window, 2)])
    shuffle = np.zeros((window, window), np.float32)
    shuffle[order, np.arange(window)] = 1.0
    return np.stack(right_f), np.stack(right_i), np.stack(left_f), np.stack(left_i), shuffle.astype(BF)


def cat(parts, axis):
    return jnp.concatenate(parts, axis=axis)


def mm(a, b):
    return jnp.dot(a, b, preferred_element_type=F32)


def make_compute(window, modes, slots, tile_rows, tile_cols, cols_n):
    w, half, quart = window, window // 2, window // 4
    ch = CH
    ext_rows, ext_cols = tile_rows + w, tile_cols + w

    def kernel(positions, counts, own, right, low, diag, probe, amps, rf, ri, lf, li, shuffle,
               g_own, g_right, g_low, g_diag, pg, along,
               ext, grad, amp_buf, win, fac, lhs, rhs, mid, far, near, amp_sem, sem):
        row_id, col_id, mine = place()
        count = counts[row_id * cols_n + col_id]
        def quarters(whole, parts):
            pairs = []
            for k in range(4):
                for t in range(2):
                    down = slice(tile_rows, ext_rows) if k >= 2 else slice(0, tile_rows)
                    pairs.append((whole.at[2 * (k % 2) + t, :, down, :], parts[k].at[:, :, 128 * t:128 * t + 128]))
            return pairs

        loads = [
            pltpu.make_async_copy(part, inside, sem.at[k])
            for k, (inside, part) in enumerate(quarters(ext, (own, right, low, diag)))
        ]
        for copy in loads:
            copy.start()

        def amp_copies(slot, place):
            return [
                pltpu.make_async_copy(
                    amps.at[slot, :, 128 * t:128 * t + 128], amp_buf.at[place, t], amp_sem.at[place, t]
                )
                for t in range(2)
            ]

        for copy in amp_copies(0, 0):
            copy.start()

        def clear(i, carry):
            at = pl.multiple_of(i * ch, ch)
            for c in range(2):
                for t in range(4):
                    grad[t, c, pl.ds(at, ch), :] = jnp.zeros((ch, 128), F32)
            return carry

        lax.fori_loop(0, ext_rows // ch, clear, 0)
        pg[...] = jnp.zeros(pg.shape, F32)

        def no_shift(i, carry):
            along[0, i] = 0.0
            along[1, i] = 0.0
            return carry

        lax.fori_loop(0, slots, no_shift, 0)
        for copy in loads:
            copy.wait()

        def put_lhs(parity, at, x):
            hi, lo = hi_lo(x)
            lhs[parity, at:at + ch, :w] = hi
            lhs[parity, at:at + ch, w:] = lo

        def put_rhs(m, q, at, x):
            hi, lo = hi_lo(x)
            rhs[m, q, at:at + ch, :] = hi
            rhs[m, q, half + at:half + at + ch, :] = lo

        def right_apply(m, table, into):
            rows = slice(m * w, (m + BATCH) * w)
            for parity in range(2):
                hi, lo = lhs[parity, rows, :w], lhs[parity, rows, w:]
                into[parity, rows, :] = mm(cat([hi, hi, lo], 1), table[parity])

        def left_apply(m, q, table):
            both = mm(table[q], rhs[m, q])
            return both[:half] + both[half:]

        def forward_rows(m):
            for r in range(0, quart, ch):
                y = [[], [], [], []]
                for parity in range(2):
                    x = [mid[parity, m * w + p * quart + r:m * w + p * quart + r + ch, :] for p in range(4)]
                    a, b, c, d = x[0] + x[2], x[1] + x[3], x[0] - x[2], x[1] - x[3]
                    y[0].append(a + b)
                    y[2].append(a - b)
                    turned = cat([d[:, half:], -d[:, :half]], 1)
                    y[1].append(c + turned)
                    y[3].append(c - turned)
                for q in range(4):
                    e, o = y[q]
                    put_rhs(m, q, r, cat([e[:, :half], o[:, :half]], 1))
                    put_rhs(m, q, quart + r, cat([e[:, half:], o[:, half:]], 1))
            for q in range(4):
                far[m, q] = left_apply(m, q, lf)

        def inverse_rows(m):
            for q in range(4):
                for r in range(0, quart, ch):
                    f = fac[q, r:r + ch, :]
                    for at in (r, quart + r):
                        put_rhs(m, q, at, f * far[m, q, at:at + ch, :])
            for q in range(4):
                far[m, q] = left_apply(m, q, li)
            for r in range(0, quart, ch):
                re = [far[m, q, r:r + ch, :] for q in range(4)]
                im = [far[m, q, quart + r:quart + r + ch, :] for q in range(4)]
                are, aim, bre, bim = re[0] + re[2], im[0] + im[2], re[1] + re[3], im[1] + im[3]
                cre, cim, dre, dim = re[0] - re[2], im[0] - im[2], re[1] - re[3], im[1] - im[3]
                outs = (
                    (are + bre, aim + bim), (cre - dim, cim + dre),
                    (are - bre, aim - bim), (cre + dim, cim - dre),
                )
                for p, (xre, xim) in enumerate(outs):
                    for parity in range(2):
                        cols = slice(parity * half, parity * half + half)
                        put_lhs(parity, m * w + p * quart + r, cat([xre[:, cols], xim[:, cols]], 1))

        def do_slot(slot, carry):
            row = positions[0, slot] - row_id * tile_rows
            col = positions[1, slot] - col_id * tile_cols
            tile_at = col // 128
            off = lax.rem(col, 128)
            back = lax.rem(w + 128 - off, w + 128)
            place_at = lax.rem(slot, 2)
            for copy in amp_copies(slot, place_at):
                copy.wait()

            @pl.when(slot + 1 < count)
            def _():
                for copy in amp_copies(slot + 1, 1 - place_at):
                    copy.start()

            for c in range(2):
                for r in range(0, w, ch):
                    wide = cat([ext[tile_at + t, c, pl.ds(row + r, ch), :] for t in range(3)], 1)
                    win[c, r:r + ch, :] = pltpu.roll(wide, back, 1)[:, :w]

            for q in range(4):
                a = cat([amp_buf[place_at, t, pl.ds(q, quart, stride=4), :] for t in range(2)], 1)
                a0, a1 = hi_lo(a)
                a2 = (a - a0.astype(F32) - a1.astype(F32)).astype(BF)
                stack = mm(cat([a0, a1, a2], 0), shuffle[...])
                fac[q] = stack[:quart] + stack[quart:2 * quart] + stack[2 * quart:]

            for m in range(modes):
                for r in range(0, w, ch):
                    vre, vim = win[0, r:r + ch, :], win[1, r:r + ch, :]
                    pre, pim = probe[0, m, r:r + ch, :], probe[1, m, r:r + ch, :]
                    are = pre * vre - pim * vim
                    aim = pre * vim + pim * vre
                    for parity in range(2):
                        if parity == 0:
                            x = cat([are[:, :half] + are[:, half:], aim[:, :half] + aim[:, half:]], 1)
                        else:
                            x = cat([are[:, :half] - are[:, half:], aim[:, :half] - aim[:, half:]], 1)
                        put_lhs(parity, m * w + r, x)
                if (m + 1) % BATCH == 0:
                    right_apply(m + 1 - BATCH, rf, mid)
                    for n in range(m + 1 - BATCH, m + 1):
                        forward_rows(n)

            for q in range(4):
                for r in range(0, quart, ch):
                    total = None
                    for m in range(modes):
                        re = far[m, q, r:r + ch, :]
                        im = far[m, q, quart + r:quart + r + ch, :]
                        term = re * re + im * im
                        total = term if total is None else total + term
                    fac[q, r:r + ch, :] = 0.25 * (1.0 - fac[q, r:r + ch, :] * lax.rsqrt(total + 0.5))

            for m in range(modes):
                inverse_rows(m)
                if (m + 1) % BATCH == 0:
                    right_apply(m + 1 - BATCH, ri, near)

            rows_sum = jnp.zeros((8, w), F32)
            cols_sum = jnp.zeros((8, w), F32)
            lanes = lax.broadcasted_iota(jnp.int32, (ch, w), 1)
            inner = (lanes >= 1) & (lanes <= w - 2)

            def near_of(m, r):
                at = m * w + r
                if not isinstance(m, int):
                    at = pl.multiple_of(at, ch)
                e, o = near[0, pl.ds(at, ch), :], near[1, pl.ds(at, ch), :]
                s, d = e + o, e - o
                return cat([s[:, :half], d[:, :half]], 1), cat([s[:, half:], d[:, half:]], 1)

            for r in range(0, w, ch):
                gre = gim = None
                for m in range(modes):
                    nre, nim = near_of(m, r)
                    pre, pim = probe[0, m, r:r + ch, :], probe[1, m, r:r + ch, :]
                    tre = pre * nre + pim * nim
                    tim = pre * nim - pim * nre
                    gre = tre if gre is None else gre + tre
                    gim = tim if gim is None else gim + tim
                for c, g in ((0, gre), (1, gim)):
                    spread = pltpu.roll(cat([g, jnp.zeros((ch, 128), F32)], 1), off, 1)
                    for t in range(3):
                        grad[tile_at + t, c, pl.ds(row + r, ch), :] += spread[:, 128 * t:128 * t + 128]
                vre, vim = win[0, r:r + ch, :], win[1, r:r + ch, :]
                nre, nim = near_of(mine, r)
                pg[0, r:r + ch, :] += vre * nre + vim * nim
                pg[1, r:r + ch, :] += vre * nim - vim * nre
                dre = pltpu.roll(vre, w - 1, 1) - pltpu.roll(vre, 1, 1)
                dim = pltpu.roll(vim, w - 1, 1) - pltpu.roll(vim, 1, 1)
                t = jnp.where(inner, gre * dre + gim * dim, 0.0)
                cols_sum = cols_sum + jnp.sum(t.reshape(ch // 8, 8, w), axis=0)
                lo_r, hi_r = max(r, 1), min(r + ch, w - 1)
                up = [ext_rows_slice(win, c, r + 1, ch, w) for c in range(2)]
                dn = [ext_rows_slice(win, c, r - 1, ch, w) for c in range(2)]
                t = gre * (up[0] - dn[0]) + gim * (up[1] - dn[1])
                if lo_r != r or hi_r != r + ch:
                    idx = lax.broadcasted_iota(jnp.int32, (ch, w), 0) + r
                    t = jnp.where((idx >= lo_r) & (idx < hi_r), t, 0.0)
                rows_sum = rows_sum + jnp.sum(t.reshape(ch // 8, 8, w), axis=0)
            along[0, slot] = jnp.sum(rows_sum) * (0.5 / w)
            along[1, slot] = jnp.sum(cols_sum) * (0.5 / w)
            return carry

        def ext_rows_slice(ref, c, start, size, width):
            if start < 0:
                return cat([ref[c, 0:1, :], ref[c, 0:size - 1, :]], 0)
            if start + size > w:
                return cat([ref[c, start:w, :], ref[c, w - 1:w, :]], 0)
            return ref[c, start:start + size, :]

        lax.fori_loop(0, count, do_slot, 0)
        stores = [
            pltpu.make_async_copy(inside, part, sem.at[k])
            for k, (inside, part) in enumerate(quarters(grad, (g_own, g_right, g_low, g_diag)))
        ]
        for copy in stores:
            copy.start()
        for copy in stores:
            copy.wait()

    hbm = pl.BlockSpec(memory_space=pl.ANY)
    vmem = pl.BlockSpec(memory_space=pltpu.VMEM)
    smem = pl.BlockSpec(memory_space=pltpu.SMEM)
    shape = jax.ShapeDtypeStruct
    return pl.pallas_call(
        kernel,
        name="slots",
        in_specs=[smem, smem, hbm, hbm, hbm, hbm, vmem, hbm, vmem, vmem, vmem, vmem, vmem],
        out_specs=[hbm, hbm, hbm, hbm, vmem, smem],
        out_shape=[
            shape((2, tile_rows, tile_cols), F32),
            shape((2, tile_rows, w), F32),
            shape((2, w, tile_cols), F32),
            shape((2, w, w), F32),
            shape((2, w, w), F32),
            shape((2, slots), F32),
        ],
        scratch_shapes=[
            pltpu.VMEM((ext_cols // 128, 2, ext_rows, 128), F32),
            pltpu.VMEM((ext_cols // 128, 2, ext_rows, 128), F32),
            pltpu.VMEM((2, 2, w, 128), F32),
            pltpu.VMEM((2, w, w), F32),
            pltpu.VMEM((4, quart, w), F32),
            pltpu.VMEM((2, modes * w, 2 * w), BF),
            pltpu.VMEM((modes, 4, w, w), BF),
            pltpu.VMEM((2, modes * w, w), F32),
            pltpu.VMEM((modes, 4, half, w), F32),
            pltpu.VMEM((2, modes * w, w), F32),
            pltpu.SemaphoreType.DMA((2, 2)),
            pltpu.SemaphoreType.DMA((8,)),
        ],
        compiler_params=pltpu.CompilerParams(vmem_limit_bytes=60 << 20),
        cost_estimate=pl.CostEstimate(flops=10**11, bytes_accessed=10**7, transcendentals=0),
    )


MESH = pl.DeviceIdType.MESH


def place():
    return lax.axis_index("row"), lax.axis_index("col"), lax.axis_index("mode")


def device(r, c, m):
    return {"row": r, "col": c, "mode": m}


def remote(src, dst, send, recv, to):
    return pltpu.make_async_remote_copy(
        src_ref=src, dst_ref=dst, send_sem=send, recv_sem=recv, device_id=to, device_id_type=MESH
    )


def greet(to):
    pl.semaphore_signal(pltpu.get_barrier_semaphore(), inc=1, device_id=to, device_id_type=MESH)


class Quarters:
    def __init__(self, src, dst, modes, rows, r, c, chunks, sems):
        me_r, me_c, m = place()
        self.m, self.modes, self.chunks = m, modes, chunks
        self.rows = rows // modes // chunks
        self.src, self.dst = src, dst
        self.ys, self.yr, self.zs, self.zr, self.ts, self.tr = sems
        self.peer = device(r, c, m)
        self.next = device(me_r, me_c, lax.rem(m + 1, modes))
        self.prev = device(me_r, me_c, lax.rem(m + modes - 1, modes))

    def part(self, ref, owner, i):
        at = pl.multiple_of((owner * self.chunks + i) * self.rows, self.rows)
        return ref.at[:, pl.ds(at, self.rows), :]

    def first(self, i):
        mine = self.part(self.src, self.m, i)
        return remote(mine, self.part(self.dst, self.m, i), self.ys.at[i], self.yr.at[i], self.peer)

    def ring(self, i, way):
        mine = self.part(self.dst, self.m, i)
        return remote(mine, mine, self.zs.at[way, i], self.zr.at[way, i], self.next if way == 0 else self.prev)

    def way(self, i):
        return 0 if i < self.chunks // 2 else 1

    def relay(self, i):
        back = self.modes - 1 if self.way(i) == 0 else 1
        block = self.part(self.dst, lax.rem(self.m + back, self.modes), i)
        return remote(block, block, self.ts.at[i], self.tr.at[i], self.next if self.way(i) == 0 else self.prev)

    def start(self):
        for i in range(self.chunks):
            self.first(i).start()

    def sent(self):
        for i in range(self.chunks):
            self.first(i).wait_send()

    def take(self, some=None):
        for i in range(self.chunks) if some is None else some:
            self.first(i).wait_recv()
            self.ring(i, 0).start()
            self.ring(i, 1).start()

    def turn(self):
        for i in range(self.chunks):
            self.ring(i, self.way(i)).wait_recv()
            self.relay(i).start()

    def finish(self):
        for i in range(self.chunks):
            self.ring(i, 1 - self.way(i)).wait_recv()
            self.relay(i).wait_recv()
        for i in range(self.chunks):
            self.ring(i, 0).wait_send()
            self.ring(i, 1).wait_send()
            self.relay(i).wait_send()


STRIP, EDGE = 4, 2


def quarter_sems(chunks):
    one = pltpu.SemaphoreType.DMA((chunks,))
    two = pltpu.SemaphoreType.DMA((2, chunks))
    return [one, one, two, two, one, one]


def when(cond, *steps):
    @pl.when(cond)
    def _():
        for step in steps:
            step()


def make_spread(window, modes, tile_rows, tile_cols, rows_n, cols_n):
    w = window

    def kernel(tile, probe, right, low, diag, gathered, *sems):
        quarter, (one_s, one_r, p_s, p_r, x_s, x_r, own_sem) = sems[:6], sems[6:]
        r, c, m = place()
        core = lax.rem(c, 2)
        other = c + 1 - 2 * core
        odd, even = core == 1, core == 0
        has_left, has_right = c > 0, c < cols_n - 1
        top = tile.at[:, pl.ds(0, w), :]

        for k in range(1, modes):
            greet(device(r, c, lax.rem(m + k, modes)))
        greet(device(r, other, m))
        greet(device(rows_n - 1 - r, c, m))
        count = modes + 1
        away = jnp.where(odd, jnp.minimum(c + 1, cols_n - 1), jnp.maximum(c - 1, 0))
        has_away = jnp.where(odd, has_right, has_left)

        @pl.when(has_away)
        def _():
            greet(device(r, away, m))

        has_diag = has_away & jnp.where(odd, r == 0, r == 1)

        @pl.when(has_diag)
        def _():
            greet(device(rows_n - 1 - r, away, m))

        pl.semaphore_wait(
            pltpu.get_barrier_semaphore(),
            count + has_away.astype(jnp.int32) + has_diag.astype(jnp.int32),
        )

        strip = Quarters(tile, right, modes, tile_rows, r, away, STRIP, quarter)
        whole = remote(tile, right, one_s.at[0], one_r.at[0], device(r, other, m))
        down = remote(top, low, one_s.at[1], one_r.at[1], device(rows_n - 1 - r, c, m))
        corner = remote(top, diag, one_s.at[2], one_r.at[2], device(rows_n - 1 - r, away, m))
        corner_on = remote(low, diag, one_s.at[2], one_r.at[2], device(r, other, m))

        def probe_copy(k):
            half = gathered.at[pl.ds(core, 1), pl.ds(m, 1)]
            return remote(
                probe.at[pl.ds(core, 1)], half, p_s.at[k], p_r.at[k], device(r, c, lax.rem(m + k, modes))
            )

        def probe_pass(k):
            half = gathered.at[pl.ds(core, 1), pl.ds(lax.rem(m + modes - k, modes), 1)]
            return remote(half, half, x_s.at[k], x_r.at[k], device(r, other, m))

        @pl.when(even & has_left)
        def _():
            strip.start()

        @pl.when(r == 1)
        def _():
            down.start()

        @pl.when(even & has_diag)
        def _():
            corner.start()

        step = jnp.where(even, 1, modes - 1)
        block = gathered.at[pl.ds(core, 1), pl.ds(lax.rem(m + modes - step, modes), 1)]
        relay = remote(block, block, p_s.at[2], p_r.at[2], device(r, c, lax.rem(m + step, modes)))
        for k in (1, modes - 1):
            probe_copy(k).start()

        @pl.when(odd)
        def _():
            whole.start()

        keep = pltpu.make_async_copy(probe, gathered.at[:, pl.ds(m, 1)], own_sem)
        keep.start()

        @pl.when(odd & has_right)
        def _():
            strip.take()

        @pl.when(r == 0)
        def _():
            down.wait_recv()

        @pl.when(odd & (r == 0))
        def _():
            corner_on.start()

        for k in (1, modes - 1):
            probe_copy(k).wait_recv()
        relay.start()
        for k in (1, modes - 1):
            probe_pass(k).start()

        @pl.when(odd & has_right)
        def _():
            strip.turn()

        relay.wait_recv()
        probe_pass(2).start()

        @pl.when(odd & has_right)
        def _():
            strip.finish()

        @pl.when(odd & has_diag)
        def _():
            corner.wait_recv()

        @pl.when(even)
        def _():
            whole.wait_recv()

        @pl.when(even & (r == 0))
        def _():
            corner_on.wait_recv()

        for k in (1, modes - 1, 2):
            probe_pass(k).wait_recv()
            probe_pass(k).wait_send()
        for k in (1, modes - 1):
            probe_copy(k).wait_send()
        relay.wait_send()
        keep.wait()

        @pl.when(odd)
        def _():
            whole.wait_send()

        @pl.when(odd & (r == 0))
        def _():
            corner_on.wait_send()

        @pl.when(even & has_left)
        def _():
            strip.sent()

        @pl.when(r == 1)
        def _():
            down.wait_send()

        @pl.when(even & has_diag)
        def _():
            corner.wait_send()

    hbm = pl.BlockSpec(memory_space=pl.ANY)
    shape = jax.ShapeDtypeStruct
    return pl.pallas_call(
        kernel,
        name="spread",
        in_specs=[hbm, hbm],
        out_specs=[hbm] * 4,
        out_shape=[
            shape((2, tile_rows, tile_cols), F32),
            shape((2, w, tile_cols), F32),
            shape((2, w, tile_cols), F32),
            shape((2, modes, w, w), F32),
        ],
        scratch_shapes=quarter_sems(STRIP) + [pltpu.SemaphoreType.DMA((3,))] * 2
        + [pltpu.SemaphoreType.DMA((modes,))] * 4 + [pltpu.SemaphoreType.DMA],
        compiler_params=pltpu.CompilerParams(collective_id=0, has_side_effects=True),
    )


def make_collect(window, modes, tile_rows, tile_cols, rows_n, cols_n):
    w = window
    chips = rows_n * cols_n // 2
    piece = 2 * w // chips

    def kernel(g_right, g_low, g_diag, pg, right, low, diag, total, *sems):
        strip_sems, low_sems, diag_sems = sems[:6], sems[6:12], sems[12:18]
        one_s, one_r, x_s, x_r, y_s, y_r, a_s, a_r, b_s, b_r, in_sem, pair, got, mine = sems[18:]
        r, c, m = place()
        core = lax.rem(c, 2)
        chip = r * (cols_n // 2) + c // 2
        other = c + 1 - 2 * core
        odd, even = core == 1, core == 0
        away = jnp.where(odd, jnp.minimum(c + 1, cols_n - 1), jnp.maximum(c - 1, 0))
        has_away = jnp.where(odd, c < cols_n - 1, c > 0)
        flip = rows_n - 1 - r
        over = jnp.where(r == 0, jnp.minimum(c + 1, cols_n - 1), jnp.maximum(c - 1, 0))
        has_over = jnp.where(r == 0, c < cols_n - 1, c > 0)

        def partner(k):
            p = lax.rem(chip + k, chips)
            return device(p // (cols_n // 2), 2 * lax.rem(p, cols_n // 2) + core, m)

        def hello(k, carry):
            greet(partner(k))
            return carry

        greet(device(r, other, m))
        for k in (1, modes - 1):
            greet(device(r, c, lax.rem(m + k, modes)))
        when(has_away, lambda: greet(device(r, away, m)))
        when(has_over, lambda: greet(device(flip, over, m)))
        when(even, lambda: greet(device(flip, c, m)))
        when(odd, lambda: lax.fori_loop(1, chips, hello, 0))
        pl.semaphore_wait(
            pltpu.get_barrier_semaphore(),
            3 + jnp.where(odd, chips - 1, 1) + has_away.astype(jnp.int32) + has_over.astype(jnp.int32),
        )

        strip = Quarters(g_right, right, modes, tile_rows, r, away, STRIP, strip_sems)
        down = Quarters(g_low, low, modes, w, flip, c, EDGE, low_sems)
        corner = Quarters(g_diag, diag, modes, w, flip, over, EDGE, diag_sems)
        whole = remote(g_right, right, one_s, one_r, device(r, other, m))
        swap = remote(pg, pair.at[0], x_s, x_r, device(r, other, m))
        own = pltpu.make_async_copy(pg, pair.at[1], in_sem)
        at_chip = pl.ds(pl.multiple_of(chip * piece, piece), piece)
        rest = got.at[pl.ds(1, chips - 1)]
        many = total.at[pl.ds(0, (chips - 1) * piece), :]
        keep = pltpu.make_async_copy(mine, total.at[at_chip, :], in_sem)
        give = remote(total, total, y_s, y_r, device(r, other, m))

        def scatter_go(k, carry):
            p = lax.rem(chip + k, chips)
            rows = pl.ds(pl.multiple_of(p * piece, piece), piece)
            remote(pair.at[1, rows, :], got.at[k], a_s, a_r, partner(k)).start()
            return carry

        def share_go(k, carry):
            remote(mine, total.at[at_chip, :], b_s, b_r, partner(k)).start()
            return carry

        def add(k, acc):
            return acc + got[k]

        def sum_pair():
            own.wait()
            swap.wait_recv()
            pair[1] = pair[0] + pair[1]
            lax.fori_loop(1, chips, scatter_go, 0)

        def sum_plane():
            pltpu.make_async_copy(rest, rest, a_r).wait()
            mine[...] = lax.fori_loop(1, chips, add, pair[1, at_chip, :]) * (1.0 / 16.0)
            keep.start()
            lax.fori_loop(1, chips, share_go, 0)

        def sum_give():
            keep.wait()
            pltpu.make_async_copy(many, many, b_r).wait()
            give.start()

        def sum_end():
            pltpu.make_async_copy(rest, rest, a_s).wait()
            pltpu.make_async_copy(many, many, b_s).wait()
            give.wait_send()

        when(even, swap.start)
        when(odd, own.start)
        when(odd & has_away, strip.start)
        when(r == 0, down.start)
        when((r == 0) & has_over, corner.start)
        when(even, whole.start)
        when(odd, sum_pair)
        when(even & has_away, strip.take)
        when(r == 1, down.take)
        when((r == 1) & has_over, corner.take)
        when(odd, sum_plane)
        when(even & has_away, strip.turn)
        when(r == 1, down.turn)
        when((r == 1) & has_over, corner.turn)
        when(odd, sum_give)
        when(even & has_away, strip.finish)
        when(r == 1, down.finish)
        when((r == 1) & has_over, corner.finish)
        when(odd, whole.wait_recv)
        when(even, give.wait_recv)
        when(even, swap.wait_send)
        when(odd, sum_end)
        when(odd & has_away, strip.sent)
        when(r == 0, down.sent)
        when((r == 0) & has_over, corner.sent)
        when(even, whole.wait_send)

    hbm = pl.BlockSpec(memory_space=pl.ANY)
    shape = jax.ShapeDtypeStruct
    dma = pltpu.SemaphoreType.DMA
    return pl.pallas_call(
        kernel,
        name="collect",
        in_specs=[hbm] * 4,
        out_specs=[hbm] * 4,
        out_shape=[
            shape((2, tile_rows, tile_cols), F32),
            shape((2, w, tile_cols), F32),
            shape((2, w, tile_cols), F32),
            shape((2 * w, w), F32),
        ],
        scratch_shapes=quarter_sems(STRIP) + quarter_sems(EDGE) + quarter_sems(EDGE) + [dma] * 11
        + [pltpu.VMEM((2, 2 * w, w), F32), pltpu.VMEM((chips, piece, w), F32), pltpu.VMEM((piece, w), F32)],
        compiler_params=pltpu.CompilerParams(collective_id=1, has_side_effects=True),
    )


def make_finish(window, tile_rows, tile_cols):
    w = window
    blocks = tile_rows // w

    def kernel(own, strip, low, diag, total, grad, probe, a, b, e, s_a, s_b, s_e, s_out):
        r, c, m = place()
        below, inner = r > 0, c > 0

        def rows(k):
            return pl.ds(k * w, w)

        loads = [
            [
                pltpu.make_async_copy(own.at[:, rows(k), :], a.at[:, rows(k), :], s_a.at[k]),
                pltpu.make_async_copy(strip.at[:, rows(k), :], b.at[:, rows(k), :], s_b.at[k]),
            ]
            for k in range(blocks)
        ]
        edges = [pltpu.make_async_copy(src, e.at[n], s_e.at[n]) for n, src in enumerate((low, diag, total))]
        for k in reversed(range(blocks)):
            for copy in loads[k]:
                copy.start()
        for copy in edges:
            copy.start()
        stores = [pltpu.make_async_copy(a.at[:, rows(k), :], grad.at[:, rows(k), :], s_out.at[k]) for k in range(blocks)]

        def add(k, x):
            for part in range(2):
                a[part, k * w:k * w + w, :] += x[part]

        for k in reversed(range(blocks)):
            for copy in loads[k]:
                copy.wait()
            when(inner, lambda: add(k, b.at[:, rows(k), :]))
            if k == 0:
                for copy in edges:
                    copy.wait()
                when(below, lambda: add(0, e.at[0]))
                when(below & inner, lambda: add(0, e.at[1]))
                last = pltpu.make_async_copy(e.at[2], probe, s_out.at[blocks])
                last.start()
            stores[k].start()
        for copy in stores + [last]:
            copy.wait()

    hbm = pl.BlockSpec(memory_space=pl.ANY)
    dma = pltpu.SemaphoreType.DMA
    tile = (2, tile_rows, tile_cols)
    return pl.pallas_call(
        kernel,
        name="finish",
        in_specs=[hbm] * 5,
        out_specs=[hbm] * 2,
        out_shape=[jax.ShapeDtypeStruct(tile, F32), jax.ShapeDtypeStruct((2, w, w), F32)],
        scratch_shapes=[
            pltpu.VMEM(tile, F32), pltpu.VMEM(tile, F32), pltpu.VMEM((3, 2, w, w), F32),
            dma((blocks,)), dma((blocks,)), dma((3,)), dma((blocks + 1,)),
        ],
        compiler_params=pltpu.CompilerParams(vmem_limit_bytes=60 << 20),
    )


def per_device(object_slab, probe_modes, amplitudes, scan_counts, scan_positions):
    window = probe_modes.shape[-1]
    tile_rows, tile_cols = object_slab.shape[1:]
    slots = amplitudes.shape[0]
    modes, cols_n, rows_n = (lax.axis_size(a) for a in ("mode", "col", "row"))
    sizes = (window, modes, tile_rows, tile_cols, rows_n, cols_n)
    right, low, diag, probe = make_spread(*sizes)(object_slab, probe_modes)
    consts = [jnp.asarray(t) for t in tables(window)]
    compute = make_compute(window, modes, slots, tile_rows, tile_cols, cols_n)
    g_own, g_right, g_low, g_diag, pg, shift = compute(
        scan_positions, scan_counts, object_slab, right, low, diag, probe, amplitudes, *consts
    )
    from_left, from_up, from_diag, total = make_collect(*sizes)(
        g_right, g_low, g_diag, pg.reshape(2 * window, window)
    )
    grad, probe_grad = make_finish(window, tile_rows, tile_cols)(
        g_own, from_left, from_up, from_diag, total.reshape(2, window, window)
    )
    return (grad, probe_grad.reshape(2, 1, window, window), shift)


def solution(mesh):
    in_specs = (
        P(None, "row", "col"),
        P(None, "mode", None, None),
        P(("row", "col"), None, None),
        P(),
        P(None, ("row", "col")),
    )
    out_specs = (P(None, "row", "col"), P(None, "mode", None, None), P(None, ("row", "col")))
    return jax.shard_map(
        per_device, mesh=mesh, in_specs=in_specs, out_specs=out_specs, check_vma=False
    )
```
